32 devices in a mesh: dp: 8 (over z, y), tensor: 4 (over x, core).
Axes of the slice: x: 2, y: 2, z: 4, core: 2. Of those that a mesh axis runs over, the one named last changes fastest.
Arguments:
- block_input: bfloat16 [24576, 240], P(('dp', 'tensor')), may hold values from -6 to 6
- lengths: int32 [128], P('dp'), may hold values from 6 to 192, as said below
- cotangent: bfloat16 [24576, 240], P(('dp', 'tensor')), may hold values from -6 to 6
- norm_params: float32 [5, 2, 240], replicated, may hold values from -0.9 to 1.45, as said below
- bn_params: float32 [2, 240], P(None, 'tensor'), may hold values from -0.9 to 1.45, as said below
- ffn_in: float32 [2, 240, 960], P(None, None, 'tensor'), may hold values from -0.375 to 0.375
- ffn_out: float32 [2, 960, 240], P(None, 'tensor'), may hold values from -0.1875 to 0.1875
- attn_in: float32 [3, 240, 240], P(None, None, 'tensor'), may hold values from -0.375 to 0.375
- attn_out: float32 [240, 240], P('tensor'), may hold values from -3.5 to 3.5
- conv_in: float32 [2, 240, 240], P(None, None, 'tensor'), may hold values from -0.375 to 0.375
- depth_kernel: float32 [15, 240], P(None, 'tensor'), may hold values from -1.5 to 1.5
- conv_out: float32 [240, 240], P('tensor'), may hold values from -0.75 to 0.75
- stat_wide: float32 [4, 11, 240, 240], P('tensor'), may hold values from 0 to 960, as said below
- stat_head: float32 [4, 8, 60, 60], P('tensor'), may hold values from 0 to 960, as said below
- stat_hidden: float32 [4, 4, 240, 240], P('tensor'), may hold values from 0 to 960, as said below
- stat_kernel: float32 [4, 15, 15], P('tensor'), may hold values from 0 to 960, as said below
- norm_second: float32 [5, 2, 240], replicated, may hold values from 1 to 16
- bn_second: float32 [2, 240], P(None, 'tensor'), may hold values from 1 to 16
- step_count: int32 [1], replicated, may hold values from 1 to 20
Outputs:
- block_out: bfloat16 [24576, 240], P(('dp', 'tensor'))
- input_grad: float32 [24576, 240], P(('dp', 'tensor'))
- grad_norm: float32 [1], replicated
- clip_norm: float32 [5, 2, 240], replicated
- clip_bn: float32 [2, 240], P(None, 'tensor')
- clip_ffn_in: float32 [2, 240, 960], P(None, None, 'tensor')
- clip_ffn_out: float32 [2, 960, 240], P(None, 'tensor')
- clip_attn_in: float32 [3, 240, 240], P(None, None, 'tensor')
- clip_attn_out: float32 [240, 240], P('tensor')
- clip_conv_in: float32 [2, 240, 240], P(None, None, 'tensor')
- clip_depth: float32 [15, 240], P(None, 'tensor')
- clip_conv_out: float32 [240, 240], P('tensor')
- new_ffn_in: float32 [2, 240, 960], P(None, None, 'tensor')
- new_ffn_out: float32 [2, 960, 240], P(None, 'tensor')
- new_attn_in: float32 [3, 240, 240], P(None, None, 'tensor')
- new_attn_out: float32 [240, 240], P('tensor')
- new_conv_in: float32 [2, 240, 240], P(None, None, 'tensor')
- new_depth: float32 [15, 240], P(None, 'tensor')
- new_conv_out: float32 [240, 240], P('tensor')
- new_norm: float32 [5, 2, 240], replicated
- new_bn: float32 [2, 240], P(None, 'tensor')
- new_norm_second: float32 [5, 2, 240], replicated
- new_bn_second: float32 [2, 240], P(None, 'tensor')
- new_stat_wide: float32 [4, 11, 240, 240], P('tensor')
- new_stat_head: float32 [4, 8, 60, 60], P('tensor')
- new_stat_hidden: float32 [4, 4, 240, 240], P('tensor')
- new_stat_kernel: float32 [4, 15, 15], P('tensor')
The draws below stay inside these ranges and needn't reach their ends.
Inputs may be any that keep to these rules, and one draw needn't show every extreme that they name: `lengths`: in each group of 16 consecutive utterances one has exactly 192 frames. `norm_params`: gains near one, biases near zero. `bn_params`: gains near one, biases near zero. `stat_wide`: each block is a positive multiple of the identity. `stat_head`: each block is a positive multiple of the identity. `stat_hidden`: each block is a positive multiple of the identity. `stat_kernel`: each block is a positive multiple of the identity.
All inputs are finite; a program needn't handle non-finite values.
Results may differ from the reference program's by a relative error of at most 0.035.
Values may be sent and summed in bfloat16 or wider, within the bound.
A program may use at most 128 MiB of HBM per device.

```python
import math
import jax
import jax.numpy as jnp
from jax import lax

D = 240
FF = 960
HEADS = 4
KS = 15
LEN = 192
ROOT_ITERS = 8
UTT_DEV = 4
HEAD = 60
UTTS = 128
FRAMES = 24576
NPARAM = 1331280
N_DP = 8
N_TENSOR = 4


def draw_lengths(key, part):
    group_size = N_TENSOR * UTT_DEV
    shortest = max(1, LEN // 30)
    values = jax.random.randint(key, (UTTS,), shortest, LEN + 1)
    chosen = jax.random.randint(jax.random.fold_in(key, 7), (UTTS // group_size,), 0, group_size)
    longest = jnp.arange(UTTS) % group_size == jnp.repeat(chosen, group_size)
    return jnp.where(longest, LEN, values).astype(jnp.int32)


def gain_and_bias(key, leading):
    noise = jnp.clip(jax.random.normal(key, leading + (2, D), jnp.float32), -3.0, 3.0)
    gains = 1.0 + 0.15 * noise[..., 0, :]
    biases = 0.3 * noise[..., 1, :]
    return jnp.stack([gains, biases], axis=-2)


def draw_norm_params(key, part):
    return gain_and_bias(key, (5,))


def draw_bn_params(key, part):
    return gain_and_bias(key, ())


def scaled_identity(key, leading, order):
    scales = jnp.exp(jax.random.uniform(key, leading + (1, 1), jnp.float32, math.log(D / 8.0), math.log(4.0 * D)))
    return scales * jnp.eye(order, dtype=jnp.float32)


def draw_stat_wide(key, part):
    return scaled_identity(key, (N_TENSOR, 11), D)


def draw_stat_head(key, part):
    return scaled_identity(key, (N_TENSOR, 8), D // N_TENSOR)


def draw_stat_hidden(key, part):
    return scaled_identity(key, (N_TENSOR, 4), FF // N_TENSOR)


def draw_stat_kernel(key, part):
    return scaled_identity(key, (N_TENSOR,), KS)


def shard_levels(rng, extent, split, least, top_value):
    level = 1.0
    for dim, blocks in split:
        steps = jax.random.uniform(jax.random.fold_in(jax.random.fold_in(rng, 6), dim), (blocks,), jnp.float32, least / len(split), top_value / len(split))
        level = level * jnp.repeat(jnp.exp(steps), extent[dim] // blocks).reshape((-1,) + (1,) * (len(extent) - 1 - dim))
    return level


def gaussian(rng, dims, width, reach, split=(), kind=jnp.bfloat16):
    result = width * jax.random.normal(rng, dims, jnp.float32)
    if split:
        result = result * shard_levels(rng, dims, split, -0.22, 0.18)
    return jnp.clip(result, -reach, reach).astype(kind)


def setup_inputs(seed: int = 0) -> dict:
    splits = jax.random.split(jax.random.key(seed), 20)
    return {
        "block_input": gaussian(splits[0], (FRAMES, D), 1.0, 6.0, ((0, 32),)),
        "lengths": draw_lengths(jax.random.fold_in(splits[19], 71), 0),
        "cotangent": gaussian(splits[2], (FRAMES, D), 1.0, 6.0, ((0, 32),)),
        "norm_params": draw_norm_params(jax.random.fold_in(splits[19], 71), 0),
        "bn_params": draw_bn_params(jax.random.fold_in(splits[19], 71), 0),
        "ffn_in": gaussian(splits[5], (2, D, FF), D ** -0.5, 0.375, ((2, 4),), jnp.float32),
        "ffn_out": gaussian(splits[6], (2, FF, D), FF ** -0.5, 0.1875, ((1, 4),), jnp.float32),
        "attn_in": gaussian(splits[7], (3, D, D), D ** -0.5, 0.375, ((2, 4),), jnp.float32),
        "attn_out": gaussian(splits[8], (D, D), (max(1, D // 64)) ** -0.5, 3.5, ((0, 4),), jnp.float32),
        "conv_in": gaussian(splits[9], (2, D, D), D ** -0.5, 0.375, ((2, 4),), jnp.float32),
        "depth_kernel": gaussian(splits[10], (KS, D), KS ** -0.5, 1.5, ((1, 4),), jnp.float32),
        "conv_out": gaussian(splits[11], (D, D), (max(1, D // 4)) ** -0.5, 0.75, ((0, 4),), jnp.float32),
        "stat_wide": draw_stat_wide(jax.random.fold_in(splits[19], 71), 0),
        "stat_head": draw_stat_head(jax.random.fold_in(splits[19], 71), 0),
        "stat_hidden": draw_stat_hidden(jax.random.fold_in(splits[19], 71), 0),
        "stat_kernel": draw_stat_kernel(jax.random.fold_in(splits[19], 71), 0),
        "norm_second": jnp.clip(jnp.exp(jax.random.uniform(splits[16], (5, 2, D), jnp.float32, math.log(1.0), math.log(16.0))), 1.0, 16.0),
        "bn_second": jnp.clip(jnp.exp(math.log(16.0) - 2.7725887 * jax.random.uniform(splits[17], (2, D), jnp.float32) ** shard_levels(splits[17], (2, D), ((1, 4),), -0.2, 0.2)), 1.0, 16.0),
        "step_count": jax.random.randint(splits[18], (1,), 1, 21).astype(jnp.int32),
    }


@jax.custom_vjp
def low(v):
    return lax.optimization_barrier(v.astype(jnp.bfloat16)).astype(jnp.float32)

@jax.custom_vjp
def low_back(v):
    return v

def low_keep(v):
    return (low(v), None)

def low_pass(kept, grad):
    return (grad,)

def back_keep(v):
    return (v, None)

def back_low(kept, grad):
    return (low(grad),)
low.defvjp(low_keep, low_pass)
low_back.defvjp(back_keep, back_low)
precise = lax.Precision.HIGHEST
PEAK_RATE = 2.0
WARM_STEPS = 4.0
SMALL_RATE = 0.3
GRAFT_SCALE = 0.6
NEG_FILL = -1000000000.0

def both_ways(value):
    return low(low_back(value))

def matmul(left_side, right_side):
    return jnp.dot(left_side, right_side, precision=precise, preferred_element_type=jnp.float32)

def layer_norm(hidden, gain_vec, bias_vec):
    mean_value = lax.optimization_barrier(jnp.mean(hidden, axis=-1, keepdims=True))
    centred = hidden - mean_value
    spread = lax.optimization_barrier(jnp.mean(centred * centred, axis=-1, keepdims=True))
    return centred * lax.rsqrt(spread + 1e-05) * gain_vec + bias_vec

def swish_act(value):
    return value * jax.nn.sigmoid(value)

def feed_forward(hidden, params, first_weight, second_weight):
    normed = low(layer_norm(hidden, params[0], params[1]))
    inner_pre = low_back(matmul(normed, low(first_weight)))
    return low_back(matmul(low(swish_act(inner_pre)), low(second_weight)))

def attend_group(operands):
    queries, key_rows, values, group_mask = operands
    scores = jnp.einsum('uqhe,ukhe->uhqk', queries, key_rows, precision=precise) * HEAD ** (-0.5)
    scores = low_back(scores)
    scores = jnp.where(group_mask[:, None, None, :] > 0, scores, NEG_FILL)
    row_max = lax.optimization_barrier(jnp.max(scores, axis=-1, keepdims=True))
    exps = jnp.exp(scores - row_max)
    prob_low = low(exps / lax.optimization_barrier(jnp.sum(exps, axis=-1, keepdims=True)))
    return jnp.einsum('uhqk,ukhe->uqhe', prob_low, values, precision=precise)

def attention(hidden, params, attn_in, attn_out, frame_mask):
    normed = low(layer_norm(hidden, params[0], params[1]))
    shape_five = (N_DP, UTTS // N_DP, LEN, HEADS, HEAD)
    queries = both_ways(matmul(normed, low(attn_in[0]))).reshape(shape_five)
    key_rows = both_ways(matmul(normed, low(attn_in[1]))).reshape(shape_five)
    values = both_ways(matmul(normed, low(attn_in[2]))).reshape(shape_five)
    grouped_mask = frame_mask.reshape(N_DP, UTTS // N_DP, LEN)
    mixture = lax.map(jax.checkpoint(attend_group), (queries, key_rows, values, grouped_mask))
    mixture = both_ways(mixture.reshape(FRAMES, D))
    return low_back(matmul(mixture, low(attn_out)))

def depthwise(frames, depth_kernel):
    half_width = KS // 2
    padded = jnp.pad(frames, ((0, 0), (half_width, KS - 1 - half_width), (0, 0)))
    running = jnp.zeros_like(frames)
    for offset in range(KS):
        running = running + padded[:, offset:offset + frames.shape[1], :] * depth_kernel[offset]
    return running

def convolve(hidden, params, conv_in, depth_kernel, bn_params, conv_out, frame_mask):
    normed = low(layer_norm(hidden, params[0], params[1]))
    value_pre = low_back(matmul(normed, low(conv_in[0])))
    gate_pre = low_back(matmul(normed, low(conv_in[1])))
    gated = value_pre * jax.nn.sigmoid(gate_pre) * frame_mask[:, None]
    conv_mid = depthwise(gated.reshape(UTTS, LEN, D), depth_kernel).reshape(FRAMES, D)
    frame_count = jnp.sum(frame_mask)
    mean_value = lax.optimization_barrier(jnp.sum(conv_mid * frame_mask[:, None], axis=0)) / frame_count
    centred = conv_mid - mean_value
    spread = lax.optimization_barrier(jnp.sum(centred * centred * frame_mask[:, None], axis=0)) / frame_count
    normal = centred * lax.rsqrt(spread + 1e-05) * bn_params[0] + bn_params[1]
    active = low(swish_act(normal) * frame_mask[:, None])
    return low_back(matmul(active, low(conv_out)))

def conformer_block(base_rows, norm_params, bn_params, ffn_in, ffn_out, attn_in, attn_out, conv_in, depth_kernel, conv_out, frame_mask):
    after_one = base_rows + 0.5 * feed_forward(base_rows, norm_params[0], ffn_in[0], ffn_out[0])
    after_two = after_one + attention(after_one, norm_params[1], attn_in, attn_out, frame_mask)
    after_three = after_two + convolve(after_two, norm_params[2], conv_in, depth_kernel, bn_params, conv_out, frame_mask)
    after_four = after_three + 0.5 * feed_forward(after_three, norm_params[3], ffn_in[1], ffn_out[1])
    return layer_norm(after_four, norm_params[4, 0], norm_params[4, 1])

def inverse_root(stat):
    identity = jnp.eye(stat.shape[-1], dtype=jnp.float32)
    frob_size = jnp.sqrt(lax.optimization_barrier(jnp.sum(stat * stat, axis=(-2, -1), keepdims=True)))
    zscale = 2.5 / frob_size
    root_est = jnp.sqrt(jnp.sqrt(zscale)) * identity
    scaled_stat = zscale * stat
    for iteration in range(ROOT_ITERS):
        stepper = 1.25 * identity - 0.25 * scaled_stat
        root_est = jnp.matmul(root_est, stepper, precision=precise)
        square = jnp.matmul(stepper, stepper, precision=precise)
        scaled_stat = jnp.matmul(jnp.matmul(square, square, precision=precise), scaled_stat, precision=precise)
    return root_est

def precondition(weight, gradient, left_stat, right_stat, step_rate):
    flipped = jnp.swapaxes(gradient, -1, -2)
    left_new = 0.5 * left_stat + 0.5 * jnp.matmul(gradient, flipped, precision=precise)
    right_new = 0.5 * right_stat + 0.5 * jnp.matmul(flipped, gradient, precision=precise)
    direction = jnp.matmul(jnp.matmul(inverse_root(left_new), gradient, precision=precise), inverse_root(right_new), precision=precise)
    weight_size = jnp.sqrt(lax.optimization_barrier(jnp.sum(weight * weight, axis=(-2, -1), keepdims=True)))
    direction_size = jnp.sqrt(lax.optimization_barrier(jnp.sum(direction * direction, axis=(-2, -1), keepdims=True)))
    graft = GRAFT_SCALE * weight_size / (direction_size + 1e-06)
    return (weight - step_rate * graft * direction, left_new, right_new)

def learning_rate(step_count):
    step_value = step_count[0].astype(jnp.float32)
    return PEAK_RATE * jnp.minimum(step_value / WARM_STEPS, jnp.sqrt(WARM_STEPS / step_value))

def column_blocks(matrix):
    return matrix.reshape(matrix.shape[0], N_TENSOR, -1).transpose(1, 0, 2)

def column_join(blocks):
    return blocks.transpose(1, 0, 2).reshape(blocks.shape[1], -1)

def row_blocks(matrix):
    return matrix.reshape(N_TENSOR, -1, matrix.shape[1])

def row_join(blocks):
    return blocks.reshape(-1, blocks.shape[2])

def reference(block_input, lengths, cotangent, norm_params, bn_params, ffn_in, ffn_out, attn_in, attn_out, conv_in, depth_kernel, conv_out, stat_wide, stat_head, stat_hidden, stat_kernel, norm_second, bn_second, step_count):
    frame_mask = (jnp.arange(LEN)[None, :] < lengths[:, None]).astype(jnp.float32).reshape(FRAMES)

    def forward(base_rows, p_norm, p_bn, p_ffn_in, p_ffn_out, p_attn_in, p_attn_out, p_conv_in, p_depth, p_conv_out):
        return conformer_block(base_rows, p_norm, p_bn, p_ffn_in, p_ffn_out, p_attn_in, p_attn_out, p_conv_in, p_depth, p_conv_out, frame_mask)
    output, pullback = jax.vjp(forward, block_input.astype(jnp.float32), norm_params, bn_params, ffn_in, ffn_out, attn_in, attn_out, conv_in, depth_kernel, conv_out)
    grads = pullback(cotangent.astype(jnp.float32))
    input_grad = grads[0]
    weight_grads = grads[1:]
    square_sum = sum((jnp.sum(gradient * gradient) for gradient in weight_grads))
    grad_norm = jnp.sqrt(square_sum)
    threshold = math.sqrt(NPARAM)
    clip_factor = threshold / jnp.maximum(grad_norm, threshold)
    c_norm, c_bn, c_ffn_in, c_ffn_out, c_attn_in, c_attn_out, c_conv_in, c_depth, c_conv_out = [gradient * clip_factor for gradient in weight_grads]
    step_rate = learning_rate(step_count)
    wide_new = [None] * 11
    head_new = [None] * 8
    hidden_new = [None] * 4
    ffn_in_new = []
    ffn_out_new = []
    conv_in_new = []
    attn_in_new = []
    for member in range(2):
        weight, wide_new[member], hidden_new[member] = precondition(column_blocks(ffn_in[member]), column_blocks(c_ffn_in[member]), stat_wide[:, member], stat_hidden[:, member], step_rate)
        ffn_in_new.append(column_join(weight))
        weight, hidden_new[2 + member], wide_new[2 + member] = precondition(row_blocks(ffn_out[member]), row_blocks(c_ffn_out[member]), stat_hidden[:, 2 + member], stat_wide[:, 2 + member], step_rate)
        ffn_out_new.append(row_join(weight))
        weight, wide_new[8 + member], head_new[4 + member] = precondition(column_blocks(conv_in[member]), column_blocks(c_conv_in[member]), stat_wide[:, 8 + member], stat_head[:, 4 + member], step_rate)
        conv_in_new.append(column_join(weight))
    for member in range(3):
        weight, wide_new[4 + member], head_new[member] = precondition(column_blocks(attn_in[member]), column_blocks(c_attn_in[member]), stat_wide[:, 4 + member], stat_head[:, member], step_rate)
        attn_in_new.append(column_join(weight))
    weight, head_new[3], wide_new[7] = precondition(row_blocks(attn_out), row_blocks(c_attn_out), stat_head[:, 3], stat_wide[:, 7], step_rate)
    attn_out_new = row_join(weight)
    weight, kernel_new, head_new[6] = precondition(column_blocks(depth_kernel), column_blocks(c_depth), stat_kernel, stat_head[:, 6], step_rate)
    depth_new = column_join(weight)
    weight, head_new[7], wide_new[10] = precondition(row_blocks(conv_out), row_blocks(c_conv_out), stat_head[:, 7], stat_wide[:, 10], step_rate)
    conv_out_new = row_join(weight)
    norm_second_new = 0.5 * norm_second + 0.5 * c_norm * c_norm
    norm_new = norm_params - step_rate * SMALL_RATE * c_norm * lax.rsqrt(norm_second_new)
    bn_second_new = 0.5 * bn_second + 0.5 * c_bn * c_bn
    bn_new = bn_params - step_rate * SMALL_RATE * c_bn * lax.rsqrt(bn_second_new)
    return (output.astype(jnp.bfloat16), input_grad, grad_norm.reshape(1), c_norm, c_bn, c_ffn_in, c_ffn_out, c_attn_in, c_attn_out, c_conv_in, c_depth, c_conv_out, jnp.stack(ffn_in_new), jnp.stack(ffn_out_new), jnp.stack(attn_in_new), attn_out_new, jnp.stack(conv_in_new), depth_new, conv_out_new, norm_new, bn_new, norm_second_new, bn_second_new, jnp.stack(wide_new, axis=1), jnp.stack(head_new, axis=1), jnp.stack(hidden_new, axis=1), kernel_new)
```

```python
import functools
import math

import jax
import jax.numpy as jnp
from jax import lax
from jax.experimental import pallas as pl
from jax.experimental.pallas import tpu as pltpu
from jax.sharding import PartitionSpec as P

D = 240
KS = 15
LEN = 192
HEAD = 60
PADH = 64
ROOT_ITERS = 8
FINE_ITERS = 4
NPARAM = 1331280
PEAK_RATE = 2.0
WARM_STEPS = 4.0
SMALL_RATE = 0.3
GRAFT_SCALE = 0.6
NEG_FILL = -1000000000.0
ROWS = 512
VMEM_CAP = 60 * 1024 * 1024

F32 = jnp.float32
BF16 = jnp.bfloat16


def nn(a, b):
    return lax.dot_general(a, b, (((1,), (0,)), ((), ())), preferred_element_type=F32)


def nt(a, b):
    return lax.dot_general(a, b, (((1,), (1,)), ((), ())), preferred_element_type=F32)


def tn(a, b):
    return lax.dot_general(a, b, (((0,), (0,)), ((), ())), preferred_element_type=F32)


def sigmoid(v):
    return 0.5 * jnp.tanh(0.5 * v) + 0.5


def standardize(h):
    centred = h - jnp.sum(h, axis=-1, keepdims=True) * (1.0 / D)
    spread = jnp.sum(centred * centred, axis=-1, keepdims=True) * (1.0 / D)
    inv = lax.rsqrt(spread + 1e-05)
    return centred * inv, inv


def norm_back(h, gain, dy):
    xhat, inv = standardize(h)
    scaled = dy * gain
    mean_a = jnp.sum(scaled, axis=-1, keepdims=True) * (1.0 / D)
    mean_b = jnp.sum(scaled * xhat, axis=-1, keepdims=True) * (1.0 / D)
    dh = inv * (scaled - mean_a - xhat * mean_b)
    return dh, jnp.sum(dy * xhat, axis=0, keepdims=True), jnp.sum(dy, axis=0, keepdims=True)


def row_mask(length):
    return (lax.broadcasted_iota(jnp.int32, (LEN, 1), 0) < length).astype(F32)


def lane_masks(dtype):
    lane = lax.broadcasted_iota(jnp.int32, (1, 128), 1)
    return ((lane < PADH).astype(dtype), (lane >= PADH).astype(dtype))


def own_length(lens_ref, step):
    return lens_ref[lax.axis_index("tensor") * pl.num_programs(0) + step]


def forward_kernel(
    lens_ref, x_ref, np_ref, ffn_ref, mix_ref, small_ref,
    n1_o, inner_o, act_o, x1_o, n2_o, q_o, k_o, v_o, p_o, mix_o, x2_o, n3_o, vp_o, gp_o, mid_o, st_o,
    pad_sc,
):
    step = pl.program_id(0)
    length = own_length(lens_ref, step)
    x0 = x_ref[...].astype(F32)
    n1 = (standardize(x0)[0] * np_ref[0, 0:1, :] + np_ref[0, 1:2, :]).astype(BF16)
    n1_o[...] = n1
    total = jnp.zeros((LEN, D), F32)
    for t in range(ffn_ref.shape[0]):
        inner = nn(n1, ffn_ref[t, 0])
        inner_o[t] = inner
        active = (inner * sigmoid(inner)).astype(BF16)
        act_o[t] = active
        total = total + nn(active, ffn_ref[t, 1])
    x1 = x0 + 0.5 * total
    x1_o[...] = x1
    n2 = (standardize(x1)[0] * np_ref[1, 0:1, :] + np_ref[1, 1:2, :]).astype(BF16)
    n2_o[...] = n2
    q_o[...] = nt(n2, mix_ref[0]).astype(BF16)
    k_o[...] = nt(n2, mix_ref[1]).astype(BF16)
    v_o[...] = nt(n2, mix_ref[2]).astype(BF16)
    key_ok = lax.broadcasted_iota(jnp.int32, (1, LEN), 1) < length
    masks = lane_masks(BF16)
    for half in range(2):
        lanes = slice(half * 128, half * 128 + 128)
        q, k, v = q_o[:, lanes], k_o[:, lanes], v_o[:, lanes]
        mixture = jnp.zeros((LEN, 128), F32)
        for side in range(2):
            scores = nt(q * masks[side], k) * HEAD ** (-0.5)
            scores = jnp.where(key_ok, scores, NEG_FILL)
            exps = jnp.exp(scores - jnp.max(scores, axis=-1, keepdims=True))
            probs = exps * (1.0 / jnp.sum(exps, axis=-1, keepdims=True))
            p_o[0, 2 * half + side] = probs
            mixture = mixture + nn(probs.astype(BF16), v * masks[side])
        mix_o[:, lanes] = mixture.astype(BF16)
    x2 = x1 + nn(mix_o[...], mix_ref[3])
    x2_o[...] = x2
    n3 = (standardize(x2)[0] * np_ref[2, 0:1, :] + np_ref[2, 1:2, :]).astype(BF16)
    n3_o[...] = n3
    value = nt(n3, mix_ref[4])
    gate = nt(n3, mix_ref[5])
    vp_o[...] = value
    gp_o[...] = gate
    mask = row_mask(length)
    gated = value * sigmoid(gate) * mask

    @pl.when(step == 0)
    def _():
        pad_sc[...] = jnp.zeros_like(pad_sc)

    count = length.astype(F32)
    for half in range(2):
        lanes = slice(half * 128, half * 128 + 128)
        pad_sc[half, 8 : 8 + LEN, :] = gated[:, lanes]
        running = jnp.zeros((LEN, 128), F32)
        for j in range(KS):
            running = running + pad_sc[half, 1 + j : 1 + j + LEN, :] * small_ref[j : j + 1, lanes]
        mid_o[:, lanes] = running
        mean = jnp.sum(running * mask, axis=0, keepdims=True) / count
        centred = (running - mean) * mask
        st_o[0, 0:1, lanes] = mean
        st_o[0, 1:2, lanes] = jnp.sum(centred * centred, axis=0, keepdims=True)
        st_o[0, 2:3, lanes] = jnp.full((1, 128), count, F32)
        st_o[0, 3:8, lanes] = jnp.zeros((5, 128), F32)


def ffn_backward(grad, inner_ref, ffn_ref, din_sc, rows):
    total = jnp.zeros((LEN, D), F32)
    for t in range(ffn_ref.shape[0]):
        inner = inner_ref[t]
        sigma = sigmoid(inner)
        d_inner = (nt(grad, ffn_ref[t, 1]) * (sigma * (1.0 + inner * (1.0 - sigma)))).astype(BF16)
        din_sc[t, rows, :] = d_inner
        total = total + nt(d_inner, ffn_ref[t, 0])
    return total


def middle_kernel(
    lens_ref, mid_ref, x2_ref, cot_ref, np_ref, bn_ref, mix_ref, ffn_ref,
    out_o, d3_o, dn_o, act3_o, gc_o, lng_o, gb_o, chunk_o,
    inner_sc, act_sc, din_sc, n4_sc, g2_sc,
):
    step = pl.program_id(0)
    rows = pl.ds(pl.multiple_of(step * LEN, LEN), LEN)
    mask = row_mask(own_length(lens_ref, step))
    mean, inv_std, gain, bias = [bn_ref[i : i + 1, :] for i in range(4)]
    xhat = (mid_ref[...] - mean) * inv_std
    normal = xhat * gain + bias
    sigma = sigmoid(normal)
    act3 = (normal * sigma * mask).astype(BF16)
    act3_o[...] = act3
    x3 = x2_ref[...] + nn(act3, mix_ref[6])
    n4 = (standardize(x3)[0] * np_ref[3, 0:1, :] + np_ref[3, 1:2, :]).astype(BF16)
    n4_sc[rows, :] = n4
    total = jnp.zeros((LEN, D), F32)
    for t in range(ffn_ref.shape[0]):
        inner = nn(n4, ffn_ref[t, 0])
        inner_sc[t] = inner
        active = (inner * sigmoid(inner)).astype(BF16)
        act_sc[t, rows, :] = active
        total = total + nn(active, ffn_ref[t, 1])
    x4 = x3 + 0.5 * total
    out_o[...] = (standardize(x4)[0] * np_ref[4, 0:1, :] + np_ref[4, 1:2, :]).astype(BF16)
    d4, gain4, bias4 = norm_back(x4, np_ref[4, 0:1, :], cot_ref[...].astype(F32))
    g2 = (0.5 * d4).astype(BF16)
    g2_sc[rows, :] = g2
    d_n4 = ffn_backward(g2, inner_sc, ffn_ref, din_sc, rows)
    d3, gain3, bias3 = norm_back(x3, np_ref[3, 0:1, :], d_n4)
    d3 = d3 + d4
    d3_o[...] = d3
    gc = d3.astype(BF16)
    gc_o[...] = gc
    d_normal = nt(gc, mix_ref[6]) * mask * (sigma * (1.0 + normal * (1.0 - sigma)))
    dn_o[...] = d_normal

    @pl.when(step == 0)
    def _():
        lng_o[...] = jnp.zeros_like(lng_o)
        gb_o[...] = jnp.zeros_like(gb_o)

    for i, part in enumerate((gain3, bias3, gain4, bias4)):
        lng_o[6 + i : 7 + i, :] += part
    gb_o[0:1, :] += jnp.sum(d_normal * xhat, axis=0, keepdims=True)
    gb_o[1:2, :] += jnp.sum(d_normal, axis=0, keepdims=True)

    @pl.when(step == pl.num_programs(0) - 1)
    def _():
        for t in range(ffn_ref.shape[0]):
            chunk_o[t, 0:D, :] = tn(n4_sc[...], din_sc[t]).astype(BF16)
            chunk_o[t, D : 2 * D, :] = tn(g2_sc[...], act_sc[t]).astype(BF16)
            chunk_o[t, 2 * D :, :] = jnp.zeros((ROWS - 2 * D, D), BF16)


def backward_kernel(
    lens_ref, x0_ref, x1_ref, x2_ref, inner_ref, p_ref, q_ref, k_ref, v_ref, vp_ref, gp_ref, mid_ref,
    d3_ref, dn_ref, np_ref, bn_ref, small_ref, mix_ref, ffn_ref, n1_ref, n2_ref, n3_ref, act1_ref,
    mixture_ref, act3_ref, gc_ref, lng_ref,
    ig_o, chunk1_o, chunk2_o,
    pad_g, pad_m, gk_sc, dv_sc, dg_sc, ga_sc, dq_sc, dk_sc, dvv_sc, g1_sc, din_sc, lng_sc,
):
    step = pl.program_id(0)
    rows = pl.ds(pl.multiple_of(step * LEN, LEN), LEN)
    mask = row_mask(own_length(lens_ref, step))

    @pl.when(step == 0)
    def _():
        pad_g[...] = jnp.zeros_like(pad_g)
        pad_m[...] = jnp.zeros_like(pad_m)
        gk_sc[...] = jnp.zeros_like(gk_sc)
        lng_sc[...] = lng_ref[...]

    mean, inv_std, gain, bias, sum_gain, sum_bias, inv_count = [bn_ref[i : i + 1, :] for i in range(7)]
    xhat = (mid_ref[...] - mean) * inv_std
    d_mid = inv_std * gain * (dn_ref[...] - mask * ((sum_bias + xhat * sum_gain) * inv_count))
    value = vp_ref[...]
    sigma = sigmoid(gp_ref[...])
    gated = value * sigma * mask
    d_n3 = jnp.zeros((LEN, D), F32)
    for half in range(2):
        lanes = slice(half * 128, half * 128 + 128)
        pad_g[half, 8 : 8 + LEN, :] = gated[:, lanes]
        pad_m[half, 8 : 8 + LEN, :] = d_mid[:, lanes]
        d_gated = jnp.zeros((LEN, 128), F32)
        mid_half = d_mid[:, lanes]
        for j in range(KS):
            d_gated = d_gated + pad_m[half, 15 - j : 15 - j + LEN, :] * small_ref[j : j + 1, lanes]
            gk_sc[j : j + 1, lanes] += jnp.sum(
                pad_g[half, 1 + j : 1 + j + LEN, :] * mid_half, axis=0, keepdims=True
            )
        d_gated = d_gated * mask
        sig = sigma[:, lanes]
        dv_sc[rows, lanes] = (d_gated * sig).astype(BF16)
        dg_sc[rows, lanes] = (d_gated * value[:, lanes] * sig * (1.0 - sig)).astype(BF16)
    d_n3 = nn(dv_sc[rows, :], mix_ref[4]) + nn(dg_sc[rows, :], mix_ref[5])
    d2, gain2, bias2 = norm_back(x2_ref[...], np_ref[2, 0:1, :], d_n3)
    d2 = d2 + d3_ref[...]
    ga = d2.astype(BF16)
    ga_sc[rows, :] = ga
    d_mix = nt(ga, mix_ref[3]).astype(BF16)
    masks = lane_masks(BF16)
    for half in range(2):
        lanes = slice(half * 128, half * 128 + 128)
        q, k, v, dm = q_ref[:, lanes], k_ref[:, lanes], v_ref[:, lanes], d_mix[:, lanes]
        dq = jnp.zeros((LEN, 128), F32)
        dk = jnp.zeros((LEN, 128), F32)
        dv = jnp.zeros((LEN, 128), F32)
        for side in range(2):
            probs = p_ref[0, 2 * half + side]
            dm_side = dm * masks[side]
            d_probs = nt(dm_side, v)
            dv = dv + tn(probs.astype(BF16), dm_side)
            row_sum = jnp.sum(probs * d_probs, axis=-1, keepdims=True)
            d_scores = (probs * (d_probs - row_sum)).astype(BF16)
            dq = dq + nn(d_scores, k * masks[side])
            dk = dk + tn(d_scores, q * masks[side])
        dq_sc[rows, lanes] = (dq * HEAD ** (-0.5)).astype(BF16)
        dk_sc[rows, lanes] = (dk * HEAD ** (-0.5)).astype(BF16)
        dvv_sc[rows, lanes] = dv.astype(BF16)
    d_n2 = nn(dq_sc[rows, :], mix_ref[0]) + nn(dk_sc[rows, :], mix_ref[1]) + nn(dvv_sc[rows, :], mix_ref[2])
    d1, gain1, bias1 = norm_back(x1_ref[...], np_ref[1, 0:1, :], d_n2)
    d1 = d1 + d2
    g1 = (0.5 * d1).astype(BF16)
    g1_sc[rows, :] = g1
    d_n1 = ffn_backward(g1, inner_ref, ffn_ref, din_sc, rows)
    d0, gain0, bias0 = norm_back(x0_ref[...].astype(F32), np_ref[0, 0:1, :], d_n1)
    ig_o[...] = d0 + d1
    for i, part in enumerate((gain0, bias0, gain1, bias1, gain2, bias2)):
        lng_sc[i : i + 1, :] += part

    @pl.when(step == pl.num_programs(0) - 1)
    def _():
        shards = ffn_ref.shape[0]
        eye = (
            lax.broadcasted_iota(jnp.int32, (16, D), 0) == lax.broadcasted_iota(jnp.int32, (16, D), 1)
        ).astype(BF16)
        pairs = (
            (dq_sc[...], n2_ref[...]),
            (dk_sc[...], n2_ref[...]),
            (dvv_sc[...], n2_ref[...]),
            (mixture_ref[...], ga_sc[...]),
            (dv_sc[...], n3_ref[...]),
            (dg_sc[...], n3_ref[...]),
            (act3_ref[...], gc_ref[...]),
            (gk_sc[...].astype(BF16), eye),
        )
        for i, (left, right) in enumerate(pairs):
            full = tn(left, right).astype(BF16)
            for t in range(shards):
                chunk1_o[t, PADH * i : PADH * (i + 1), :] = full[PADH * t : PADH * (t + 1), :]
        for t in range(shards):
            chunk2_o[t, 0:D, :] = tn(n1_ref[...], din_sc[t]).astype(BF16)
            chunk2_o[t, D : 2 * D, :] = tn(g1_sc[...], act1_ref[t]).astype(BF16)
            chunk2_o[t, 2 * D : 2 * D + 16, :] = lng_sc[...].astype(BF16)
            chunk2_o[t, 2 * D + 16 :, :] = jnp.zeros((ROWS - 2 * D - 16, D), BF16)


def split(a):
    high = a.astype(BF16)
    return high, (a - high.astype(F32)).astype(BF16)


def mul_fine(a, b):
    a_high, a_low = a
    b_high, b_low = b
    return nn(a_high, b_high) + (nn(a_high, b_low) + nn(a_low, b_high))


def eye_of(n):
    return (lax.broadcasted_iota(jnp.int32, (n, n), 0) == lax.broadcasted_iota(jnp.int32, (n, n), 1)).astype(F32)


def next_gap(gap, eye, fine):
    if fine:
        own = split(gap)
        square = split(mul_fine(own, own))
        inner = mul_fine(square, split((15.0 / 256.0) * eye + (1.0 / 256.0) * gap))
        return mul_fine(square, split(0.625 * eye + 0.3125 * gap + inner))
    own = gap.astype(BF16)
    square = nn(own, own).astype(BF16)
    inner = nn(square, ((15.0 / 256.0) * eye + (1.0 / 256.0) * gap).astype(BF16))
    return nn(square, (0.625 * eye + 0.3125 * gap + inner).astype(BF16))


def total_of(a):
    return jnp.sum(jnp.sum(a, axis=1, keepdims=True), axis=0, keepdims=True)


def update_kernel(
    step_ref, tot_ref, red_ref, gbn_ref, fi_ref, fo_ref, ai_ref, ao_ref, ci_ref, dk_ref, co_ref,
    sw_ref, sh_ref, sd_ref, sk_ref, np_ref, ns_ref, bp_ref, bs_ref,
    gn_o, cn_o, cb_o, cfi_o, cfo_o, cai_o, cao_o, cci_o, cdk_o, cco_o,
    nfi_o, nfo_o, nai_o, nao_o, nci_o, ndk_o, nco_o, nn_o, nb_o, nns_o, nbs_o,
    nsw_o, nsh_o, nsd_o, nsk_o,
    gap_f, gap_b, dir_f, dir_b,
):
    steps = jnp.full((1, 1), step_ref[0], jnp.int32).astype(F32)
    rate = PEAK_RATE * jnp.minimum(steps / WARM_STEPS, jnp.sqrt(WARM_STEPS / steps))
    grad_norm = jnp.sqrt(tot_ref[0:1, 0:1])
    threshold = math.sqrt(NPARAM)
    factor = threshold / jnp.maximum(grad_norm, threshold)
    square_factor = factor * factor
    gn_o[...] = jnp.broadcast_to(grad_norm, gn_o.shape)

    c_norm = red_ref[2, 2 * D : 2 * D + 16, :].astype(F32) * factor
    for i in range(5):
        clipped = c_norm[2 * i : 2 * i + 2, :]
        second = 0.5 * ns_ref[i] + 0.5 * clipped * clipped
        cn_o[i] = clipped
        nns_o[i] = second
        nn_o[i] = np_ref[i] - rate * SMALL_RATE * clipped * lax.rsqrt(second)
    c_bn = gbn_ref[...] * factor
    second = 0.5 * bs_ref[...] + 0.5 * c_bn * c_bn
    cb_o[...] = c_bn
    nbs_o[...] = second
    nb_o[...] = bp_ref[...] - rate * SMALL_RATE * c_bn * lax.rsqrt(second)

    eye_d = eye_of(D)
    scales_f = []
    for i in range(4):
        member, is_out = i // 2, i % 2
        chunk = (2, 0)[member]
        low = red_ref[chunk, is_out * D : is_out * D + D, :]
        wide_c = sw_ref[0, 2 * is_out + member, 0:1, 0:1]
        hidden_c = sd_ref[0, 2 * is_out + member, 0:1, 0:1]
        gram = tn(low, low) * square_factor
        wide = nt(low, low) * square_factor
        nsw_o[0, 2 * is_out + member] = 0.5 * wide_c * eye_d + 0.5 * wide
        nsd_o[0, 2 * is_out + member] = 0.5 * hidden_c * eye_d + 0.5 * gram
        clipped = low.astype(F32) * factor
        if is_out:
            cfo_o[member] = clipped.T
        else:
            cfi_o[member] = clipped
        dir_f[i] = clipped
        trace = total_of(clipped * clipped)
        power = total_of(gram * gram)
        scale = 1.0
        for k, c in enumerate((wide_c, hidden_c)):
            zoom = 2.5 * lax.rsqrt(0.25 * c * c * D + 0.5 * c * trace + 0.25 * power)
            gap_f[2 * i + k] = eye_d - zoom * (0.5 * c * eye_d + 0.5 * gram)
            scale = scale * jnp.sqrt(jnp.sqrt(zoom))
        scales_f.append(scale)

    eye_b = eye_of(4 * PADH)
    row_block = lax.broadcasted_iota(jnp.int32, (4 * PADH, 1), 0) // PADH
    lane_block = lax.broadcasted_iota(jnp.int32, (1, 4 * PADH), 1) // PADH
    same_block = row_block == lane_block
    wide_of = (4, 5, 6, 7, 8, 9, 10, None)
    head_of = (0, 1, 2, 3, 4, 5, 7, 6)
    scales_b = []

    def spread(values):
        column = jnp.zeros((4 * PADH, 1), F32)
        for i, value in enumerate(values):
            column = jnp.where(row_block == i, value, column)
        return column

    for group in range(2):
        low = red_ref[1, group * 4 * PADH : (group + 1) * 4 * PADH, :]
        clipped = low.astype(F32) * factor
        dir_b[group] = clipped
        gram = jnp.where(same_block, nt(low, low), 0.0) * square_factor
        row_trace = jnp.sum(clipped * clipped, axis=1, keepdims=True)
        row_power = jnp.sum(gram * gram, axis=1, keepdims=True)
        wide_cs, head_cs, traces, powers, dims = [], [], [], [], []
        for i in range(4):
            index = group * 4 + i
            part = slice(i * PADH, (i + 1) * PADH)
            piece = low[part, :]
            head_c = sh_ref[0, head_of[index], 0:1, 0:1]
            own_gram = nt(piece, piece)[:HEAD, :HEAD] * square_factor
            nsh_o[0, head_of[index]] = 0.5 * head_c * eye_d[:HEAD, :HEAD] + 0.5 * own_gram
            wide = tn(piece, piece) * square_factor
            if wide_of[index] is None:
                wide_c = sk_ref[0, 0:1, 0:1]
                nsk_o[0] = 0.5 * wide_c * eye_d[:KS, :KS] + 0.5 * wide[:KS, :KS]
                dims.append(KS)
            else:
                wide_c = sw_ref[0, wide_of[index], 0:1, 0:1]
                nsw_o[0, wide_of[index]] = 0.5 * wide_c * eye_d + 0.5 * wide
                dims.append(D)
            wide_cs.append(wide_c)
            head_cs.append(head_c)
            traces.append(jnp.sum(row_trace[part], axis=0, keepdims=True))
            powers.append(jnp.sum(row_power[part], axis=0, keepdims=True))
        scale = [1.0] * 4
        for k, (cs, sizes) in enumerate(((wide_cs, dims), (head_cs, [HEAD] * 4))):
            zooms = [
                2.5 * lax.rsqrt(0.25 * c * c * n + 0.5 * c * trace + 0.25 * power)
                for c, n, trace, power in zip(cs, sizes, traces, powers)
            ]
            gap_b[2 * group + k] = eye_b - spread(zooms) * (0.5 * spread(cs) * eye_b + 0.5 * gram)
            scale = [s * jnp.sqrt(jnp.sqrt(zoom)) for s, zoom in zip(scale, zooms)]
        scales_b.append(scale)

    def advance(fine, last):
        for k in range(2):
            for i in range(4):
                gap = gap_f[2 * i + k]
                dir_f[i] = dir_f[i] + 0.25 * nn(dir_f[i].astype(BF16), gap.astype(BF16))
                if not last:
                    gap_f[2 * i + k] = next_gap(gap, eye_d, fine)
            for i in range(2):
                gap = gap_b[2 * i + k]
                dir_b[i] = dir_b[i] + 0.25 * nn(gap.astype(BF16), dir_b[i].astype(BF16))
                if not last:
                    gap_b[2 * i + k] = next_gap(gap, eye_b, fine)

    def fine_step(i, carry):
        advance(True, False)
        return carry

    def coarse_step(i, carry):
        advance(False, False)
        return carry

    lax.fori_loop(0, FINE_ITERS, fine_step, 0)
    lax.fori_loop(0, ROOT_ITERS - 1 - FINE_ITERS, coarse_step, 0)
    advance(False, True)

    def graft(weight, direction):
        size = jnp.sqrt(total_of(weight * weight))
        return rate * GRAFT_SCALE * size / (jnp.sqrt(total_of(direction * direction)) + 1e-06)

    for i in range(4):
        member, is_out = i // 2, i % 2
        direction = dir_f[i] * scales_f[i]
        weight = (fi_ref, fo_ref)[is_out][member]
        if is_out:
            direction = direction.T
        (nfi_o, nfo_o)[is_out][member] = weight - graft(weight, direction) * direction
    for index in range(8):
        group, i = index // 4, index % 4
        part = slice(i * PADH, i * PADH + HEAD)
        direction = dir_b[group][part, :] * scales_b[group][i]
        clipped = red_ref[1, index * PADH : (index + 1) * PADH, :][:HEAD, :].astype(F32) * factor
        if index in (3, 6):
            weight_ref, clip_o, new_o = ((ao_ref, cao_o, nao_o), None, None, (co_ref, cco_o, nco_o))[index - 3]
            clip_o[...] = clipped
            new_o[...] = weight_ref[...] - graft(weight_ref[...], direction) * direction
        elif index == 7:
            turned = direction.T[:KS, :]
            cdk_o[...] = clipped.T[:KS, :]
            ndk_o[...] = dk_ref[...] - graft(dk_ref[...], turned) * turned
        else:
            weight_ref, clip_o, new_o = (ai_ref, cai_o, nai_o) if index < 3 else (ci_ref, cci_o, nci_o)
            m = index if index < 3 else index - 4
            turned = direction.T
            clip_o[m] = clipped.T
            new_o[m] = weight_ref[m] - graft(weight_ref[m], turned) * turned


def shape(dims, dtype=F32):
    return jax.ShapeDtypeStruct(dims, dtype)


def whole(dims):
    zeros = (0,) * len(dims)
    return pl.BlockSpec(dims, lambda u: zeros)


def tile(width):
    return pl.BlockSpec((LEN, width), lambda u: (u, 0))


SMEM_SPEC = pl.BlockSpec(memory_space=pltpu.SMEM)
VMEM_SPEC = pl.BlockSpec(memory_space=pltpu.VMEM)
PARAMS = pltpu.CompilerParams(vmem_limit_bytes=VMEM_CAP)


def forward_call(lengths, x, norm_params, ffn, mix, small):
    frames = x.shape[0]
    shards = ffn.shape[0]
    utts = frames // LEN
    wide = 4 * PADH
    shard_tile = pl.BlockSpec((shards, LEN, D), lambda u: (0, u, 0))
    return pl.pallas_call(
        forward_kernel,
        grid=(utts,),
        in_specs=[SMEM_SPEC, tile(D), whole(norm_params.shape), whole(ffn.shape), whole(mix.shape), whole(small.shape)],
        out_specs=[
            tile(D), shard_tile, shard_tile, tile(D), tile(D), tile(wide), tile(wide), tile(wide),
            pl.BlockSpec((1, 4, LEN, LEN), lambda u: (u, 0, 0, 0)),
            tile(wide), tile(D), tile(D), tile(wide), tile(wide), tile(wide),
            pl.BlockSpec((1, 8, wide), lambda u: (u, 0, 0)),
        ],
        out_shape=[
            shape((frames, D), BF16), shape((shards, frames, D)), shape((shards, frames, D), BF16),
            shape((frames, D)), shape((frames, D), BF16),
            shape((frames, wide), BF16), shape((frames, wide), BF16), shape((frames, wide), BF16),
            shape((utts, 4, LEN, LEN)), shape((frames, wide), BF16), shape((frames, D)), shape((frames, D), BF16),
            shape((frames, wide)), shape((frames, wide)), shape((frames, wide)), shape((utts, 8, wide)),
        ],
        scratch_shapes=[pltpu.VMEM((2, LEN + 16, 128), F32)],
        compiler_params=PARAMS,
        name="forward_part",
    )(lengths, x, norm_params, ffn, mix, small)


def middle_call(lengths, mid, x2, cot, norm_params, bn, mix, ffn):
    frames = x2.shape[0]
    shards = ffn.shape[0]
    wide = 4 * PADH
    return pl.pallas_call(
        middle_kernel,
        grid=(frames // LEN,),
        in_specs=[
            SMEM_SPEC, tile(wide), tile(D), tile(D), whole(norm_params.shape), whole(bn.shape),
            whole(mix.shape), whole(ffn.shape),
        ],
        out_specs=[
            tile(D), tile(D), tile(wide), tile(wide), tile(D), whole((16, D)), whole((8, wide)),
            whole((shards, ROWS, D)),
        ],
        out_shape=[
            shape((frames, D), BF16), shape((frames, D)), shape((frames, wide)), shape((frames, wide), BF16),
            shape((frames, D), BF16), shape((16, D)), shape((8, wide)), shape((shards, ROWS, D), BF16),
        ],
        scratch_shapes=[
            pltpu.VMEM((shards, LEN, D), F32), pltpu.VMEM((shards, frames, D), BF16),
            pltpu.VMEM((shards, frames, D), BF16), pltpu.VMEM((frames, D), BF16), pltpu.VMEM((frames, D), BF16),
        ],
        compiler_params=PARAMS,
        name="middle_part",
    )(lengths, mid, x2, cot, norm_params, bn, mix, ffn)


def backward_call(lengths, tiles, small_args, wholes):
    x0, x1, x2, inner, probs, q, k, v, vp, gp, mid, d3, dn = tiles
    norm_params, bn, small, mix, ffn = small_args
    frames = x1.shape[0]
    shards = ffn.shape[0]
    wide = 4 * PADH
    half_pad = pltpu.VMEM((2, LEN + 16, 128), F32)
    wide_low = pltpu.VMEM((frames, wide), BF16)
    thin_low = pltpu.VMEM((frames, D), BF16)
    return pl.pallas_call(
        backward_kernel,
        grid=(frames // LEN,),
        in_specs=[
            SMEM_SPEC, tile(D), tile(D), tile(D),
            pl.BlockSpec((shards, LEN, D), lambda u: (0, u, 0)),
            pl.BlockSpec((1, 4, LEN, LEN), lambda u: (u, 0, 0, 0)),
            tile(wide), tile(wide), tile(wide), tile(wide), tile(wide), tile(wide), tile(D), tile(wide),
        ] + [whole(a.shape) for a in small_args] + [whole(a.shape) for a in wholes],
        out_specs=[tile(D), whole((shards, ROWS, D)), whole((shards, ROWS, D))],
        out_shape=[shape((frames, D)), shape((shards, ROWS, D), BF16), shape((shards, ROWS, D), BF16)],
        scratch_shapes=[
            half_pad, half_pad, pltpu.VMEM((16, wide), F32), wide_low, wide_low, thin_low,
            wide_low, wide_low, wide_low, thin_low, pltpu.VMEM((shards, frames, D), BF16), pltpu.VMEM((16, D), F32),
        ],
        compiler_params=PARAMS,
        name="backward_part",
    )(lengths, *tiles, *small_args, *wholes)


def update_call(step_count, total_square, reduced, gbn, weights, stats, norm_params, norm_second, bn_params, bn_second):
    stat_wide, stat_head, stat_hidden, stat_kernel = stats
    corner = lambda a: pl.BlockSpec((1, a.shape[1], 8, 128), lambda i: (0, 0, 0, 0))
    one = lambda a: whole(a.shape)
    n_stat = lambda a: whole(a.shape)
    out_arrays = [
        shape((1, 128)), norm_params, bn_params, *weights, *weights, norm_params, bn_params, norm_params, bn_params,
        stat_wide, stat_head, stat_hidden, stat_kernel,
    ]
    in_arrays = [total_square, reduced, gbn, *weights]
    wide = 4 * PADH
    return pl.pallas_call(
        update_kernel,
        grid=(1,),
        in_specs=[SMEM_SPEC] + [one(a) for a in in_arrays]
        + [corner(stat_wide), one(stat_head), corner(stat_hidden), one(stat_kernel)]
        + [one(a) for a in (norm_params, norm_second, bn_params, bn_second)],
        out_specs=[one(a) for a in out_arrays],
        out_shape=[shape(a.shape) for a in out_arrays],
        scratch_shapes=[
            pltpu.VMEM((8, D, D), F32), pltpu.VMEM((4, wide, wide), F32),
            pltpu.VMEM((4, D, D), F32), pltpu.VMEM((2, wide, D), F32),
        ],
        compiler_params=PARAMS,
        name="update_part",
    )(step_count, *in_arrays, *stats, norm_params, norm_second, bn_params, bn_second)


def pack_weights(ffn_in, ffn_out, attn_in, attn_out, conv_in, depth_kernel, conv_out, bn_params):
    ffn = [jnp.stack([ffn_in[m], ffn_out[m]]).astype(BF16) for m in range(2)]
    rows = jnp.concatenate(
        [attn_in.swapaxes(1, 2), attn_out[None], conv_in.swapaxes(1, 2), conv_out[None]]
    ).astype(BF16)
    mix = jnp.pad(rows, ((0, 0), (0, PADH - HEAD), (0, 0)))
    small = jnp.pad(
        jnp.concatenate([depth_kernel, jnp.zeros((1, HEAD), F32), bn_params]), ((0, 6), (0, PADH - HEAD))
    )
    return ffn[0], ffn[1], mix, small


def local(
    block_input, lengths, cotangent, norm_params, bn_params, ffn_in, ffn_out, attn_in, attn_out, conv_in,
    depth_kernel, conv_out, stat_wide, stat_head, stat_hidden, stat_kernel, norm_second, bn_second, step_count,
):
    ffn_one, ffn_two, mix, small = pack_weights(
        ffn_in, ffn_out, attn_in, attn_out, conv_in, depth_kernel, conv_out, bn_params
    )
    ffn_one, ffn_two = [lax.all_gather(a, "tensor") for a in (ffn_one, ffn_two)]
    mix = lax.all_gather(mix, "tensor", axis=1, tiled=True)
    small = lax.all_gather(small, "tensor", axis=1, tiled=True)
    (n1, inner1, act1, x1, n2, q, k, v, probs, mixture, x2, n3, vp, gp, mid, stat) = forward_call(
        lengths, block_input, norm_params, ffn_one, mix, small
    )
    count_here = jnp.sum(stat[:, 2, 0])
    mean_here = jnp.sum(stat[:, 0] * stat[:, 2], axis=0) / count_here
    power_here = jnp.sum(stat[:, 1] + stat[:, 2] * (stat[:, 0] - mean_here) ** 2, axis=0)
    count, first = lax.psum((count_here, mean_here * count_here), ("dp", "tensor"))
    mean = first / count
    power = lax.psum(power_here + count_here * (mean_here - mean) ** 2, ("dp", "tensor"))
    inv_std = lax.rsqrt(power / count + 1e-05)
    zero = jnp.zeros_like(mean)
    bn = jnp.stack([mean, inv_std, small[16], small[17], zero, zero, zero, zero])
    block_out, d3, dn, act3, gc, lng, gb, chunk0 = middle_call(
        lengths, mid, x2, cotangent, norm_params, bn, mix, ffn_two
    )
    gb = lax.psum(gb[:2], ("dp", "tensor"))
    bn = jnp.stack([mean, inv_std, small[16], small[17], gb[0], gb[1], zero + 1.0 / count, zero])
    input_grad, chunk1, chunk2 = backward_call(
        lengths,
        (block_input, x1, x2, inner1, probs, q, k, v, vp, gp, mid, d3, dn),
        (norm_params, bn, small, mix, ffn_one),
        (n1, n2, n3, act1, mixture, act3, gc, lng),
    )
    chunks = jnp.concatenate([chunk0, chunk1, chunk2], axis=1)
    chunks = lax.psum_scatter(chunks, "tensor", scatter_dimension=0, tiled=True)
    reduced = lax.psum(chunks, "dp").reshape(3, ROWS, D)
    gbn = lax.dynamic_slice(gb, (0, lax.axis_index("tensor") * PADH), (2, PADH))[:, :HEAD]
    high = reduced.astype(F32)
    norm_rows = high[2, 2 * D : 2 * D + 16]
    square = jnp.sum(high * high) - jnp.sum(norm_rows * norm_rows) + jnp.sum(gbn * gbn)
    square = lax.psum(square, "tensor") + jnp.sum(norm_rows * norm_rows)
    total_square = jnp.broadcast_to(square, (8, 128))
    weights = (ffn_in, ffn_out, attn_in, attn_out, conv_in, depth_kernel, conv_out)
    outs = update_call(
        step_count, total_square, reduced, gbn, weights, (stat_wide, stat_head, stat_hidden, stat_kernel),
        norm_params, norm_second, bn_params, bn_second,
    )
    return (block_out, input_grad, outs[0][0, :1], *outs[1:])


def solution(mesh):
    weights_specs = (
        P(None, None, "tensor"), P(None, "tensor", None), P(None, None, "tensor"), P("tensor", None),
        P(None, None, "tensor"), P(None, "tensor"), P("tensor", None),
    )
    stat_specs = (
        P("tensor", None, None, None), P("tensor", None, None, None), P("tensor", None, None, None),
        P("tensor", None, None),
    )
    frames = P(("dp", "tensor"), None)
    channels = P(None, "tensor")
    return jax.shard_map(
        local,
        mesh=mesh,
        in_specs=(frames, P("dp"), frames, P(), channels, *weights_specs, *stat_specs, P(), channels, P()),
        out_specs=(
            frames, frames, P(), P(), channels, *weights_specs, *weights_specs, P(), channels, P(), channels,
            *stat_specs,
        ),
        check_vma=False,
    )
```

```python
import functools
import math

import jax
import jax.numpy as jnp
from jax import lax
from jax.experimental import pallas as pl
from jax.experimental.pallas import tpu as pltpu
from jax.sharding import PartitionSpec as P

D = 240
KS = 15
LEN = 192
HEAD = 60
PADH = 64
ROOT_ITERS = 8
FINE_ITERS = 4
NPARAM = 1331280
PEAK_RATE = 2.0
WARM_STEPS = 4.0
SMALL_RATE = 0.3
GRAFT_SCALE = 0.6
NEG_FILL = -1000000000.0
ROWS = 512
VMEM_CAP = 60 * 1024 * 1024

F32 = jnp.float32
BF16 = jnp.bfloat16


def nn(a, b):
    return lax.dot_general(a, b, (((1,), (0,)), ((), ())), preferred_element_type=F32)


def nt(a, b):
    return lax.dot_general(a, b, (((1,), (1,)), ((), ())), preferred_element_type=F32)


def tn(a, b):
    return lax.dot_general(a, b, (((0,), (0,)), ((), ())), preferred_element_type=F32)


def sigmoid(v):
    return 0.5 * jnp.tanh(0.5 * v) + 0.5


def standardize(h):
    centred = h - jnp.sum(h, axis=-1, keepdims=True) * (1.0 / D)
    spread = jnp.sum(centred * centred, axis=-1, keepdims=True) * (1.0 / D)
    inv = lax.rsqrt(spread + 1e-05)
    return centred * inv, inv


def norm_back(h, gain, dy):
    xhat, inv = standardize(h)
    scaled = dy * gain
    mean_a = jnp.sum(scaled, axis=-1, keepdims=True) * (1.0 / D)
    mean_b = jnp.sum(scaled * xhat, axis=-1, keepdims=True) * (1.0 / D)
    dh = inv * (scaled - mean_a - xhat * mean_b)
    return dh, jnp.sum(dy * xhat, axis=0, keepdims=True), jnp.sum(dy, axis=0, keepdims=True)


def row_mask(length):
    return (lax.broadcasted_iota(jnp.int32, (LEN, 1), 0) < length).astype(F32)


def lane_masks(dtype):
    lane = lax.broadcasted_iota(jnp.int32, (1, 128), 1)
    return ((lane < PADH).astype(dtype), (lane >= PADH).astype(dtype))


def own_length(lens_ref, step):
    return lens_ref[lax.axis_index("tensor") * pl.num_programs(0) + step]


def forward_kernel(
    lens_ref, x_ref, np_ref, ffn_ref, mix_ref, small_ref,
    n1_o, inner_o, act_o, x1_o, n2_o, q_o, k_o, v_o, p_o, mix_o, x2_o, n3_o, vp_o, gp_o, mid_o, st_o,
    pad_sc,
):
    step = pl.program_id(0)
    length = own_length(lens_ref, step)
    x0 = x_ref[...].astype(F32)
    n1 = (standardize(x0)[0] * np_ref[0, 0:1, :] + np_ref[0, 1:2, :]).astype(BF16)
    n1_o[...] = n1
    total = jnp.zeros((LEN, D), F32)
    for t in range(ffn_ref.shape[0]):
        inner = nn(n1, ffn_ref[t, 0])
        inner_o[t] = inner
        active = (inner * sigmoid(inner)).astype(BF16)
        act_o[t] = active
        total = total + nn(active, ffn_ref[t, 1])
    x1 = x0 + 0.5 * total
    x1_o[...] = x1
    n2 = (standardize(x1)[0] * np_ref[1, 0:1, :] + np_ref[1, 1:2, :]).astype(BF16)
    n2_o[...] = n2
    q_o[...] = nt(n2, mix_ref[0]).astype(BF16)
    k_o[...] = nt(n2, mix_ref[1]).astype(BF16)
    v_o[...] = nt(n2, mix_ref[2]).astype(BF16)
    key_ok = lax.broadcasted_iota(jnp.int32, (1, LEN), 1) < length
    masks = lane_masks(BF16)
    for half in range(2):
        lanes = slice(half * 128, half * 128 + 128)
        q, k, v = q_o[:, lanes], k_o[:, lanes], v_o[:, lanes]
        mixture = jnp.zeros((LEN, 128), F32)
        for side in range(2):
            scores = nt(q * masks[side], k) * HEAD ** (-0.5)
            scores = jnp.where(key_ok, scores, NEG_FILL)
            exps = jnp.exp(scores - jnp.max(scores, axis=-1, keepdims=True))
            probs = exps * (1.0 / jnp.sum(exps, axis=-1, keepdims=True))
            p_o[0, 2 * half + side] = probs
            mixture = mixture + nn(probs.astype(BF16), v * masks[side])
        mix_o[:, lanes] = mixture.astype(BF16)
    x2 = x1 + nn(mix_o[...], mix_ref[3])
    x2_o[...] = x2
    n3 = (standardize(x2)[0] * np_ref[2, 0:1, :] + np_ref[2, 1:2, :]).astype(BF16)
    n3_o[...] = n3
    value = nt(n3, mix_ref[4])
    gate = nt(n3, mix_ref[5])
    vp_o[...] = value
    gp_o[...] = gate
    mask = row_mask(length)
    gated = value * sigmoid(gate) * mask

    @pl.when(step == 0)
    def _():
        pad_sc[...] = jnp.zeros_like(pad_sc)

    count = length.astype(F32)
    for half in range(2):
        lanes = slice(half * 128, half * 128 + 128)
        pad_sc[half, 8 : 8 + LEN, :] = gated[:, lanes]
        running = jnp.zeros((LEN, 128), F32)
        for j in range(KS):
            running = running + pad_sc[half, 1 + j : 1 + j + LEN, :] * small_ref[j : j + 1, lanes]
        mid_o[:, lanes] = running
        mean = jnp.sum(running * mask, axis=0, keepdims=True) / count
        centred = (running - mean) * mask
        st_o[0, 0:1, lanes] = mean
        st_o[0, 1:2, lanes] = jnp.sum(centred * centred, axis=0, keepdims=True)
        st_o[0, 2:3, lanes] = jnp.full((1, 128), count, F32)
        st_o[0, 3:8, lanes] = jnp.zeros((5, 128), F32)


def ffn_backward(grad, inner_ref, ffn_ref, din_sc, rows):
    total = jnp.zeros((LEN, D), F32)
    for t in range(ffn_ref.shape[0]):
        inner = inner_ref[t]
        sigma = sigmoid(inner)
        d_inner = (nt(grad, ffn_ref[t, 1]) * (sigma * (1.0 + inner * (1.0 - sigma)))).astype(BF16)
        din_sc[t, rows, :] = d_inner
        total = total + nt(d_inner, ffn_ref[t, 0])
    return total


def middle_kernel(
    lens_ref, mid_ref, x2_ref, cot_ref, np_ref, bn_ref, mix_ref, ffn_ref,
    out_o, d3_o, dn_o, act3_o, gc_o, lng_o, gb_o, chunk_o,
    inner_sc, act_sc, din_sc, n4_sc, g2_sc,
):
    step = pl.program_id(0)
    rows = pl.ds(pl.multiple_of(step * LEN, LEN), LEN)
    mask = row_mask(own_length(lens_ref, step))
    mean, inv_std, gain, bias = [bn_ref[i : i + 1, :] for i in range(4)]
    xhat = (mid_ref[...] - mean) * inv_std
    normal = xhat * gain + bias
    sigma = sigmoid(normal)
    act3 = (normal * sigma * mask).astype(BF16)
    act3_o[...] = act3
    x3 = x2_ref[...] + nn(act3, mix_ref[6])
    n4 = (standardize(x3)[0] * np_ref[3, 0:1, :] + np_ref[3, 1:2, :]).astype(BF16)
    n4_sc[rows, :] = n4
    total = jnp.zeros((LEN, D), F32)
    for t in range(ffn_ref.shape[0]):
        inner = nn(n4, ffn_ref[t, 0])
        inner_sc[t] = inner
        active = (inner * sigmoid(inner)).astype(BF16)
        act_sc[t, rows, :] = active
        total = total + nn(active, ffn_ref[t, 1])
    x4 = x3 + 0.5 * total
    out_o[...] = (standardize(x4)[0] * np_ref[4, 0:1, :] + np_ref[4, 1:2, :]).astype(BF16)
    d4, gain4, bias4 = norm_back(x4, np_ref[4, 0:1, :], cot_ref[...].astype(F32))
    g2 = (0.5 * d4).astype(BF16)
    g2_sc[rows, :] = g2
    d_n4 = ffn_backward(g2, inner_sc, ffn_ref, din_sc, rows)
    d3, gain3, bias3 = norm_back(x3, np_ref[3, 0:1, :], d_n4)
    d3 = d3 + d4
    d3_o[...] = d3
    gc = d3.astype(BF16)
    gc_o[...] = gc
    d_normal = nt(gc, mix_ref[6]) * mask * (sigma * (1.0 + normal * (1.0 - sigma)))
    dn_o[...] = d_normal

    @pl.when(step == 0)
    def _():
        lng_o[...] = jnp.zeros_like(lng_o)
        gb_o[...] = jnp.zeros_like(gb_o)

    for i, part in enumerate((gain3, bias3, gain4, bias4)):
        lng_o[6 + i : 7 + i, :] += part
    gb_o[0:1, :] += jnp.sum(d_normal * xhat, axis=0, keepdims=True)
    gb_o[1:2, :] += jnp.sum(d_normal, axis=0, keepdims=True)

    @pl.when(step == pl.num_programs(0) - 1)
    def _():
        for t in range(ffn_ref.shape[0]):
            chunk_o[t, 0:D, :] = tn(n4_sc[...], din_sc[t]).astype(BF16)
            chunk_o[t, D : 2 * D, :] = tn(g2_sc[...], act_sc[t]).astype(BF16)
            chunk_o[t, 2 * D :, :] = jnp.zeros((ROWS - 2 * D, D), BF16)


def backward_kernel(
    lens_ref, x0_ref, x1_ref, x2_ref, inner_ref, p_ref, q_ref, k_ref, v_ref, vp_ref, gp_ref, mid_ref,
    d3_ref, dn_ref, np_ref, bn_ref, small_ref, mix_ref, ffn_ref, n1_ref, n2_ref, n3_ref, act1_ref,
    mixture_ref, act3_ref, gc_ref, lng_ref,
    ig_o, chunk1_o, chunk2_o,
    pad_g, pad_m, gk_sc, dv_sc, dg_sc, ga_sc, dq_sc, dk_sc, dvv_sc, g1_sc, din_sc, lng_sc,
):
    step = pl.program_id(0)
    rows = pl.ds(pl.multiple_of(step * LEN, LEN), LEN)
    mask = row_mask(own_length(lens_ref, step))

    @pl.when(step == 0)
    def _():
        pad_g[...] = jnp.zeros_like(pad_g)
        pad_m[...] = jnp.zeros_like(pad_m)
        gk_sc[...] = jnp.zeros_like(gk_sc)
        lng_sc[...] = lng_ref[...]

    mean, inv_std, gain, bias, sum_gain, sum_bias, inv_count = [bn_ref[i : i + 1, :] for i in range(7)]
    xhat = (mid_ref[...] - mean) * inv_std
    d_mid = inv_std * gain * (dn_ref[...] - mask * ((sum_bias + xhat * sum_gain) * inv_count))
    value = vp_ref[...]
    sigma = sigmoid(gp_ref[...])
    gated = value * sigma * mask
    d_n3 = jnp.zeros((LEN, D), F32)
    for half in range(2):
        lanes = slice(half * 128, half * 128 + 128)
        pad_g[half, 8 : 8 + LEN, :] = gated[:, lanes]
        pad_m[half, 8 : 8 + LEN, :] = d_mid[:, lanes]
        d_gated = jnp.zeros((LEN, 128), F32)
        mid_half = d_mid[:, lanes]
        for j in range(KS):
            d_gated = d_gated + pad_m[half, 15 - j : 15 - j + LEN, :] * small_ref[j : j + 1, lanes]
            gk_sc[j : j + 1, lanes] += jnp.sum(
                pad_g[half, 1 + j : 1 + j + LEN, :] * mid_half, axis=0, keepdims=True
            )
        d_gated = d_gated * mask
        sig = sigma[:, lanes]
        dv_sc[rows, lanes] = (d_gated * sig).astype(BF16)
        dg_sc[rows, lanes] = (d_gated * value[:, lanes] * sig * (1.0 - sig)).astype(BF16)
    d_n3 = nn(dv_sc[rows, :], mix_ref[4]) + nn(dg_sc[rows, :], mix_ref[5])
    d2, gain2, bias2 = norm_back(x2_ref[...], np_ref[2, 0:1, :], d_n3)
    d2 = d2 + d3_ref[...]
    ga = d2.astype(BF16)
    ga_sc[rows, :] = ga
    d_mix = nt(ga, mix_ref[3]).astype(BF16)
    masks = lane_masks(BF16)
    for half in range(2):
        lanes = slice(half * 128, half * 128 + 128)
        q, k, v, dm = q_ref[:, lanes], k_ref[:, lanes], v_ref[:, lanes], d_mix[:, lanes]
        dq = jnp.zeros((LEN, 128), F32)
        dk = jnp.zeros((LEN, 128), F32)
        dv = jnp.zeros((LEN, 128), F32)
        for side in range(2):
            probs = p_ref[0, 2 * half + side]
            dm_side = dm * masks[side]
            d_probs = nt(dm_side, v)
            dv = dv + tn(probs.astype(BF16), dm_side)
            row_sum = jnp.sum(probs * d_probs, axis=-1, keepdims=True)
            d_scores = (probs * (d_probs - row_sum)).astype(BF16)
            dq = dq + nn(d_scores, k * masks[side])
            dk = dk + tn(d_scores, q * masks[side])
        dq_sc[rows, lanes] = (dq * HEAD ** (-0.5)).astype(BF16)
        dk_sc[rows, lanes] = (dk * HEAD ** (-0.5)).astype(BF16)
        dvv_sc[rows, lanes] = dv.astype(BF16)
    d_n2 = nn(dq_sc[rows, :], mix_ref[0]) + nn(dk_sc[rows, :], mix_ref[1]) + nn(dvv_sc[rows, :], mix_ref[2])
    d1, gain1, bias1 = norm_back(x1_ref[...], np_ref[1, 0:1, :], d_n2)
    d1 = d1 + d2
    g1 = (0.5 * d1).astype(BF16)
    g1_sc[rows, :] = g1
    d_n1 = ffn_backward(g1, inner_ref, ffn_ref, din_sc, rows)
    d0, gain0, bias0 = norm_back(x0_ref[...].astype(F32), np_ref[0, 0:1, :], d_n1)
    ig_o[...] = d0 + d1
    for i, part in enumerate((gain0, bias0, gain1, bias1, gain2, bias2)):
        lng_sc[i : i + 1, :] += part

    @pl.when(step == pl.num_programs(0) - 1)
    def _():
        shards = ffn_ref.shape[0]
        eye = (
            lax.broadcasted_iota(jnp.int32, (16, D), 0) == lax.broadcasted_iota(jnp.int32, (16, D), 1)
        ).astype(BF16)
        pairs = (
            (dq_sc[...], n2_ref[...]),
            (dk_sc[...], n2_ref[...]),
            (dvv_sc[...], n2_ref[...]),
            (mixture_ref[...], ga_sc[...]),
            (dv_sc[...], n3_ref[...]),
            (dg_sc[...], n3_ref[...]),
            (act3_ref[...], gc_ref[...]),
            (gk_sc[...].astype(BF16), eye),
        )
        for i, (left, right) in enumerate(pairs):
            full = tn(left, right).astype(BF16)
            for t in range(shards):
                chunk1_o[t, PADH * i : PADH * (i + 1), :] = full[PADH * t : PADH * (t + 1), :]
        for t in range(shards):
            chunk2_o[t, 0:D, :] = tn(n1_ref[...], din_sc[t]).astype(BF16)
            chunk2_o[t, D : 2 * D, :] = tn(g1_sc[...], act1_ref[t]).astype(BF16)
            chunk2_o[t, 2 * D : 2 * D + 16, :] = lng_sc[...].astype(BF16)
            chunk2_o[t, 2 * D + 16 :, :] = jnp.zeros((ROWS - 2 * D - 16, D), BF16)


def split(a):
    high = a.astype(BF16)
    return high, (a - high.astype(F32)).astype(BF16)


def mul_fine(a, b):
    a_high, a_low = a
    b_high, b_low = b
    return nn(a_high, b_high) + (nn(a_high, b_low) + nn(a_low, b_high))


def eye_of(n):
    return (lax.broadcasted_iota(jnp.int32, (n, n), 0) == lax.broadcasted_iota(jnp.int32, (n, n), 1)).astype(F32)


def next_gap(gap, eye, fine):
    if fine:
        own = split(gap)
        square = split(mul_fine(own, own))
        inner = mul_fine(square, split((15.0 / 256.0) * eye + (1.0 / 256.0) * gap))
        return mul_fine(square, split(0.625 * eye + 0.3125 * gap + inner))
    own = gap.astype(BF16)
    square = nn(own, own).astype(BF16)
    inner = nn(square, ((15.0 / 256.0) * eye + (1.0 / 256.0) * gap).astype(BF16))
    return nn(square, (0.625 * eye + 0.3125 * gap + inner).astype(BF16))


def total_of(a):
    return jnp.sum(jnp.sum(a, axis=1, keepdims=True), axis=0, keepdims=True)


def update_kernel(
    step_ref, tot_ref, red_ref, gbn_ref, fi_ref, fo_ref, ai_ref, ao_ref, ci_ref, dk_ref, co_ref,
    sw_ref, sh_ref, sd_ref, sk_ref, np_ref, ns_ref, bp_ref, bs_ref,
    gn_o, cn_o, cb_o, cfi_o, cfo_o, cai_o, cao_o, cci_o, cdk_o, cco_o,
    nfi_o, nfo_o, nai_o, nao_o, nci_o, ndk_o, nco_o, nn_o, nb_o, nns_o, nbs_o,
    nsw_o, nsh_o, nsd_o, nsk_o,
    gap_f, gap_b, dir_f, dir_b,
):
    steps = jnp.full((1, 1), step_ref[0], jnp.int32).astype(F32)
    rate = PEAK_RATE * jnp.minimum(steps / WARM_STEPS, jnp.sqrt(WARM_STEPS / steps))
    grad_norm = jnp.sqrt(tot_ref[0:1, 0:1])
    threshold = math.sqrt(NPARAM)
    factor = threshold / jnp.maximum(grad_norm, threshold)
    square_factor = factor * factor
    gn_o[...] = jnp.broadcast_to(grad_norm, gn_o.shape)

    c_norm = red_ref[2, 2 * D : 2 * D + 16, :].astype(F32) * factor
    for i in range(5):
        clipped = c_norm[2 * i : 2 * i + 2, :]
        second = 0.5 * ns_ref[i] + 0.5 * clipped * clipped
        cn_o[i] = clipped
        nns_o[i] = second
        nn_o[i] = np_ref[i] - rate * SMALL_RATE * clipped * lax.rsqrt(second)
    c_bn = gbn_ref[0:2, 0:HEAD] * factor
    second = 0.5 * bs_ref[...] + 0.5 * c_bn * c_bn
    cb_o[...] = c_bn
    nbs_o[...] = second
    nb_o[...] = bp_ref[...] - rate * SMALL_RATE * c_bn * lax.rsqrt(second)

    eye_d = eye_of(D)
    scales_f = []
    for i in range(4):
        member, is_out = i // 2, i % 2
        chunk = (2, 0)[member]
        low = red_ref[chunk, is_out * D : is_out * D + D, :]
        wide_c = sw_ref[0, 2 * is_out + member, 0:1, 0:1]
        hidden_c = sd_ref[0, 2 * is_out + member, 0:1, 0:1]
        gram = tn(low, low) * square_factor
        wide = nt(low, low) * square_factor
        nsw_o[0, 2 * is_out + member] = 0.5 * wide_c * eye_d + 0.5 * wide
        nsd_o[0, 2 * is_out + member] = 0.5 * hidden_c * eye_d + 0.5 * gram
        clipped = low.astype(F32) * factor
        if is_out:
            cfo_o[member] = clipped.T
        else:
            cfi_o[member] = clipped
        dir_f[i] = clipped
        trace = total_of(clipped * clipped)
        power = total_of(gram * gram)
        scale = 1.0
        for k, c in enumerate((wide_c, hidden_c)):
            zoom = 2.5 * lax.rsqrt(0.25 * c * c * D + 0.5 * c * trace + 0.25 * power)
            gap_f[2 * i + k] = eye_d - zoom * (0.5 * c * eye_d + 0.5 * gram)
            scale = scale * jnp.sqrt(jnp.sqrt(zoom))
        scales_f.append(scale)

    eye_b = eye_of(4 * PADH)
    row_block = lax.broadcasted_iota(jnp.int32, (4 * PADH, 1), 0) // PADH
    lane_block = lax.broadcasted_iota(jnp.int32, (1, 4 * PADH), 1) // PADH
    same_block = row_block == lane_block
    wide_of = (4, 5, 6, 7, 8, 9, 10, None)
    head_of = (0, 1, 2, 3, 4, 5, 7, 6)
    scales_b = []

    def spread(values):
        column = jnp.zeros((4 * PADH, 1), F32)
        for i, value in enumerate(values):
            column = jnp.where(row_block == i, value, column)
        return column

    for group in range(2):
        low = red_ref[1, group * 4 * PADH : (group + 1) * 4 * PADH, :]
        clipped = low.astype(F32) * factor
        dir_b[group] = clipped
        gram = jnp.where(same_block, nt(low, low), 0.0) * square_factor
        row_trace = jnp.sum(clipped * clipped, axis=1, keepdims=True)
        row_power = jnp.sum(gram * gram, axis=1, keepdims=True)
        wide_cs, head_cs, traces, powers, dims = [], [], [], [], []
        for i in range(4):
            index = group * 4 + i
            part = slice(i * PADH, (i + 1) * PADH)
            piece = low[part, :]
            head_c = sh_ref[0, 0, head_of[index] : head_of[index] + 1, 0:1]
            own_gram = nt(piece, piece)[:HEAD, :HEAD] * square_factor
            nsh_o[0, :, head_of[index], :] = 0.5 * head_c * eye_d[:HEAD, :HEAD] + 0.5 * own_gram
            wide = tn(piece, piece) * square_factor
            if wide_of[index] is None:
                wide_c = sk_ref[0, 0:1, 0:1]
                nsk_o[:, 0, :] = 0.5 * wide_c * eye_d[:KS, :KS] + 0.5 * wide[:KS, :KS]
                dims.append(KS)
            else:
                wide_c = sw_ref[0, wide_of[index], 0:1, 0:1]
                nsw_o[0, wide_of[index]] = 0.5 * wide_c * eye_d + 0.5 * wide
                dims.append(D)
            wide_cs.append(wide_c)
            head_cs.append(head_c)
            traces.append(jnp.sum(row_trace[part], axis=0, keepdims=True))
            powers.append(jnp.sum(row_power[part], axis=0, keepdims=True))
        scale = [1.0] * 4
        for k, (cs, sizes) in enumerate(((wide_cs, dims), (head_cs, [HEAD] * 4))):
            zooms = [
                2.5 * lax.rsqrt(0.25 * c * c * n + 0.5 * c * trace + 0.25 * power)
                for c, n, trace, power in zip(cs, sizes, traces, powers)
            ]
            gap_b[2 * group + k] = eye_b - spread(zooms) * (0.5 * spread(cs) * eye_b + 0.5 * gram)
            scale = [s * jnp.sqrt(jnp.sqrt(zoom)) for s, zoom in zip(scale, zooms)]
        scales_b.append(scale)

    def advance(fine, last):
        for k in range(2):
            for i in range(4):
                gap = gap_f[2 * i + k]
                dir_f[i] = dir_f[i] + 0.25 * nn(dir_f[i].astype(BF16), gap.astype(BF16))
                if not last:
                    gap_f[2 * i + k] = next_gap(gap, eye_d, fine)
            for i in range(2):
                gap = gap_b[2 * i + k]
                dir_b[i] = dir_b[i] + 0.25 * nn(gap.astype(BF16), dir_b[i].astype(BF16))
                if not last:
                    gap_b[2 * i + k] = next_gap(gap, eye_b, fine)

    def fine_step(i, carry):
        advance(True, False)
        return carry

    def coarse_step(i, carry):
        advance(False, False)
        return carry

    lax.fori_loop(0, FINE_ITERS, fine_step, 0)
    lax.fori_loop(0, ROOT_ITERS - 1 - FINE_ITERS, coarse_step, 0)
    advance(False, True)

    def graft(weight, direction):
        size = jnp.sqrt(total_of(weight * weight))
        return rate * GRAFT_SCALE * size / (jnp.sqrt(total_of(direction * direction)) + 1e-06)

    for i in range(4):
        member, is_out = i // 2, i % 2
        direction = dir_f[i] * scales_f[i]
        weight = (fi_ref, fo_ref)[is_out][member]
        if is_out:
            direction = direction.T
        (nfi_o, nfo_o)[is_out][member] = weight - graft(weight, direction) * direction
    for index in range(8):
        group, i = index // 4, index % 4
        part = slice(i * PADH, i * PADH + HEAD)
        direction = dir_b[group][part, :] * scales_b[group][i]
        clipped = red_ref[1, index * PADH : (index + 1) * PADH, :][:HEAD, :].astype(F32) * factor
        if index in (3, 6):
            weight_ref, clip_o, new_o = ((ao_ref, cao_o, nao_o), None, None, (co_ref, cco_o, nco_o))[index - 3]
            clip_o[...] = clipped
            new_o[...] = weight_ref[...] - graft(weight_ref[...], direction) * direction
        elif index == 7:
            turned = direction.T[:KS, :]
            cdk_o[...] = clipped.T[:KS, :]
            ndk_o[...] = dk_ref[...] - graft(dk_ref[...], turned) * turned
        else:
            weight_ref, clip_o, new_o = (ai_ref, cai_o, nai_o) if index < 3 else (ci_ref, cci_o, nci_o)
            at = (index,) if index < 3 else (slice(None), index - 4)
            weight = weight_ref[at]
            clip_o[at] = clipped
            new_o[at] = weight - graft(weight, direction) * direction


def shape(dims, dtype=F32):
    return jax.ShapeDtypeStruct(dims, dtype)


def whole(dims):
    zeros = (0,) * len(dims)
    return pl.BlockSpec(dims, lambda u: zeros)


def tile(width):
    return pl.BlockSpec((LEN, width), lambda u: (u, 0))


SMEM_SPEC = pl.BlockSpec(memory_space=pltpu.SMEM)
VMEM_SPEC = pl.BlockSpec(memory_space=pltpu.VMEM)
PARAMS = pltpu.CompilerParams(vmem_limit_bytes=VMEM_CAP)


def forward_call(lengths, x, norm_params, ffn, mix, small):
    frames = x.shape[0]
    shards = ffn.shape[0]
    utts = frames // LEN
    wide = 4 * PADH
    shard_tile = pl.BlockSpec((shards, LEN, D), lambda u: (0, u, 0))
    return pl.pallas_call(
        forward_kernel,
        grid=(utts,),
        in_specs=[SMEM_SPEC, tile(D), whole(norm_params.shape), whole(ffn.shape), whole(mix.shape), whole(small.shape)],
        out_specs=[
            tile(D), shard_tile, shard_tile, tile(D), tile(D), tile(wide), tile(wide), tile(wide),
            pl.BlockSpec((1, 4, LEN, LEN), lambda u: (u, 0, 0, 0)),
            tile(wide), tile(D), tile(D), tile(wide), tile(wide), tile(wide),
            pl.BlockSpec((1, 8, wide), lambda u: (u, 0, 0)),
        ],
        out_shape=[
            shape((frames, D), BF16), shape((shards, frames, D)), shape((shards, frames, D), BF16),
            shape((frames, D)), shape((frames, D), BF16),
            shape((frames, wide), BF16), shape((frames, wide), BF16), shape((frames, wide), BF16),
            shape((utts, 4, LEN, LEN)), shape((frames, wide), BF16), shape((frames, D)), shape((frames, D), BF16),
            shape((frames, wide)), shape((frames, wide)), shape((frames, wide)), shape((utts, 8, wide)),
        ],
        scratch_shapes=[pltpu.VMEM((2, LEN + 16, 128), F32)],
        compiler_params=PARAMS,
        name="forward_part",
    )(lengths, x, norm_params, ffn, mix, small)


def middle_call(lengths, mid, x2, cot, norm_params, bn, mix, ffn):
    frames = x2.shape[0]
    shards = ffn.shape[0]
    wide = 4 * PADH
    return pl.pallas_call(
        middle_kernel,
        grid=(frames // LEN,),
        in_specs=[
            SMEM_SPEC, tile(wide), tile(D), tile(D), whole(norm_params.shape), whole(bn.shape),
            whole(mix.shape), whole(ffn.shape),
        ],
        out_specs=[
            tile(D), tile(D), tile(wide), tile(wide), tile(D), whole((16, D)), whole((8, wide)),
            whole((shards, ROWS, D)),
        ],
        out_shape=[
            shape((frames, D), BF16), shape((frames, D)), shape((frames, wide)), shape((frames, wide), BF16),
            shape((frames, D), BF16), shape((16, D)), shape((8, wide)), shape((shards, ROWS, D), BF16),
        ],
        scratch_shapes=[
            pltpu.VMEM((shards, LEN, D), F32), pltpu.VMEM((shards, frames, D), BF16),
            pltpu.VMEM((shards, frames, D), BF16), pltpu.VMEM((frames, D), BF16), pltpu.VMEM((frames, D), BF16),
        ],
        compiler_params=PARAMS,
        name="middle_part",
    )(lengths, mid, x2, cot, norm_params, bn, mix, ffn)


def backward_call(lengths, tiles, small_args, wholes):
    x0, x1, x2, inner, probs, q, k, v, vp, gp, mid, d3, dn = tiles
    norm_params, bn, small, mix, ffn = small_args
    frames = x1.shape[0]
    shards = ffn.shape[0]
    wide = 4 * PADH
    half_pad = pltpu.VMEM((2, LEN + 16, 128), F32)
    wide_low = pltpu.VMEM((frames, wide), BF16)
    thin_low = pltpu.VMEM((frames, D), BF16)
    return pl.pallas_call(
        backward_kernel,
        grid=(frames // LEN,),
        in_specs=[
            SMEM_SPEC, tile(D), tile(D), tile(D),
            pl.BlockSpec((shards, LEN, D), lambda u: (0, u, 0)),
            pl.BlockSpec((1, 4, LEN, LEN), lambda u: (u, 0, 0, 0)),
            tile(wide), tile(wide), tile(wide), tile(wide), tile(wide), tile(wide), tile(D), tile(wide),
        ] + [whole(a.shape) for a in small_args] + [whole(a.shape) for a in wholes],
        out_specs=[tile(D), whole((shards, ROWS, D)), whole((shards, ROWS, D))],
        out_shape=[shape((frames, D)), shape((shards, ROWS, D), BF16), shape((shards, ROWS, D), BF16)],
        scratch_shapes=[
            half_pad, half_pad, pltpu.VMEM((16, wide), F32), wide_low, wide_low, thin_low,
            wide_low, wide_low, wide_low, thin_low, pltpu.VMEM((shards, frames, D), BF16), pltpu.VMEM((16, D), F32),
        ],
        compiler_params=PARAMS,
        name="backward_part",
    )(lengths, *tiles, *small_args, *wholes)


def update_call(step_count, total_square, reduced, gbn, weights, stats, norm_params, norm_second, bn_params, bn_second):
    stat_wide, stat_head, stat_hidden, stat_kernel = stats
    corner = lambda a: pl.BlockSpec((1, a.shape[1], 8, 128), lambda i: (0, 0, 0, 0))
    one = lambda a: whole(a.shape)
    n_stat = lambda a: whole(a.shape)
    out_arrays = [
        shape((1, 128)), norm_params, bn_params, *weights, *weights, norm_params, bn_params, norm_params, bn_params,
        stat_wide, stat_head, stat_hidden, stat_kernel,
    ]
    in_arrays = [total_square, reduced, gbn, *weights]
    wide = 4 * PADH
    return pl.pallas_call(
        update_kernel,
        grid=(1,),
        in_specs=[SMEM_SPEC] + [one(a) for a in in_arrays]
        + [corner(stat_wide), one(stat_head), corner(stat_hidden), one(stat_kernel)]
        + [one(a) for a in (norm_params, norm_second, bn_params, bn_second)],
        out_specs=[one(a) for a in out_arrays],
        out_shape=[shape(a.shape) for a in out_arrays],
        scratch_shapes=[
            pltpu.VMEM((8, D, D), F32), pltpu.VMEM((4, wide, wide), F32),
            pltpu.VMEM((4, D, D), F32), pltpu.VMEM((2, wide, D), F32),
        ],
        compiler_params=PARAMS,
        name="update_part",
    )(step_count, *in_arrays, *stats, norm_params, norm_second, bn_params, bn_second)


MESH = pl.DeviceIdType.MESH


def flip(index, bit):
    step = 2 ** bit
    return index + step - 2 * step * ((index // step) % 2)


def greet(peers):
    barrier = pltpu.get_barrier_semaphore()
    for peer in peers:
        pl.semaphore_signal(barrier, inc=1, device_id=peer, device_id_type=MESH)
    pl.semaphore_wait(barrier, len(peers))


def bits_of(count):
    bits = count.bit_length() - 1
    if 2 ** bits != count:
        raise ValueError("axis size")
    return bits


def gather_kernel(
    fi_ref, fo_ref, ai_ref, ao_ref, ci_ref, co_ref, dk_ref, bp_ref,
    ffn1_o, mix_o, ffn2_o, small_o,
    small_sc, send_sem, recv_sem,
):
    t = lax.axis_index("tensor")
    near, far = flip(t, 0), flip(t, 1)
    own = pl.ds(pl.multiple_of(t * PADH, PADH), PADH)
    parts = (
        lambda i: small_sc.at[i],
        lambda i: ffn1_o.at[i],
        lambda i: mix_o.at[:, pl.ds(pl.multiple_of(i * PADH, PADH), PADH), :],
        lambda i: ffn2_o.at[i],
    )

    def copy(part, shard, peer, slot):
        return pltpu.make_async_remote_copy(
            src_ref=part(shard), dst_ref=part(shard), send_sem=send_sem.at[slot], recv_sem=recv_sem.at[slot],
            device_id={"tensor": peer}, device_id_type=MESH,
        )

    small_sc[t] = jnp.zeros((24, 128), F32)
    small_sc[t, 0:KS, 0:HEAD] = dk_ref[...]
    small_sc[t, 16:18, 0:HEAD] = bp_ref[...]
    for m, target in enumerate((ffn1_o, ffn2_o)):
        target[t, 0] = fi_ref[m].astype(BF16)
        target[t, 1] = fo_ref[m].astype(BF16)
    blank = jnp.zeros((PADH - HEAD, D), F32)
    pieces = [ai_ref[m] for m in range(3)] + [ao_ref[...]] + [ci_ref[:, m, :] for m in range(2)] + [co_ref[...]]
    for i, piece in enumerate(pieces):
        mix_o[i, own, :] = jnp.concatenate([piece, blank], axis=0).astype(BF16)
    greet([{"tensor": peer} for peer in (near, far)])
    flights = []
    for g, part in enumerate(parts):
        flights.append((copy(part, t, far, 3 * g), copy(part, t, near, 3 * g + 1)))
        flights[g][0].start()
        flights[g][1].start()
    passes = []
    for g, part in enumerate(parts):
        flights[g][0].wait()
        passes.append(copy(part, far, near, 3 * g + 2))
        passes[g].start()
    for g in range(len(parts)):
        flights[g][1].wait()
        passes[g].wait()
    for i in range(2):
        small_o[:, 128 * i : 128 * i + PADH] = small_sc[2 * i, :, 0:PADH]
        small_o[:, 128 * i + PADH : 128 * i + 128] = small_sc[2 * i + 1, :, 0:PADH]


def gather_call(ffn_in, ffn_out, attn_in, attn_out, conv_in, conv_out, depth_kernel, bn_params):
    shards = lax.axis_size("tensor")
    wide = 4 * PADH
    return pl.pallas_call(
        gather_kernel,
        in_specs=[VMEM_SPEC] * 8,
        out_specs=[VMEM_SPEC] * 4,
        out_shape=[
            shape((shards, 2, D, D), BF16), shape((7, wide, D), BF16), shape((shards, 2, D, D), BF16),
            shape((24, wide)),
        ],
        scratch_shapes=[
            pltpu.VMEM((shards, 24, 128), F32), pltpu.SemaphoreType.DMA((12,)), pltpu.SemaphoreType.DMA((12,)),
        ],
        compiler_params=pltpu.CompilerParams(collective_id=0, has_side_effects=True, vmem_limit_bytes=VMEM_CAP),
        name="gather_part",
    )(ffn_in, ffn_out, attn_in, attn_out, conv_in, conv_out, depth_kernel, bn_params)


def share(axis, count, slots, send_sem, recv_sem):
    me = lax.axis_index(axis)

    def copy(slot, peer, sent):
        return pltpu.make_async_remote_copy(
            src_ref=slots.at[slot], dst_ref=slots.at[slot], send_sem=send_sem.at[sent], recv_sem=recv_sem.at[slot],
            device_id={axis: peer}, device_id_type=MESH,
        )

    def start(k, carry):
        peer = lax.rem(me + k, count)
        copy(me, peer, peer).start()
        return carry

    def finish(k, carry):
        peer = lax.rem(me + k, count)
        copy(me, peer, peer).wait_send()
        copy(peer, peer, peer).wait_recv()
        return carry

    lax.fori_loop(1, count, start, 0)
    lax.fori_loop(1, count, finish, 0)


def greet_axes(counts):
    barrier = pltpu.get_barrier_semaphore()
    for axis, count in counts:
        me = lax.axis_index(axis)

        def signal(k, carry, axis=axis, count=count, me=me):
            pl.semaphore_signal(
                barrier, inc=1, device_id={axis: lax.rem(me + k, count)}, device_id_type=MESH
            )
            return carry

        lax.fori_loop(1, count, signal, 0)
    pl.semaphore_wait(barrier, sum(count - 1 for axis, count in counts))


def pool(slots, count):
    total = lax.fori_loop(0, count, lambda i, a: a + slots[i, 2:3, :], jnp.zeros((1, 4 * PADH), F32))
    mean = (
        lax.fori_loop(0, count, lambda i, a: a + slots[i, 0:1, :] * slots[i, 2:3, :], jnp.zeros((1, 4 * PADH), F32))
        / total
    )

    def power(i, a):
        off = slots[i, 0:1, :] - mean
        return a + slots[i, 1:2, :] + slots[i, 2:3, :] * off * off

    return mean, lax.fori_loop(0, count, power, jnp.zeros((1, 4 * PADH), F32)), total


def moments_kernel(counts, st_ref, small_ref, bn_o, dp_sc, tensor_sc, *sems):
    held = pool(st_ref, st_ref.shape[0])
    slots_of = {"dp": dp_sc, "tensor": tensor_sc}
    greet_axes(counts)
    for i, (axis, count) in enumerate(counts):
        slots = slots_of[axis]
        me = lax.axis_index(axis)
        for row, value in enumerate(held):
            slots[me, row : row + 1, :] = value
        share(axis, count, slots, sems[2 * i], sems[2 * i + 1])
        held = pool(slots, count)
    mean, power, total = held
    bn_o[0:1, :] = mean
    bn_o[1:2, :] = lax.rsqrt(power / total + 1e-05)
    bn_o[2:4, :] = small_ref[16:18, :]
    bn_o[4:6, :] = jnp.zeros((2, 4 * PADH), F32)
    bn_o[6:7, :] = 1.0 / total
    bn_o[7:8, :] = jnp.zeros((1, 4 * PADH), F32)


def totals_kernel(counts, gb_ref, bn_ref, bn_o, dp_sc, tensor_sc, *sems):
    held = gb_ref[...]
    slots_of = {"dp": dp_sc, "tensor": tensor_sc}
    greet_axes(counts)
    for i, (axis, count) in enumerate(counts):
        slots = slots_of[axis]
        slots[lax.axis_index(axis)] = held
        share(axis, count, slots, sems[2 * i], sems[2 * i + 1])
        held = lax.fori_loop(1, count, lambda i, a: a + slots[i], slots[0])
    bn_o[0:4, :] = bn_ref[0:4, :]
    bn_o[4:6, :] = held[0:2, :]
    bn_o[6:8, :] = bn_ref[6:8, :]


def exchange_call(kernel, collective_id, name, *operands):
    counts = tuple((axis, lax.axis_size(axis)) for axis in ("dp", "tensor"))
    wide = 4 * PADH
    return pl.pallas_call(
        functools.partial(kernel, counts),
        in_specs=[VMEM_SPEC] * len(operands),
        out_specs=VMEM_SPEC,
        out_shape=shape((8, wide)),
        scratch_shapes=[pltpu.VMEM((count, 8, wide), F32) for axis, count in counts]
        + [pltpu.SemaphoreType.DMA((count,)) for axis, count in counts for side in range(2)],
        compiler_params=pltpu.CompilerParams(collective_id=collective_id, has_side_effects=True),
        name=name,
    )(*operands)


def reduce_kernel(
    dp_count, c0_ref, c1_ref, c2_ref, bn_ref, red_o, tot_o, gbn_o,
    acc, near_sc, far_sc, dp_sc, out, norm_sc, send_sem, recv_sem, nsend_sem, nrecv_sem,
):
    chunks = (c0_ref, c1_ref, c2_ref)
    t, d = lax.axis_index("tensor"), lax.axis_index("dp")
    near, far = flip(t, 0), flip(t, 1)
    bits = bits_of(dp_count)
    greet(
        [{"tensor": near}, {"tensor": far}, {"tensor": flip(near, 1)}] + [{"dp": flip(d, bit)} for bit in range(bits)]
    )
    plan = []
    length = ROWS
    for bit in range(bits):
        halved = length % 32 == 0
        plan.append((bit, length, halved))
        length = length // 2 if halved else length
    width = 3 + 2 * bits

    def copy(src, dst, chunk, slot, peer):
        return pltpu.make_async_remote_copy(
            src_ref=src, dst_ref=dst, send_sem=send_sem.at[chunk, slot], recv_sem=recv_sem.at[chunk, slot],
            device_id=peer, device_id_type=MESH,
        )

    def add(target, other):
        return (target.astype(F32) + other.astype(F32)).astype(BF16)

    def chain(c):
        source = chunks[c]
        flights = [
            copy(source.at[near], near_sc.at[c, 0], c, 0, {"tensor": near}),
            copy(source.at[flip(near, 1)], near_sc.at[c, 1], c, 1, {"tensor": near}),
        ]
        for flight in flights:
            flight.start()
        yield
        for flight in flights[::-1]:
            flight.wait()
        acc[c, 1] = add(source[far], near_sc[c, 1])
        flight = copy(acc.at[c, 1], far_sc.at[c], c, 2, {"tensor": far})
        flight.start()
        acc[c, 0] = add(source[t], near_sc[c, 0])
        yield
        flight.wait()
        acc[c, 0] = add(acc[c, 0], far_sc[c])
        offset = 0
        trail = []
        for bit, length, halved in plan:
            peer = {"dp": flip(d, bit)}
            slot = 3 + bit
            landing = dp_sc.at[c, bit, pl.ds(0, length // 2 if halved else length)]
            if halved:
                half = length // 2
                side = (d // 2 ** bit) % 2
                keep = pl.ds(pl.multiple_of(offset + side * half, 16), half)
                give = pl.ds(pl.multiple_of(offset + (1 - side) * half, 16), half)
                trail.append((bit, offset))
                offset = offset + side * half
            else:
                half = length
                keep = give = pl.ds(pl.multiple_of(offset, 16), half)
            flight = copy(acc.at[c, 0, give], landing, c, slot, peer)
            flight.start()
            yield
            flight.wait()
            acc[c, 0, keep] = add(acc[c, 0, keep], dp_sc[c, bit, 0:half])
        size = plan[-1][1] // 2 if plan and plan[-1][2] else (plan[-1][1] if plan else ROWS)
        here = pl.ds(pl.multiple_of(offset, 16), size)
        out[c, here] = acc[c, 0, here]
        for bit, before in trail[::-1]:
            here = pl.ds(pl.multiple_of(offset, 16), size)
            flight = copy(out.at[c, here], out.at[c, here], c, 3 + bits + bit, {"dp": flip(d, bit)})
            flight.start()
            yield
            flight.wait()
            offset = before
            size = size * 2

    live = [chain(c) for c in range(len(chunks))]
    for step in range(2 + 2 * bits + len(chunks)):
        for c in range(min(step + 1, len(chunks))):
            next(live[c], None)

    def square_of(a):
        a = a.astype(F32)
        return total_of(a * a)

    own_block = lax.broadcasted_iota(jnp.int32, (1, 4 * PADH), 1) // PADH == t
    gb = bn_ref[4:6, :]
    gbn_o[...] = jnp.zeros_like(gbn_o)
    for i in range(4):
        @pl.when(t == i)
        def _():
            gbn_o[0:2, 0:PADH] = gb[:, i * PADH : (i + 1) * PADH]

    square = square_of(out[0]) + square_of(out[1]) + square_of(out[2, 0 : 2 * D])
    square = square + total_of(jnp.where(own_block, gb * gb, 0.0))
    norm_sc[t] = jnp.broadcast_to(square, (8, 128))
    share("tensor", 4, norm_sc, nsend_sem, nrecv_sem)
    total = norm_sc[0] + norm_sc[1] + norm_sc[2] + norm_sc[3]
    tot_o[...] = total + jnp.broadcast_to(square_of(out[2, 2 * D : 2 * D + 16]), (8, 128))
    red_o[...] = out[...]


def reduce_call(chunks, bn):
    dp_count = lax.axis_size("dp")
    bits = bits_of(dp_count)
    width = 3 + 2 * bits
    low = lambda *dims: pltpu.VMEM(dims + (ROWS, D), BF16)
    dma = pltpu.SemaphoreType.DMA
    return pl.pallas_call(
        functools.partial(reduce_kernel, dp_count),
        in_specs=[VMEM_SPEC] * 4,
        out_specs=[VMEM_SPEC] * 3,
        out_shape=[shape((3, ROWS, D), BF16), shape((8, 128)), shape((8, 128))],
        scratch_shapes=[
            low(3, 2), low(3, 2), low(3), pltpu.VMEM((3, bits, ROWS // 2, D), BF16), low(3),
            pltpu.VMEM((4, 8, 128), F32), dma((3, width)), dma((3, width)), dma((4,)), dma((4,)),
        ],
        compiler_params=pltpu.CompilerParams(collective_id=3, has_side_effects=True, vmem_limit_bytes=VMEM_CAP),
        name="reduce_part",
    )(*chunks, bn)


def local(
    block_input, lengths, cotangent, norm_params, bn_params, ffn_in, ffn_out, attn_in, attn_out, conv_in,
    depth_kernel, conv_out, stat_wide, stat_head, stat_hidden, stat_kernel, norm_second, bn_second, step_count,
):
    attn_in, conv_in = attn_in.swapaxes(1, 2), conv_in.transpose(2, 0, 1)
    stat_head, stat_kernel = stat_head.swapaxes(1, 2), stat_kernel.swapaxes(0, 1)
    ffn_one, mix, ffn_two, small = gather_call(
        ffn_in, ffn_out, attn_in, attn_out, conv_in, conv_out, depth_kernel, bn_params
    )
    (n1, inner1, act1, x1, n2, q, k, v, probs, mixture, x2, n3, vp, gp, mid, stat) = forward_call(
        lengths, block_input, norm_params, ffn_one, mix, small
    )
    bn = exchange_call(moments_kernel, 1, "moments_part", stat, small)
    block_out, d3, dn, act3, gc, lng, gb, chunk0 = middle_call(
        lengths, mid, x2, cotangent, norm_params, bn, mix, ffn_two
    )
    bn = exchange_call(totals_kernel, 2, "totals_part", gb, bn)
    input_grad, chunk1, chunk2 = backward_call(
        lengths,
        (block_input, x1, x2, inner1, probs, q, k, v, vp, gp, mid, d3, dn),
        (norm_params, bn, small, mix, ffn_one),
        (n1, n2, n3, act1, mixture, act3, gc, lng),
    )
    reduced, total_square, gbn = reduce_call((chunk0, chunk1, chunk2), bn)
    weights = (ffn_in, ffn_out, attn_in, attn_out, conv_in, depth_kernel, conv_out)
    outs = list(
        update_call(
            step_count, total_square, reduced, gbn, weights, (stat_wide, stat_head, stat_hidden, stat_kernel),
            norm_params, norm_second, bn_params, bn_second,
        )
    )
    for i in (5, 12):
        outs[i] = outs[i].swapaxes(1, 2)
    for i in (7, 14):
        outs[i] = outs[i].transpose(1, 2, 0)
    outs[22] = outs[22].swapaxes(1, 2)
    outs[24] = outs[24].swapaxes(0, 1)
    return (block_out, input_grad, outs[0][0, :1], *outs[1:])


def solution(mesh):
    weights_specs = (
        P(None, None, "tensor"), P(None, "tensor", None), P(None, None, "tensor"), P("tensor", None),
        P(None, None, "tensor"), P(None, "tensor"), P("tensor", None),
    )
    stat_specs = (
        P("tensor", None, None, None), P("tensor", None, None, None), P("tensor", None, None, None),
        P("tensor", None, None),
    )
    frames = P(("dp", "tensor"), None)
    channels = P(None, "tensor")
    return jax.shard_map(
        local,
        mesh=mesh,
        in_specs=(frames, P("dp"), frames, P(), channels, *weights_specs, *stat_specs, P(), channels, P()),
        out_specs=(
            frames, frames, P(), P(), channels, *weights_specs, *weights_specs, P(), channels, P(), channels,
            *stat_specs,
        ),
        check_vma=False,
    )
```

```python
import functools
import math

import jax
import jax.numpy as jnp
from jax import lax
from jax.experimental import pallas as pl
from jax.experimental.pallas import tpu as pltpu
from jax.sharding import PartitionSpec as P

D = 240
KS = 15
LEN = 192
HEAD = 60
PADH = 64
ROOT_ITERS = 8
NPARAM = 1331280
PEAK_RATE = 2.0
WARM_STEPS = 4.0
SMALL_RATE = 0.3
GRAFT_SCALE = 0.6
NEG_FILL = -1000000000.0
ROWS = 512
VMEM_CAP = 60 * 1024 * 1024

F32 = jnp.float32
BF16 = jnp.bfloat16


def nn(a, b):
    return lax.dot_general(a, b, (((1,), (0,)), ((), ())), preferred_element_type=F32)


def nt(a, b):
    return lax.dot_general(a, b, (((1,), (1,)), ((), ())), preferred_element_type=F32)


def tn(a, b):
    return lax.dot_general(a, b, (((0,), (0,)), ((), ())), preferred_element_type=F32)


def sigmoid(v):
    return 0.5 * jnp.tanh(0.5 * v) + 0.5


def standardize(h):
    centred = h - jnp.sum(h, axis=-1, keepdims=True) * (1.0 / D)
    spread = jnp.sum(centred * centred, axis=-1, keepdims=True) * (1.0 / D)
    inv = lax.rsqrt(spread + 1e-05)
    return centred * inv, inv


def norm_back(h, gain, dy):
    xhat, inv = standardize(h)
    scaled = dy * gain
    mean_a = jnp.sum(scaled, axis=-1, keepdims=True) * (1.0 / D)
    mean_b = jnp.sum(scaled * xhat, axis=-1, keepdims=True) * (1.0 / D)
    dh = inv * (scaled - mean_a - xhat * mean_b)
    return dh, jnp.sum(dy * xhat, axis=0, keepdims=True), jnp.sum(dy, axis=0, keepdims=True)


def row_mask(length):
    return (lax.broadcasted_iota(jnp.int32, (LEN, 1), 0) < length).astype(F32)


def lane_masks(dtype):
    lane = lax.broadcasted_iota(jnp.int32, (1, 128), 1)
    return ((lane < PADH).astype(dtype), (lane >= PADH).astype(dtype))


def own_length(lens_ref, step):
    return lens_ref[lax.axis_index("tensor") * pl.num_programs(0) + step]


def forward_kernel(
    lens_ref, x_ref, np_ref, ffn_ref, mix_ref, small_ref,
    n1_o, inner_o, act_o, x1_o, n2_o, q_o, k_o, v_o, p_o, mix_o, x2_o, n3_o, vp_o, gp_o, mid_o, st_o,
    pad_sc,
):
    step = pl.program_id(0)
    length = own_length(lens_ref, step)
    x0 = x_ref[...].astype(F32)
    n1 = (standardize(x0)[0] * np_ref[0, 0:1, :] + np_ref[0, 1:2, :]).astype(BF16)
    n1_o[...] = n1
    total = jnp.zeros((LEN, D), F32)
    for t in range(ffn_ref.shape[0]):
        inner = nn(n1, ffn_ref[t, 0])
        inner_o[t] = inner
        active = (inner * sigmoid(inner)).astype(BF16)
        act_o[t] = active
        total = total + nn(active, ffn_ref[t, 1])
    x1 = x0 + 0.5 * total
    x1_o[...] = x1
    n2 = (standardize(x1)[0] * np_ref[1, 0:1, :] + np_ref[1, 1:2, :]).astype(BF16)
    n2_o[...] = n2
    q_o[...] = nt(n2, mix_ref[0]).astype(BF16)
    k_o[...] = nt(n2, mix_ref[1]).astype(BF16)
    v_o[...] = nt(n2, mix_ref[2]).astype(BF16)
    key_ok = lax.broadcasted_iota(jnp.int32, (1, LEN), 1) < length
    masks = lane_masks(BF16)
    for half in range(2):
        lanes = slice(half * 128, half * 128 + 128)
        q, k, v = q_o[:, lanes], k_o[:, lanes], v_o[:, lanes]
        mixture = jnp.zeros((LEN, 128), F32)
        for side in range(2):
            scores = nt(q * masks[side], k) * HEAD ** (-0.5)
            scores = jnp.where(key_ok, scores, NEG_FILL)
            exps = jnp.exp(scores - jnp.max(scores, axis=-1, keepdims=True))
            probs = exps * (1.0 / jnp.sum(exps, axis=-1, keepdims=True))
            p_o[0, 2 * half + side] = probs
            mixture = mixture + nn(probs.astype(BF16), v * masks[side])
        mix_o[:, lanes] = mixture.astype(BF16)
    x2 = x1 + nn(mix_o[...], mix_ref[3])
    x2_o[...] = x2
    n3 = (standardize(x2)[0] * np_ref[2, 0:1, :] + np_ref[2, 1:2, :]).astype(BF16)
    n3_o[...] = n3
    value = nt(n3, mix_ref[4])
    gate = nt(n3, mix_ref[5])
    vp_o[...] = value
    gp_o[...] = gate
    mask = row_mask(length)
    gated = value * sigmoid(gate) * mask

    @pl.when(step == 0)
    def _():
        pad_sc[...] = jnp.zeros_like(pad_sc)

    count = length.astype(F32)
    for half in range(2):
        lanes = slice(half * 128, half * 128 + 128)
        pad_sc[half, 8 : 8 + LEN, :] = gated[:, lanes]
        running = jnp.zeros((LEN, 128), F32)
        for j in range(KS):
            running = running + pad_sc[half, 1 + j : 1 + j + LEN, :] * small_ref[j : j + 1, lanes]
        mid_o[:, lanes] = running
        mean = jnp.sum(running * mask, axis=0, keepdims=True) / count
        centred = (running - mean) * mask
        st_o[0, 0:1, lanes] = mean
        st_o[0, 1:2, lanes] = jnp.sum(centred * centred, axis=0, keepdims=True)
        st_o[0, 2:3, lanes] = jnp.full((1, 128), count, F32)
        st_o[0, 3:8, lanes] = jnp.zeros((5, 128), F32)


def ffn_backward(grad, inner_ref, ffn_ref, din_sc, rows):
    total = jnp.zeros((LEN, D), F32)
    for t in range(ffn_ref.shape[0]):
        inner = inner_ref[t]
        sigma = sigmoid(inner)
        d_inner = (nt(grad, ffn_ref[t, 1]) * (sigma * (1.0 + inner * (1.0 - sigma)))).astype(BF16)
        din_sc[t, rows, :] = d_inner
        total = total + nt(d_inner, ffn_ref[t, 0])
    return total


def middle_kernel(
    lens_ref, mid_ref, x2_ref, cot_ref, np_ref, bn_ref, mix_ref, ffn_ref,
    out_o, d3_o, dn_o, act3_o, gc_o, lng_o, gb_o, chunk_o,
    inner_sc, act_sc, din_sc, n4_sc, g2_sc,
):
    step = pl.program_id(0)
    rows = pl.ds(pl.multiple_of(step * LEN, LEN), LEN)
    mask = row_mask(own_length(lens_ref, step))
    mean, inv_std, gain, bias = [bn_ref[i : i + 1, :] for i in range(4)]
    xhat = (mid_ref[...] - mean) * inv_std
    normal = xhat * gain + bias
    sigma = sigmoid(normal)
    act3 = (normal * sigma * mask).astype(BF16)
    act3_o[...] = act3
    x3 = x2_ref[...] + nn(act3, mix_ref[6])
    n4 = (standardize(x3)[0] * np_ref[3, 0:1, :] + np_ref[3, 1:2, :]).astype(BF16)
    n4_sc[rows, :] = n4
    total = jnp.zeros((LEN, D), F32)
    for t in range(ffn_ref.shape[0]):
        inner = nn(n4, ffn_ref[t, 0])
        inner_sc[t] = inner
        active = (inner * sigmoid(inner)).astype(BF16)
        act_sc[t, rows, :] = active
        total = total + nn(active, ffn_ref[t, 1])
    x4 = x3 + 0.5 * total
    out_o[...] = (standardize(x4)[0] * np_ref[4, 0:1, :] + np_ref[4, 1:2, :]).astype(BF16)
    d4, gain4, bias4 = norm_back(x4, np_ref[4, 0:1, :], cot_ref[...].astype(F32))
    g2 = (0.5 * d4).astype(BF16)
    g2_sc[rows, :] = g2
    d_n4 = ffn_backward(g2, inner_sc, ffn_ref, din_sc, rows)
    d3, gain3, bias3 = norm_back(x3, np_ref[3, 0:1, :], d_n4)
    d3 = d3 + d4
    d3_o[...] = d3
    gc = d3.astype(BF16)
    gc_o[...] = gc
    d_normal = nt(gc, mix_ref[6]) * mask * (sigma * (1.0 + normal * (1.0 - sigma)))
    dn_o[...] = d_normal

    @pl.when(step == 0)
    def _():
        lng_o[...] = jnp.zeros_like(lng_o)
        gb_o[...] = jnp.zeros_like(gb_o)

    for i, part in enumerate((gain3, bias3, gain4, bias4)):
        lng_o[6 + i : 7 + i, :] += part
    gb_o[0:1, :] += jnp.sum(d_normal * xhat, axis=0, keepdims=True)
    gb_o[1:2, :] += jnp.sum(d_normal, axis=0, keepdims=True)

    @pl.when(step == pl.num_programs(0) - 1)
    def _():
        for t in range(ffn_ref.shape[0]):
            chunk_o[t, 0:D, :] = tn(n4_sc[...], din_sc[t]).astype(BF16)
            chunk_o[t, D : 2 * D, :] = tn(g2_sc[...], act_sc[t]).astype(BF16)
            chunk_o[t, 2 * D :, :] = jnp.zeros((ROWS - 2 * D, D), BF16)


def backward_kernel(
    lens_ref, x0_ref, x1_ref, x2_ref, inner_ref, p_ref, q_ref, k_ref, v_ref, vp_ref, gp_ref, mid_ref,
    d3_ref, dn_ref, np_ref, bn_ref, small_ref, mix_ref, ffn_ref, n1_ref, n2_ref, n3_ref, act1_ref,
    mixture_ref, act3_ref, gc_ref, lng_ref,
    ig_o, chunk1_o, chunk2_o,
    pad_g, pad_m, gk_sc, dv_sc, dg_sc, ga_sc, dq_sc, dk_sc, dvv_sc, g1_sc, din_sc, lng_sc,
):
    step = pl.program_id(0)
    rows = pl.ds(pl.multiple_of(step * LEN, LEN), LEN)
    mask = row_mask(own_length(lens_ref, step))

    @pl.when(step == 0)
    def _():
        pad_g[...] = jnp.zeros_like(pad_g)
        pad_m[...] = jnp.zeros_like(pad_m)
        gk_sc[...] = jnp.zeros_like(gk_sc)
        lng_sc[...] = lng_ref[...]

    mean, inv_std, gain, bias, sum_gain, sum_bias, inv_count = [bn_ref[i : i + 1, :] for i in range(7)]
    xhat = (mid_ref[...] - mean) * inv_std
    d_mid = inv_std * gain * (dn_ref[...] - mask * ((sum_bias + xhat * sum_gain) * inv_count))
    value = vp_ref[...]
    sigma = sigmoid(gp_ref[...])
    gated = value * sigma * mask
    d_n3 = jnp.zeros((LEN, D), F32)
    for half in range(2):
        lanes = slice(half * 128, half * 128 + 128)
        pad_g[half, 8 : 8 + LEN, :] = gated[:, lanes]
        pad_m[half, 8 : 8 + LEN, :] = d_mid[:, lanes]
        d_gated = jnp.zeros((LEN, 128), F32)
        mid_half = d_mid[:, lanes]
        for j in range(KS):
            d_gated = d_gated + pad_m[half, 15 - j : 15 - j + LEN, :] * small_ref[j : j + 1, lanes]
            gk_sc[j : j + 1, lanes] += jnp.sum(
                pad_g[half, 1 + j : 1 + j + LEN, :] * mid_half, axis=0, keepdims=True
            )
        d_gated = d_gated * mask
        sig = sigma[:, lanes]
        dv_sc[rows, lanes] = (d_gated * sig).astype(BF16)
        dg_sc[rows, lanes] = (d_gated * value[:, lanes] * sig * (1.0 - sig)).astype(BF16)
    d_n3 = nn(dv_sc[rows, :], mix_ref[4]) + nn(dg_sc[rows, :], mix_ref[5])
    d2, gain2, bias2 = norm_back(x2_ref[...], np_ref[2, 0:1, :], d_n3)
    d2 = d2 + d3_ref[...]
    ga = d2.astype(BF16)
    ga_sc[rows, :] = ga
    d_mix = nt(ga, mix_ref[3]).astype(BF16)
    masks = lane_masks(BF16)
    for half in range(2):
        lanes = slice(half * 128, half * 128 + 128)
        q, k, v, dm = q_ref[:, lanes], k_ref[:, lanes], v_ref[:, lanes], d_mix[:, lanes]
        dq = jnp.zeros((LEN, 128), F32)
        dk = jnp.zeros((LEN, 128), F32)
        dv = jnp.zeros((LEN, 128), F32)
        for side in range(2):
            probs = p_ref[0, 2 * half + side]
            dm_side = dm * masks[side]
            d_probs = nt(dm_side, v)
            dv = dv + tn(probs.astype(BF16), dm_side)
            row_sum = jnp.sum(probs * d_probs, axis=-1, keepdims=True)
            d_scores = (probs * (d_probs - row_sum)).astype(BF16)
            dq = dq + nn(d_scores, k * masks[side])
            dk = dk + tn(d_scores, q * masks[side])
        dq_sc[rows, lanes] = (dq * HEAD ** (-0.5)).astype(BF16)
        dk_sc[rows, lanes] = (dk * HEAD ** (-0.5)).astype(BF16)
        dvv_sc[rows, lanes] = dv.astype(BF16)
    d_n2 = nn(dq_sc[rows, :], mix_ref[0]) + nn(dk_sc[rows, :], mix_ref[1]) + nn(dvv_sc[rows, :], mix_ref[2])
    d1, gain1, bias1 = norm_back(x1_ref[...], np_ref[1, 0:1, :], d_n2)
    d1 = d1 + d2
    g1 = (0.5 * d1).astype(BF16)
    g1_sc[rows, :] = g1
    d_n1 = ffn_backward(g1, inner_ref, ffn_ref, din_sc, rows)
    d0, gain0, bias0 = norm_back(x0_ref[...].astype(F32), np_ref[0, 0:1, :], d_n1)
    ig_o[...] = d0 + d1
    for i, part in enumerate((gain0, bias0, gain1, bias1, gain2, bias2)):
        lng_sc[i : i + 1, :] += part

    @pl.when(step == pl.num_programs(0) - 1)
    def _():
        shards = ffn_ref.shape[0]
        eye = (
            lax.broadcasted_iota(jnp.int32, (16, D), 0) == lax.broadcasted_iota(jnp.int32, (16, D), 1)
        ).astype(BF16)
        pairs = (
            (dq_sc[...], n2_ref[...]),
            (dk_sc[...], n2_ref[...]),
            (dvv_sc[...], n2_ref[...]),
            (mixture_ref[...], ga_sc[...]),
            (dv_sc[...], n3_ref[...]),
            (dg_sc[...], n3_ref[...]),
            (act3_ref[...], gc_ref[...]),
            (gk_sc[...].astype(BF16), eye),
        )
        for i, (left, right) in enumerate(pairs):
            full = tn(left, right).astype(BF16)
            for t in range(shards):
                chunk1_o[t, PADH * i : PADH * (i + 1), :] = full[PADH * t : PADH * (t + 1), :]
        for t in range(shards):
            chunk2_o[t, 0:D, :] = tn(n1_ref[...], din_sc[t]).astype(BF16)
            chunk2_o[t, D : 2 * D, :] = tn(g1_sc[...], act1_ref[t]).astype(BF16)
            chunk2_o[t, 2 * D : 2 * D + 16, :] = lng_sc[...].astype(BF16)
            chunk2_o[t, 2 * D + 16 :, :] = jnp.zeros((ROWS - 2 * D - 16, D), BF16)


def split(a):
    high = a.astype(BF16)
    return high, (a - high.astype(F32)).astype(BF16)


def stacked(lefts, right):
    full = nn(jnp.concatenate(lefts, axis=0), right)
    places, at = [], 0
    for left in lefts:
        places.append(full[at : at + left.shape[0]])
        at += left.shape[0]
    return places


def mul_fine(a, b, rider=None):
    high, cross, *rest = stacked([*a] + ([] if rider is None else [rider]), b[0])
    return (high + (nn(a[0], b[1]) + cross), *rest)


def eye_of(n):
    return (lax.broadcasted_iota(jnp.int32, (n, n), 0) == lax.broadcasted_iota(jnp.int32, (n, n), 1)).astype(F32)


def next_power(own, direction, fine):
    rider = direction.astype(BF16)
    if fine:
        parts = split(own)
        square, moved = mul_fine(parts, parts, rider)
        step = 0.0625 * square - 0.625 * own
        halves = split(step)
        once = mul_fine(halves, parts)[0]
        twice = mul_fine(halves, split(once))[0]
    else:
        low = own.astype(BF16)
        square, moved = stacked([low, rider], low)
        step = (0.0625 * square - 0.625 * own).astype(BF16)
        once = nn(step, low)
        twice = nn(step, once.astype(BF16))
    return 2.44140625 * own + 3.125 * once + twice, 1.25 * direction - 0.25 * moved


def total_of(a):
    return jnp.sum(jnp.sum(a, axis=1, keepdims=True), axis=0, keepdims=True)


def update_kernel(
    step_ref, tot_ref, red_ref, gbn_ref, fi_ref, fo_ref, ai_ref, ao_ref, ci_ref, dk_ref, co_ref,
    sw_ref, sh_ref, sd_ref, sk_ref, np_ref, ns_ref, bp_ref, bs_ref,
    gn_o, cn_o, cb_o, cfi_o, cfo_o, cai_o, cao_o, cci_o, cdk_o, cco_o,
    nfi_o, nfo_o, nai_o, nao_o, nci_o, ndk_o, nco_o, nn_o, nb_o, nns_o, nbs_o,
    nsw_o, nsh_o, nsd_o, nsk_o,
    mat_f, mat_b, dir_f, dir_b,
):
    steps = jnp.full((1, 1), step_ref[0], jnp.int32).astype(F32)
    rate = PEAK_RATE * jnp.minimum(steps / WARM_STEPS, jnp.sqrt(WARM_STEPS / steps))
    grad_norm = jnp.sqrt(tot_ref[0:1, 0:1])
    threshold = math.sqrt(NPARAM)
    factor = threshold / jnp.maximum(grad_norm, threshold)
    square_factor = factor * factor
    gn_o[...] = jnp.broadcast_to(grad_norm, gn_o.shape)

    c_norm = red_ref[2, 2 * D : 2 * D + 16, :].astype(F32) * factor
    for i in range(5):
        clipped = c_norm[2 * i : 2 * i + 2, :]
        second = 0.5 * ns_ref[i] + 0.5 * clipped * clipped
        cn_o[i] = clipped
        nns_o[i] = second
        nn_o[i] = np_ref[i] - rate * SMALL_RATE * clipped * lax.rsqrt(second)
    c_bn = gbn_ref[0:2, 0:HEAD] * factor
    second = 0.5 * bs_ref[...] + 0.5 * c_bn * c_bn
    cb_o[...] = c_bn
    nbs_o[...] = second
    nb_o[...] = bp_ref[...] - rate * SMALL_RATE * c_bn * lax.rsqrt(second)

    eye_d = eye_of(D)
    scales_f = []
    for i in range(4):
        member, is_out = i // 2, i % 2
        chunk = (2, 0)[member]
        low = red_ref[chunk, is_out * D : is_out * D + D, :]
        wide_c = sw_ref[0, 2 * is_out + member, 0:1, 0:1]
        hidden_c = sd_ref[0, 2 * is_out + member, 0:1, 0:1]
        gram = tn(low, low) * square_factor
        wide = nt(low, low) * square_factor
        nsw_o[0, 2 * is_out + member] = 0.5 * wide_c * eye_d + 0.5 * wide
        nsd_o[0, 2 * is_out + member] = 0.5 * hidden_c * eye_d + 0.5 * gram
        clipped = low.astype(F32) * factor
        if is_out:
            cfo_o[member] = clipped.T
        else:
            cfi_o[member] = clipped
        dir_f[i] = clipped
        trace = total_of(clipped * clipped)
        power = total_of(gram * gram)
        scale = 1.0
        for k, c in enumerate((wide_c, hidden_c)):
            zoom = 2.5 * lax.rsqrt(0.25 * c * c * D + 0.5 * c * trace + 0.25 * power)
            mat_f[2 * i + k] = zoom * (0.5 * c * eye_d + 0.5 * gram)
            scale = scale * jnp.sqrt(jnp.sqrt(zoom))
        scales_f.append(scale)

    eye_b = eye_of(4 * PADH)
    row_block = lax.broadcasted_iota(jnp.int32, (4 * PADH, 1), 0) // PADH
    lane_block = lax.broadcasted_iota(jnp.int32, (1, 4 * PADH), 1) // PADH
    same_block = row_block == lane_block
    wide_of = (4, 5, 6, 7, 8, 9, 10, None)
    head_of = (0, 1, 2, 3, 4, 5, 7, 6)
    scales_b = []

    def spread(values):
        column = jnp.zeros((4 * PADH, 1), F32)
        for i, value in enumerate(values):
            column = jnp.where(row_block == i, value, column)
        return column

    for group in range(2):
        low = red_ref[1, group * 4 * PADH : (group + 1) * 4 * PADH, :]
        clipped = low.astype(F32) * factor
        dir_b[group] = clipped.T
        gram = jnp.where(same_block, nt(low, low), 0.0) * square_factor
        row_trace = jnp.sum(clipped * clipped, axis=1, keepdims=True)
        row_power = jnp.sum(gram * gram, axis=1, keepdims=True)
        wide_cs, head_cs, traces, powers, dims = [], [], [], [], []
        for i in range(4):
            index = group * 4 + i
            part = slice(i * PADH, (i + 1) * PADH)
            piece = low[part, :]
            head_c = sh_ref[0, 0, head_of[index] : head_of[index] + 1, 0:1]
            own_gram = nt(piece, piece)[:HEAD, :HEAD] * square_factor
            nsh_o[0, :, head_of[index], :] = 0.5 * head_c * eye_d[:HEAD, :HEAD] + 0.5 * own_gram
            wide = tn(piece, piece) * square_factor
            if wide_of[index] is None:
                wide_c = sk_ref[0, 0:1, 0:1]
                nsk_o[:, 0, :] = 0.5 * wide_c * eye_d[:KS, :KS] + 0.5 * wide[:KS, :KS]
                dims.append(KS)
            else:
                wide_c = sw_ref[0, wide_of[index], 0:1, 0:1]
                nsw_o[0, wide_of[index]] = 0.5 * wide_c * eye_d + 0.5 * wide
                dims.append(D)
            wide_cs.append(wide_c)
            head_cs.append(head_c)
            traces.append(jnp.sum(row_trace[part], axis=0, keepdims=True))
            powers.append(jnp.sum(row_power[part], axis=0, keepdims=True))
        scale = [1.0] * 4
        for k, (cs, sizes) in enumerate(((wide_cs, dims), (head_cs, [HEAD] * 4))):
            zooms = [
                2.5 * lax.rsqrt(0.25 * c * c * n + 0.5 * c * trace + 0.25 * power)
                for c, n, trace, power in zip(cs, sizes, traces, powers)
            ]
            mat_b[2 * group + k] = spread(zooms) * (0.5 * spread(cs) * eye_b + 0.5 * gram)
            scale = [s * jnp.sqrt(jnp.sqrt(zoom)) for s, zoom in zip(scale, zooms)]
        scales_b.append(scale)

    def advance(fine):
        for k in range(2):
            for mats, dirs, count in ((mat_f, dir_f, 4), (mat_b, dir_b, 2)):
                for i in range(count):
                    mats[2 * i + k], dirs[i] = next_power(mats[2 * i + k], dirs[i], fine)

    def coarse_step(i, carry):
        advance(False)
        return carry

    advance(True)
    lax.fori_loop(0, ROOT_ITERS - 2, coarse_step, 0)
    for k in range(2):
        for mats, dirs, count in ((mat_f, dir_f, 4), (mat_b, dir_b, 2)):
            for i in range(count):
                moved = nn(dirs[i].astype(BF16), mats[2 * i + k].astype(BF16))
                dirs[i] = 1.25 * dirs[i] - 0.25 * moved

    def graft(weight, direction):
        size = jnp.sqrt(total_of(weight * weight))
        return rate * GRAFT_SCALE * size / (jnp.sqrt(total_of(direction * direction)) + 1e-06)

    for i in range(4):
        member, is_out = i // 2, i % 2
        direction = dir_f[i] * scales_f[i]
        weight = (fi_ref, fo_ref)[is_out][member]
        if is_out:
            direction = direction.T
        (nfi_o, nfo_o)[is_out][member] = weight - graft(weight, direction) * direction
    turned_b = [dir_b[group].T for group in range(2)]
    for index in range(8):
        group, i = index // 4, index % 4
        part = slice(i * PADH, i * PADH + HEAD)
        direction = turned_b[group][part, :] * scales_b[group][i]
        clipped = red_ref[1, index * PADH : (index + 1) * PADH, :][:HEAD, :].astype(F32) * factor
        if index in (3, 6):
            weight_ref, clip_o, new_o = ((ao_ref, cao_o, nao_o), None, None, (co_ref, cco_o, nco_o))[index - 3]
            clip_o[...] = clipped
            new_o[...] = weight_ref[...] - graft(weight_ref[...], direction) * direction
        elif index == 7:
            turned = direction.T[:KS, :]
            cdk_o[...] = clipped.T[:KS, :]
            ndk_o[...] = dk_ref[...] - graft(dk_ref[...], turned) * turned
        else:
            weight_ref, clip_o, new_o = (ai_ref, cai_o, nai_o) if index < 3 else (ci_ref, cci_o, nci_o)
            at = (index,) if index < 3 else (slice(None), index - 4)
            weight = weight_ref[at]
            clip_o[at] = clipped
            new_o[at] = weight - graft(weight, direction) * direction


def shape(dims, dtype=F32):
    return jax.ShapeDtypeStruct(dims, dtype)


def whole(dims):
    zeros = (0,) * len(dims)
    return pl.BlockSpec(dims, lambda u: zeros)


def tile(width):
    return pl.BlockSpec((LEN, width), lambda u: (u, 0))


SMEM_SPEC = pl.BlockSpec(memory_space=pltpu.SMEM)
VMEM_SPEC = pl.BlockSpec(memory_space=pltpu.VMEM)
PARAMS = pltpu.CompilerParams(vmem_limit_bytes=VMEM_CAP)


def forward_call(lengths, x, norm_params, ffn, mix, small):
    frames = x.shape[0]
    shards = ffn.shape[0]
    utts = frames // LEN
    wide = 4 * PADH
    shard_tile = pl.BlockSpec((shards, LEN, D), lambda u: (0, u, 0))
    return pl.pallas_call(
        forward_kernel,
        grid=(utts,),
        in_specs=[SMEM_SPEC, tile(D), whole(norm_params.shape), whole(ffn.shape), whole(mix.shape), whole(small.shape)],
        out_specs=[
            tile(D), shard_tile, shard_tile, tile(D), tile(D), tile(wide), tile(wide), tile(wide),
            pl.BlockSpec((1, 4, LEN, LEN), lambda u: (u, 0, 0, 0)),
            tile(wide), tile(D), tile(D), tile(wide), tile(wide), tile(wide),
            pl.BlockSpec((1, 8, wide), lambda u: (u, 0, 0)),
        ],
        out_shape=[
            shape((frames, D), BF16), shape((shards, frames, D)), shape((shards, frames, D), BF16),
            shape((frames, D)), shape((frames, D), BF16),
            shape((frames, wide), BF16), shape((frames, wide), BF16), shape((frames, wide), BF16),
            shape((utts, 4, LEN, LEN)), shape((frames, wide), BF16), shape((frames, D)), shape((frames, D), BF16),
            shape((frames, wide)), shape((frames, wide)), shape((frames, wide)), shape((utts, 8, wide)),
        ],
        scratch_shapes=[pltpu.VMEM((2, LEN + 16, 128), F32)],
        compiler_params=PARAMS,
        name="forward_part",
    )(lengths, x, norm_params, ffn, mix, small)


def middle_call(lengths, mid, x2, cot, norm_params, bn, mix, ffn):
    frames = x2.shape[0]
    shards = ffn.shape[0]
    wide = 4 * PADH
    return pl.pallas_call(
        middle_kernel,
        grid=(frames // LEN,),
        in_specs=[
            SMEM_SPEC, tile(wide), tile(D), tile(D), whole(norm_params.shape), whole(bn.shape),
            whole(mix.shape), whole(ffn.shape),
        ],
        out_specs=[
            tile(D), tile(D), tile(wide), tile(wide), tile(D), whole((16, D)), whole((8, wide)),
            whole((shards, ROWS, D)),
        ],
        out_shape=[
            shape((frames, D), BF16), shape((frames, D)), shape((frames, wide)), shape((frames, wide), BF16),
            shape((frames, D), BF16), shape((16, D)), shape((8, wide)), shape((shards, ROWS, D), BF16),
        ],
        scratch_shapes=[
            pltpu.VMEM((shards, LEN, D), F32), pltpu.VMEM((shards, frames, D), BF16),
            pltpu.VMEM((shards, frames, D), BF16), pltpu.VMEM((frames, D), BF16), pltpu.VMEM((frames, D), BF16),
        ],
        compiler_params=PARAMS,
        name="middle_part",
    )(lengths, mid, x2, cot, norm_params, bn, mix, ffn)


def backward_call(lengths, tiles, small_args, wholes):
    x0, x1, x2, inner, probs, q, k, v, vp, gp, mid, d3, dn = tiles
    norm_params, bn, small, mix, ffn = small_args
    frames = x1.shape[0]
    shards = ffn.shape[0]
    wide = 4 * PADH
    half_pad = pltpu.VMEM((2, LEN + 16, 128), F32)
    wide_low = pltpu.VMEM((frames, wide), BF16)
    thin_low = pltpu.VMEM((frames, D), BF16)
    return pl.pallas_call(
        backward_kernel,
        grid=(frames // LEN,),
        in_specs=[
            SMEM_SPEC, tile(D), tile(D), tile(D),
            pl.BlockSpec((shards, LEN, D), lambda u: (0, u, 0)),
            pl.BlockSpec((1, 4, LEN, LEN), lambda u: (u, 0, 0, 0)),
            tile(wide), tile(wide), tile(wide), tile(wide), tile(wide), tile(wide), tile(D), tile(wide),
        ] + [whole(a.shape) for a in small_args] + [whole(a.shape) for a in wholes],
        out_specs=[tile(D), whole((shards, ROWS, D)), whole((shards, ROWS, D))],
        out_shape=[shape((frames, D)), shape((shards, ROWS, D), BF16), shape((shards, ROWS, D), BF16)],
        scratch_shapes=[
            half_pad, half_pad, pltpu.VMEM((16, wide), F32), wide_low, wide_low, thin_low,
            wide_low, wide_low, wide_low, thin_low, pltpu.VMEM((shards, frames, D), BF16), pltpu.VMEM((16, D), F32),
        ],
        compiler_params=PARAMS,
        name="backward_part",
    )(lengths, *tiles, *small_args, *wholes)


def update_call(step_count, total_square, reduced, gbn, weights, stats, norm_params, norm_second, bn_params, bn_second):
    stat_wide, stat_head, stat_hidden, stat_kernel = stats
    corner = lambda a: pl.BlockSpec((1, a.shape[1], 8, 128), lambda i: (0, 0, 0, 0))
    one = lambda a: whole(a.shape)
    n_stat = lambda a: whole(a.shape)
    out_arrays = [
        shape((1, 128)), norm_params, bn_params, *weights, *weights, norm_params, bn_params, norm_params, bn_params,
        stat_wide, stat_head, stat_hidden, stat_kernel,
    ]
    in_arrays = [total_square, reduced, gbn, *weights]
    wide = 4 * PADH
    return pl.pallas_call(
        update_kernel,
        grid=(1,),
        in_specs=[SMEM_SPEC] + [one(a) for a in in_arrays]
        + [corner(stat_wide), one(stat_head), corner(stat_hidden), one(stat_kernel)]
        + [one(a) for a in (norm_params, norm_second, bn_params, bn_second)],
        out_specs=[one(a) for a in out_arrays],
        out_shape=[shape(a.shape) for a in out_arrays],
        scratch_shapes=[
            pltpu.VMEM((8, D, D), F32), pltpu.VMEM((4, wide, wide), F32),
            pltpu.VMEM((4, D, D), F32), pltpu.VMEM((2, D, wide), F32),
        ],
        compiler_params=PARAMS,
        name="update_part",
    )(step_count, *in_arrays, *stats, norm_params, norm_second, bn_params, bn_second)


MESH = pl.DeviceIdType.MESH


def flip(index, bit):
    step = 2 ** bit
    return index + step - 2 * step * ((index // step) % 2)


def greet(peers):
    barrier = pltpu.get_barrier_semaphore()
    for peer in peers:
        pl.semaphore_signal(barrier, inc=1, device_id=peer, device_id_type=MESH)
    pl.semaphore_wait(barrier, len(peers))


def bits_of(count):
    bits = count.bit_length() - 1
    if 2 ** bits != count:
        raise ValueError("axis size")
    return bits


def gather_kernel(
    fi_ref, fo_ref, ai_ref, ao_ref, ci_ref, co_ref, dk_ref, bp_ref,
    ffn1_o, mix_o, ffn2_o, small_o,
    small_sc, send_sem, recv_sem,
):
    t = lax.axis_index("tensor")
    near, far = flip(t, 0), flip(t, 1)
    own = pl.ds(pl.multiple_of(t * PADH, PADH), PADH)
    parts = (
        lambda i: small_sc.at[i],
        lambda i: ffn1_o.at[i],
        lambda i: mix_o.at[:, pl.ds(pl.multiple_of(i * PADH, PADH), PADH), :],
        lambda i: ffn2_o.at[i],
    )

    def copy(part, shard, peer, slot):
        return pltpu.make_async_remote_copy(
            src_ref=part(shard), dst_ref=part(shard), send_sem=send_sem.at[slot], recv_sem=recv_sem.at[slot],
            device_id={"tensor": peer}, device_id_type=MESH,
        )

    small_sc[t] = jnp.zeros((24, 128), F32)
    small_sc[t, 0:KS, 0:HEAD] = dk_ref[...]
    small_sc[t, 16:18, 0:HEAD] = bp_ref[...]
    for m, target in enumerate((ffn1_o, ffn2_o)):
        target[t, 0] = fi_ref[m].astype(BF16)
        target[t, 1] = fo_ref[m].astype(BF16)
    blank = jnp.zeros((PADH - HEAD, D), F32)
    pieces = [ai_ref[m] for m in range(3)] + [ao_ref[...]] + [ci_ref[:, m, :] for m in range(2)] + [co_ref[...]]
    for i, piece in enumerate(pieces):
        mix_o[i, own, :] = jnp.concatenate([piece, blank], axis=0).astype(BF16)
    greet([{"tensor": peer} for peer in (near, far)])
    flights = []
    for g, part in enumerate(parts):
        flights.append((copy(part, t, far, 3 * g), copy(part, t, near, 3 * g + 1)))
        flights[g][0].start()
        flights[g][1].start()
    passes = []
    for g, part in enumerate(parts):
        flights[g][0].wait()
        passes.append(copy(part, far, near, 3 * g + 2))
        passes[g].start()
    for g in range(len(parts)):
        flights[g][1].wait()
        passes[g].wait()
    for i in range(2):
        small_o[:, 128 * i : 128 * i + PADH] = small_sc[2 * i, :, 0:PADH]
        small_o[:, 128 * i + PADH : 128 * i + 128] = small_sc[2 * i + 1, :, 0:PADH]


def gather_call(ffn_in, ffn_out, attn_in, attn_out, conv_in, conv_out, depth_kernel, bn_params):
    shards = lax.axis_size("tensor")
    wide = 4 * PADH
    return pl.pallas_call(
        gather_kernel,
        in_specs=[VMEM_SPEC] * 8,
        out_specs=[VMEM_SPEC] * 4,
        out_shape=[
            shape((shards, 2, D, D), BF16), shape((7, wide, D), BF16), shape((shards, 2, D, D), BF16),
            shape((24, wide)),
        ],
        scratch_shapes=[
            pltpu.VMEM((shards, 24, 128), F32), pltpu.SemaphoreType.DMA((12,)), pltpu.SemaphoreType.DMA((12,)),
        ],
        compiler_params=pltpu.CompilerParams(collective_id=0, has_side_effects=True, vmem_limit_bytes=VMEM_CAP),
        name="gather_part",
    )(ffn_in, ffn_out, attn_in, attn_out, conv_in, conv_out, depth_kernel, bn_params)


def share(axis, count, slots, send_sem, recv_sem):
    me = lax.axis_index(axis)

    def copy(slot, peer, sent):
        return pltpu.make_async_remote_copy(
            src_ref=slots.at[slot], dst_ref=slots.at[slot], send_sem=send_sem.at[sent], recv_sem=recv_sem.at[slot],
            device_id={axis: peer}, device_id_type=MESH,
        )

    def start(k, carry):
        peer = lax.rem(me + k, count)
        copy(me, peer, peer).start()
        return carry

    def finish(k, carry):
        peer = lax.rem(me + k, count)
        copy(me, peer, peer).wait_send()
        copy(peer, peer, peer).wait_recv()
        return carry

    lax.fori_loop(1, count, start, 0)
    lax.fori_loop(1, count, finish, 0)


def greet_axes(counts):
    barrier = pltpu.get_barrier_semaphore()
    for axis, count in counts:
        me = lax.axis_index(axis)

        def signal(k, carry, axis=axis, count=count, me=me):
            pl.semaphore_signal(
                barrier, inc=1, device_id={axis: lax.rem(me + k, count)}, device_id_type=MESH
            )
            return carry

        lax.fori_loop(1, count, signal, 0)
    pl.semaphore_wait(barrier, sum(count - 1 for axis, count in counts))


def pool(slots, count):
    total = lax.fori_loop(0, count, lambda i, a: a + slots[i, 2:3, :], jnp.zeros((1, 4 * PADH), F32))
    mean = (
        lax.fori_loop(0, count, lambda i, a: a + slots[i, 0:1, :] * slots[i, 2:3, :], jnp.zeros((1, 4 * PADH), F32))
        / total
    )

    def power(i, a):
        off = slots[i, 0:1, :] - mean
        return a + slots[i, 1:2, :] + slots[i, 2:3, :] * off * off

    return mean, lax.fori_loop(0, count, power, jnp.zeros((1, 4 * PADH), F32)), total


def moments_kernel(counts, st_ref, small_ref, bn_o, dp_sc, tensor_sc, *sems):
    held = pool(st_ref, st_ref.shape[0])
    slots_of = {"dp": dp_sc, "tensor": tensor_sc}
    greet_axes(counts)
    for i, (axis, count) in enumerate(counts):
        slots = slots_of[axis]
        me = lax.axis_index(axis)
        for row, value in enumerate(held):
            slots[me, row : row + 1, :] = value
        share(axis, count, slots, sems[2 * i], sems[2 * i + 1])
        held = pool(slots, count)
    mean, power, total = held
    bn_o[0:1, :] = mean
    bn_o[1:2, :] = lax.rsqrt(power / total + 1e-05)
    bn_o[2:4, :] = small_ref[16:18, :]
    bn_o[4:6, :] = jnp.zeros((2, 4 * PADH), F32)
    bn_o[6:7, :] = 1.0 / total
    bn_o[7:8, :] = jnp.zeros((1, 4 * PADH), F32)


def totals_kernel(counts, gb_ref, bn_ref, bn_o, dp_sc, tensor_sc, *sems):
    held = gb_ref[...]
    slots_of = {"dp": dp_sc, "tensor": tensor_sc}
    greet_axes(counts)
    for i, (axis, count) in enumerate(counts):
        slots = slots_of[axis]
        slots[lax.axis_index(axis)] = held
        share(axis, count, slots, sems[2 * i], sems[2 * i + 1])
        held = lax.fori_loop(1, count, lambda i, a: a + slots[i], slots[0])
    bn_o[0:4, :] = bn_ref[0:4, :]
    bn_o[4:6, :] = held[0:2, :]
    bn_o[6:8, :] = bn_ref[6:8, :]


def exchange_call(kernel, collective_id, name, *operands):
    counts = tuple((axis, lax.axis_size(axis)) for axis in ("dp", "tensor"))
    wide = 4 * PADH
    return pl.pallas_call(
        functools.partial(kernel, counts),
        in_specs=[VMEM_SPEC] * len(operands),
        out_specs=VMEM_SPEC,
        out_shape=shape((8, wide)),
        scratch_shapes=[pltpu.VMEM((count, 8, wide), F32) for axis, count in counts]
        + [pltpu.SemaphoreType.DMA((count,)) for axis, count in counts for side in range(2)],
        compiler_params=pltpu.CompilerParams(collective_id=collective_id, has_side_effects=True),
        name=name,
    )(*operands)


def reduce_kernel(
    dp_count, c0_ref, c1_ref, c2_ref, bn_ref, red_o, tot_o, gbn_o,
    acc, near_sc, far_sc, dp_sc, out, norm_sc, send_sem, recv_sem, nsend_sem, nrecv_sem,
):
    chunks = (c0_ref, c1_ref, c2_ref)
    t, d = lax.axis_index("tensor"), lax.axis_index("dp")
    near, far = flip(t, 0), flip(t, 1)
    bits = bits_of(dp_count)
    greet(
        [{"tensor": near}, {"tensor": far}, {"tensor": flip(near, 1)}] + [{"dp": flip(d, bit)} for bit in range(bits)]
    )
    plan = []
    length = ROWS
    for bit in range(bits):
        halved = length % 32 == 0
        plan.append((bit, length, halved))
        length = length // 2 if halved else length
    width = 3 + 2 * bits

    def copy(src, dst, chunk, slot, peer):
        return pltpu.make_async_remote_copy(
            src_ref=src, dst_ref=dst, send_sem=send_sem.at[chunk, slot], recv_sem=recv_sem.at[chunk, slot],
            device_id=peer, device_id_type=MESH,
        )

    def add(target, other):
        return (target.astype(F32) + other.astype(F32)).astype(BF16)

    def chain(c):
        source = chunks[c]
        flights = [
            copy(source.at[near], near_sc.at[c, 0], c, 0, {"tensor": near}),
            copy(source.at[flip(near, 1)], near_sc.at[c, 1], c, 1, {"tensor": near}),
        ]
        for flight in flights:
            flight.start()
        yield
        for flight in flights[::-1]:
            flight.wait()
        acc[c, 1] = add(source[far], near_sc[c, 1])
        flight = copy(acc.at[c, 1], far_sc.at[c], c, 2, {"tensor": far})
        flight.start()
        acc[c, 0] = add(source[t], near_sc[c, 0])
        yield
        flight.wait()
        acc[c, 0] = add(acc[c, 0], far_sc[c])
        offset = 0
        trail = []
        for bit, length, halved in plan:
            peer = {"dp": flip(d, bit)}
            slot = 3 + bit
            landing = dp_sc.at[c, bit, pl.ds(0, length // 2 if halved else length)]
            if halved:
                half = length // 2
                side = (d // 2 ** bit) % 2
                keep = pl.ds(pl.multiple_of(offset + side * half, 16), half)
                give = pl.ds(pl.multiple_of(offset + (1 - side) * half, 16), half)
                trail.append((bit, offset))
                offset = offset + side * half
            else:
                half = length
                keep = give = pl.ds(pl.multiple_of(offset, 16), half)
            flight = copy(acc.at[c, 0, give], landing, c, slot, peer)
            flight.start()
            yield
            flight.wait()
            acc[c, 0, keep] = add(acc[c, 0, keep], dp_sc[c, bit, 0:half])
        size = plan[-1][1] // 2 if plan and plan[-1][2] else (plan[-1][1] if plan else ROWS)
        here = pl.ds(pl.multiple_of(offset, 16), size)
        out[c, here] = acc[c, 0, here]
        for bit, before in trail[::-1]:
            here = pl.ds(pl.multiple_of(offset, 16), size)
            flight = copy(out.at[c, here], out.at[c, here], c, 3 + bits + bit, {"dp": flip(d, bit)})
            flight.start()
            yield
            flight.wait()
            offset = before
            size = size * 2

    live = [chain(c) for c in range(len(chunks))]
    for step in range(2 + 2 * bits + len(chunks)):
        for c in range(min(step + 1, len(chunks))):
            next(live[c], None)

    def square_of(a):
        a = a.astype(F32)
        return total_of(a * a)

    own_block = lax.broadcasted_iota(jnp.int32, (1, 4 * PADH), 1) // PADH == t
    gb = bn_ref[4:6, :]
    gbn_o[...] = jnp.zeros_like(gbn_o)
    for i in range(4):
        @pl.when(t == i)
        def _():
            gbn_o[0:2, 0:PADH] = gb[:, i * PADH : (i + 1) * PADH]

    square = square_of(out[0]) + square_of(out[1]) + square_of(out[2, 0 : 2 * D])
    square = square + total_of(jnp.where(own_block, gb * gb, 0.0))
    norm_sc[t] = jnp.broadcast_to(square, (8, 128))
    share("tensor", 4, norm_sc, nsend_sem, nrecv_sem)
    total = norm_sc[0] + norm_sc[1] + norm_sc[2] + norm_sc[3]
    tot_o[...] = total + jnp.broadcast_to(square_of(out[2, 2 * D : 2 * D + 16]), (8, 128))
    red_o[...] = out[...]


def reduce_call(chunks, bn):
    dp_count = lax.axis_size("dp")
    bits = bits_of(dp_count)
    width = 3 + 2 * bits
    low = lambda *dims: pltpu.VMEM(dims + (ROWS, D), BF16)
    dma = pltpu.SemaphoreType.DMA
    return pl.pallas_call(
        functools.partial(reduce_kernel, dp_count),
        in_specs=[VMEM_SPEC] * 4,
        out_specs=[VMEM_SPEC] * 3,
        out_shape=[shape((3, ROWS, D), BF16), shape((8, 128)), shape((8, 128))],
        scratch_shapes=[
            low(3, 2), low(3, 2), low(3), pltpu.VMEM((3, bits, ROWS // 2, D), BF16), low(3),
            pltpu.VMEM((4, 8, 128), F32), dma((3, width)), dma((3, width)), dma((4,)), dma((4,)),
        ],
        compiler_params=pltpu.CompilerParams(collective_id=3, has_side_effects=True, vmem_limit_bytes=VMEM_CAP),
        name="reduce_part",
    )(*chunks, bn)


def local(
    block_input, lengths, cotangent, norm_params, bn_params, ffn_in, ffn_out, attn_in, attn_out, conv_in,
    depth_kernel, conv_out, stat_wide, stat_head, stat_hidden, stat_kernel, norm_second, bn_second, step_count,
):
    attn_in, conv_in = attn_in.swapaxes(1, 2), conv_in.transpose(2, 0, 1)
    stat_head, stat_kernel = stat_head.swapaxes(1, 2), stat_kernel.swapaxes(0, 1)
    ffn_one, mix, ffn_two, small = gather_call(
        ffn_in, ffn_out, attn_in, attn_out, conv_in, conv_out, depth_kernel, bn_params
    )
    (n1, inner1, act1, x1, n2, q, k, v, probs, mixture, x2, n3, vp, gp, mid, stat) = forward_call(
        lengths, block_input, norm_params, ffn_one, mix, small
    )
    bn = exchange_call(moments_kernel, 1, "moments_part", stat, small)
    block_out, d3, dn, act3, gc, lng, gb, chunk0 = middle_call(
        lengths, mid, x2, cotangent, norm_params, bn, mix, ffn_two
    )
    bn = exchange_call(totals_kernel, 2, "totals_part", gb, bn)
    input_grad, chunk1, chunk2 = backward_call(
        lengths,
        (block_input, x1, x2, inner1, probs, q, k, v, vp, gp, mid, d3, dn),
        (norm_params, bn, small, mix, ffn_one),
        (n1, n2, n3, act1, mixture, act3, gc, lng),
    )
    reduced, total_square, gbn = reduce_call((chunk0, chunk1, chunk2), bn)
    weights = (ffn_in, ffn_out, attn_in, attn_out, conv_in, depth_kernel, conv_out)
    outs = list(
        update_call(
            step_count, total_square, reduced, gbn, weights, (stat_wide, stat_head, stat_hidden, stat_kernel),
            norm_params, norm_second, bn_params, bn_second,
        )
    )
    for i in (5, 12):
        outs[i] = outs[i].swapaxes(1, 2)
    for i in (7, 14):
        outs[i] = outs[i].transpose(1, 2, 0)
    outs[22] = outs[22].swapaxes(1, 2)
    outs[24] = outs[24].swapaxes(0, 1)
    return (block_out, input_grad, outs[0][0, :1], *outs[1:])


def solution(mesh):
    weights_specs = (
        P(None, None, "tensor"), P(None, "tensor", None), P(None, None, "tensor"), P("tensor", None),
        P(None, None, "tensor"), P(None, "tensor"), P("tensor", None),
    )
    stat_specs = (
        P("tensor", None, None, None), P("tensor", None, None, None), P("tensor", None, None, None),
        P("tensor", None, None),
    )
    frames = P(("dp", "tensor"), None)
    channels = P(None, "tensor")
    return jax.shard_map(
        local,
        mesh=mesh,
        in_specs=(frames, P("dp"), frames, P(), channels, *weights_specs, *stat_specs, P(), channels, P()),
        out_specs=(
            frames, frames, P(), P(), channels, *weights_specs, *weights_specs, P(), channels, P(), channels,
            *stat_specs,
        ),
        check_vma=False,
    )
```

```python
import functools
import itertools
import math
import types

import jax
import jax.numpy as jnp
from jax import lax
from jax.experimental import pallas as pl
from jax.experimental.pallas import tpu as pltpu
from jax.sharding import PartitionSpec as P

D = 240
KS = 15
LEN = 192
HEAD = 60
PADH = 64
ROOT_ITERS = 8
NPARAM = 1331280
PEAK_RATE = 2.0
WARM_STEPS = 4.0
SMALL_RATE = 0.3
GRAFT_SCALE = 0.6
NEG_FILL = -1000000000.0
VMEM_CAP = 60 * 1024 * 1024

F32 = jnp.float32
BF16 = jnp.bfloat16


def nn(a, b):
    return lax.dot_general(a, b, (((1,), (0,)), ((), ())), preferred_element_type=F32)


def nt(a, b):
    return lax.dot_general(a, b, (((1,), (1,)), ((), ())), preferred_element_type=F32)


def tn(a, b):
    return lax.dot_general(a, b, (((0,), (0,)), ((), ())), preferred_element_type=F32)


def sigmoid(v):
    return 0.5 * jnp.tanh(0.5 * v) + 0.5


def standardize(h):
    centred = h - jnp.sum(h, axis=-1, keepdims=True) * (1.0 / D)
    spread = jnp.sum(centred * centred, axis=-1, keepdims=True) * (1.0 / D)
    inv = lax.rsqrt(spread + 1e-05)
    return centred * inv, inv


def norm_back(h, gain, dy):
    xhat, inv = standardize(h)
    scaled = dy * gain
    mean_a = jnp.sum(scaled, axis=-1, keepdims=True) * (1.0 / D)
    mean_b = jnp.sum(scaled * xhat, axis=-1, keepdims=True) * (1.0 / D)
    dh = inv * (scaled - mean_a - xhat * mean_b)
    return dh, jnp.sum(dy * xhat, axis=0, keepdims=True), jnp.sum(dy, axis=0, keepdims=True)


def row_mask(length):
    return (lax.broadcasted_iota(jnp.int32, (LEN, 1), 0) < length).astype(F32)


def lane_masks(dtype):
    lane = lax.broadcasted_iota(jnp.int32, (1, 128), 1)
    return ((lane < PADH).astype(dtype), (lane >= PADH).astype(dtype))


def split(a):
    high = a.astype(BF16)
    return high, (a - high.astype(F32)).astype(BF16)


def stacked(lefts, right):
    full = nn(jnp.concatenate(lefts, axis=0), right)
    places, at = [], 0
    for left in lefts:
        places.append(full[at : at + left.shape[0]])
        at += left.shape[0]
    return places


def mul_fine(a, b, rider=None):
    high, cross, *rest = stacked([*a] + ([] if rider is None else [rider]), b[0])
    return (high + (nn(a[0], b[1]) + cross), *rest)


def eye_of(n):
    return (lax.broadcasted_iota(jnp.int32, (n, n), 0) == lax.broadcasted_iota(jnp.int32, (n, n), 1)).astype(F32)


def next_power(own, direction, fine):
    rider = direction.astype(BF16)
    if fine:
        parts = split(own)
        square, moved = mul_fine(parts, parts, rider)
        step = 0.0625 * square - 0.625 * own
        halves = split(step)
        once = mul_fine(halves, parts)[0]
        twice = mul_fine(halves, split(once))[0]
    else:
        low = own.astype(BF16)
        square, moved = stacked([low, rider], low)
        step = (0.0625 * square - 0.625 * own).astype(BF16)
        once = nn(step, low)
        twice = nn(step, once.astype(BF16))
    return 2.44140625 * own + 3.125 * once + twice, 1.25 * direction - 0.25 * moved


def total_of(a):
    return jnp.sum(jnp.sum(a, axis=1, keepdims=True), axis=0, keepdims=True)


def update_kernel(
    step_ref, tot_ref, red_ref, lng_ref, gbn_ref, fi_ref, fo_ref, ai_ref, ao_ref, ci_ref, dk_ref, co_ref,
    sw_ref, sh_ref, sd_ref, sk_ref, np_ref, ns_ref, bp_ref, bs_ref,
    gn_o, cn_o, cb_o, cfi_o, cfo_o, cai_o, cao_o, cci_o, cdk_o, cco_o,
    nfi_o, nfo_o, nai_o, nao_o, nci_o, ndk_o, nco_o, nn_o, nb_o, nns_o, nbs_o,
    nsw_o, nsh_o, nsd_o, nsk_o,
    mat_f, mat_b, dir_f, dir_b,
):
    steps = jnp.full((1, 1), step_ref[0], jnp.int32).astype(F32)
    rate = PEAK_RATE * jnp.minimum(steps / WARM_STEPS, jnp.sqrt(WARM_STEPS / steps))
    grad_norm = jnp.sqrt(tot_ref[0:1, 0:1])
    threshold = math.sqrt(NPARAM)
    factor = threshold / jnp.maximum(grad_norm, threshold)
    square_factor = factor * factor
    gn_o[...] = jnp.broadcast_to(grad_norm, gn_o.shape)

    c_norm = lng_ref[...] * factor
    for i in range(5):
        clipped = c_norm[2 * i : 2 * i + 2, :]
        second = 0.5 * ns_ref[i] + 0.5 * clipped * clipped
        cn_o[i] = clipped
        nns_o[i] = second
        nn_o[i] = np_ref[i] - rate * SMALL_RATE * clipped * lax.rsqrt(second)
    c_bn = gbn_ref[0:2, 0:HEAD] * factor
    second = 0.5 * bs_ref[...] + 0.5 * c_bn * c_bn
    cb_o[...] = c_bn
    nbs_o[...] = second
    nb_o[...] = bp_ref[...] - rate * SMALL_RATE * c_bn * lax.rsqrt(second)

    eye_d = eye_of(D)
    scales_f = []
    for i in range(4):
        member, is_out = i // 2, i % 2
        chunk = (2, 0)[member]
        start = is_out * (D, 256)[chunk // 2]
        low = red_ref[chunk, start : start + D, :]
        wide_c = sw_ref[0, 2 * is_out + member, 0:1, 0:1]
        hidden_c = sd_ref[0, 2 * is_out + member, 0:1, 0:1]
        gram = tn(low, low) * square_factor
        wide = nt(low, low) * square_factor
        nsw_o[0, 2 * is_out + member] = 0.5 * wide_c * eye_d + 0.5 * wide
        nsd_o[0, 2 * is_out + member] = 0.5 * hidden_c * eye_d + 0.5 * gram
        clipped = low.astype(F32) * factor
        if is_out:
            cfo_o[member] = clipped.T
        else:
            cfi_o[member] = clipped
        dir_f[i] = clipped
        trace = total_of(clipped * clipped)
        power = total_of(gram * gram)
        scale = 1.0
        for k, c in enumerate((wide_c, hidden_c)):
            zoom = 2.5 * lax.rsqrt(0.25 * c * c * D + 0.5 * c * trace + 0.25 * power)
            mat_f[2 * i + k] = zoom * (0.5 * c * eye_d + 0.5 * gram)
            scale = scale * jnp.sqrt(jnp.sqrt(zoom))
        scales_f.append(scale)

    eye_b = eye_of(4 * PADH)
    row_block = lax.broadcasted_iota(jnp.int32, (4 * PADH, 1), 0) // PADH
    lane_block = lax.broadcasted_iota(jnp.int32, (1, 4 * PADH), 1) // PADH
    same_block = row_block == lane_block
    wide_of = (4, 5, 6, 10, 8, 9, 7, None)
    head_of = (0, 1, 2, 7, 4, 5, 3, 6)
    scales_b = []

    def spread(values):
        column = jnp.zeros((4 * PADH, 1), F32)
        for i, value in enumerate(values):
            column = jnp.where(row_block == i, value, column)
        return column

    for group in range(2):
        low = red_ref[1, group * 4 * PADH : (group + 1) * 4 * PADH, :]
        clipped = low.astype(F32) * factor
        dir_b[group] = clipped.T
        gram = jnp.where(same_block, nt(low, low), 0.0) * square_factor
        row_trace = jnp.sum(clipped * clipped, axis=1, keepdims=True)
        row_power = jnp.sum(gram * gram, axis=1, keepdims=True)
        wide_cs, head_cs, traces, powers, dims = [], [], [], [], []
        for i in range(4):
            index = group * 4 + i
            part = slice(i * PADH, (i + 1) * PADH)
            piece = low[part, :]
            head_c = sh_ref[0, 0, head_of[index] : head_of[index] + 1, 0:1]
            own_gram = nt(piece, piece)[:HEAD, :HEAD] * square_factor
            nsh_o[0, :, head_of[index], :] = 0.5 * head_c * eye_d[:HEAD, :HEAD] + 0.5 * own_gram
            wide = tn(piece, piece) * square_factor
            if wide_of[index] is None:
                wide_c = sk_ref[0, 0:1, 0:1]
                nsk_o[:, 0, :] = 0.5 * wide_c * eye_d[:KS, :KS] + 0.5 * wide[:KS, :KS]
                dims.append(KS)
            else:
                wide_c = sw_ref[0, wide_of[index], 0:1, 0:1]
                nsw_o[0, wide_of[index]] = 0.5 * wide_c * eye_d + 0.5 * wide
                dims.append(D)
            wide_cs.append(wide_c)
            head_cs.append(head_c)
            traces.append(jnp.sum(row_trace[part], axis=0, keepdims=True))
            powers.append(jnp.sum(row_power[part], axis=0, keepdims=True))
        scale = [1.0] * 4
        for k, (cs, sizes) in enumerate(((wide_cs, dims), (head_cs, [HEAD] * 4))):
            zooms = [
                2.5 * lax.rsqrt(0.25 * c * c * n + 0.5 * c * trace + 0.25 * power)
                for c, n, trace, power in zip(cs, sizes, traces, powers)
            ]
            mat_b[2 * group + k] = spread(zooms) * (0.5 * spread(cs) * eye_b + 0.5 * gram)
            scale = [s * jnp.sqrt(jnp.sqrt(zoom)) for s, zoom in zip(scale, zooms)]
        scales_b.append(scale)

    def advance(fine):
        for k in range(2):
            for mats, dirs, count in ((mat_f, dir_f, 4), (mat_b, dir_b, 2)):
                for i in range(count):
                    mats[2 * i + k], dirs[i] = next_power(mats[2 * i + k], dirs[i], fine)

    def coarse_step(i, carry):
        advance(False)
        return carry

    advance(True)
    lax.fori_loop(0, ROOT_ITERS - 2, coarse_step, 0)
    for k in range(2):
        for mats, dirs, count in ((mat_f, dir_f, 4), (mat_b, dir_b, 2)):
            for i in range(count):
                moved = nn(dirs[i].astype(BF16), mats[2 * i + k].astype(BF16))
                dirs[i] = 1.25 * dirs[i] - 0.25 * moved

    def graft(weight, direction):
        size = jnp.sqrt(total_of(weight * weight))
        return rate * GRAFT_SCALE * size / (jnp.sqrt(total_of(direction * direction)) + 1e-06)

    for i in range(4):
        member, is_out = i // 2, i % 2
        direction = dir_f[i] * scales_f[i]
        weight = (fi_ref, fo_ref)[is_out][member]
        if is_out:
            direction = direction.T
        (nfi_o, nfo_o)[is_out][member] = weight - graft(weight, direction) * direction
    turned_b = [dir_b[group].T for group in range(2)]
    for index in range(8):
        group, i = index // 4, index % 4
        part = slice(i * PADH, i * PADH + HEAD)
        direction = turned_b[group][part, :] * scales_b[group][i]
        clipped = red_ref[1, index * PADH : (index + 1) * PADH, :][:HEAD, :].astype(F32) * factor
        if index in (3, 6):
            weight_ref, clip_o, new_o = ((co_ref, cco_o, nco_o), None, None, (ao_ref, cao_o, nao_o))[index - 3]
            clip_o[...] = clipped
            new_o[...] = weight_ref[...] - graft(weight_ref[...], direction) * direction
        elif index == 7:
            turned = direction.T[:KS, :]
            cdk_o[...] = clipped.T[:KS, :]
            ndk_o[...] = dk_ref[...] - graft(dk_ref[...], turned) * turned
        else:
            weight_ref, clip_o, new_o = (ai_ref, cai_o, nai_o) if index < 3 else (ci_ref, cci_o, nci_o)
            at = (index,) if index < 3 else (slice(None), index - 4)
            weight = weight_ref[at]
            clip_o[at] = clipped
            new_o[at] = weight - graft(weight, direction) * direction


def shape(dims, dtype=F32):
    return jax.ShapeDtypeStruct(dims, dtype)


def whole(dims):
    zeros = (0,) * len(dims)
    return pl.BlockSpec(dims, lambda u: zeros)


SMEM_SPEC = pl.BlockSpec(memory_space=pltpu.SMEM)
VMEM_SPEC = pl.BlockSpec(memory_space=pltpu.VMEM)
PARAMS = pltpu.CompilerParams(vmem_limit_bytes=VMEM_CAP)


def update_call(step_count, total_square, reduced, lng, gbn, weights, stats, norm_params, norm_second, bn_params, bn_second):
    stat_wide, stat_head, stat_hidden, stat_kernel = stats
    corner = lambda a: pl.BlockSpec((1, a.shape[1], 8, 128), lambda i: (0, 0, 0, 0))
    one = lambda a: whole(a.shape)
    n_stat = lambda a: whole(a.shape)
    out_arrays = [
        shape((1, 128)), norm_params, bn_params, *weights, *weights, norm_params, bn_params, norm_params, bn_params,
        stat_wide, stat_head, stat_hidden, stat_kernel,
    ]
    in_arrays = [total_square, reduced, lng, gbn, *weights]
    wide = 4 * PADH
    return pl.pallas_call(
        update_kernel,
        grid=(1,),
        in_specs=[SMEM_SPEC] + [one(a) for a in in_arrays]
        + [corner(stat_wide), one(stat_head), corner(stat_hidden), one(stat_kernel)]
        + [one(a) for a in (norm_params, norm_second, bn_params, bn_second)],
        out_specs=[one(a) for a in out_arrays],
        out_shape=[shape(a.shape) for a in out_arrays],
        scratch_shapes=[
            pltpu.VMEM((8, D, D), F32), pltpu.VMEM((4, wide, wide), F32),
            pltpu.VMEM((4, D, D), F32), pltpu.VMEM((2, D, wide), F32),
        ],
        compiler_params=PARAMS,
        name="update_part",
    )(step_count, *in_arrays, *stats, norm_params, norm_second, bn_params, bn_second)


MESH = pl.DeviceIdType.MESH


def flip(index, bit):
    step = 2 ** bit
    return index + step - 2 * step * ((index // step) % 2)


def bits_of(count):
    bits = count.bit_length() - 1
    if 2 ** bits != count:
        raise ValueError("axis size")
    return bits


def greet_axes(counts):
    barrier = pltpu.get_barrier_semaphore()
    for axis, count in counts:
        me = lax.axis_index(axis)

        def signal(k, carry, axis=axis, count=count, me=me):
            pl.semaphore_signal(
                barrier, inc=1, device_id={axis: lax.rem(me + k, count)}, device_id_type=MESH
            )
            return carry

        lax.fori_loop(1, count, signal, 0)


def greeted(counts):
    pl.semaphore_wait(pltpu.get_barrier_semaphore(), sum(count - 1 for axis, count in counts))


def share_copy(axis, slots, sems, slot, peer, sent):
    return pltpu.make_async_remote_copy(
        src_ref=slots.at[slot], dst_ref=slots.at[slot], send_sem=sems[0].at[sent], recv_sem=sems[1].at[slot],
        device_id={axis: peer}, device_id_type=MESH,
    )


def share_start(axis, count, slots, sems):
    me = lax.axis_index(axis)

    def start(k, carry):
        peer = lax.rem(me + k, count)
        share_copy(axis, slots, sems, me, peer, peer).start()
        return carry

    lax.fori_loop(1, count, start, 0)


def share_finish(axis, count, slots, sems):
    me = lax.axis_index(axis)

    def finish(k, carry):
        peer = lax.rem(me + k, count)
        share_copy(axis, slots, sems, me, peer, peer).wait_send()
        share_copy(axis, slots, sems, peer, peer, peer).wait_recv()
        return carry

    lax.fori_loop(1, count, finish, 0)


def pool(slots, count):
    blank = jnp.zeros((1, 4 * PADH), F32)
    total = lax.fori_loop(0, count, lambda i, a: a + slots[i, 2:3, :], blank)
    mean = lax.fori_loop(0, count, lambda i, a: a + slots[i, 0:1, :] * slots[i, 2:3, :], blank) / total

    def power(i, a):
        off = slots[i, 0:1, :] - mean
        return a + slots[i, 1:2, :] + slots[i, 2:3, :] * off * off

    return mean, lax.fori_loop(0, count, power, blank), total


CHAINS = ((0, 0, 512), (1, 256, 256), (1, 0, 256), (2, 256, 256), (2, 0, 256))


def plan_of(dp_count, length):
    bits = bits_of(dp_count)
    radices = [2] * (bits % 2) + [4] * (bits // 2)
    plan, stride = [], 1
    for radix in radices:
        cut = length % (16 * radix) == 0
        length = length // radix if cut else length
        plan.append((stride, radix, cut, length))
        stride *= radix
    return plan


def landing_rows(dp_count):
    return sum(radix * piece for _, _, n in CHAINS for _, radix, _, piece in plan_of(dp_count, n))


def copy_count(dp_count):
    return sum(
        3 + sum((radix - 1) * (1 + cut) for _, radix, cut, _ in plan_of(dp_count, n)) for _, _, n in CHAINS
    )


def swish_slope(inner):
    sigma = sigmoid(inner)
    return sigma * (1.0 + inner * (1.0 - sigma))


HALVES = tuple(slice(i * 128, i * 128 + 128) for i in range(2))


def step_kernel(
    counts, names, lens_ref, x_ref, cot_ref, np_ref, fi_ref, fo_ref, ai_ref, ao_ref, ci_ref, co_ref, dk_ref, bp_ref,
    out_o, ig_o, red_o, lng_o, tot_o, gbn_o, *scratch,
):
    s = types.SimpleNamespace(**dict(zip(names, scratch)))
    dp_count = dict(counts)["dp"]
    shards = s.ffn1.shape[0]
    frames = x_ref.shape[0]
    utts = frames // LEN
    t, d = lax.axis_index("tensor"), lax.axis_index("dp")
    near, far = flip(t, 0), flip(t, 1)
    last = flip(near, 1)
    wide = 4 * PADH

    def rows_of(u, size=LEN):
        return pl.ds(pl.multiple_of(u * size, size), size)

    def length_of(u):
        return lens_ref[t * utts + u]

    def each(body, start=0, stop=utts):
        def turn(u, carry):
            body(u)
            return carry

        lax.fori_loop(start, stop, turn, 0)

    greet_axes(counts)

    own = pl.ds(pl.multiple_of(t * PADH, PADH), PADH)
    parts = (
        lambda i: s.small_parts.at[i],
        lambda i: s.ffn1.at[i],
        lambda i: s.mix.at[:, pl.ds(pl.multiple_of(i * PADH, PADH), PADH), :],
        lambda i: s.ffn2.at[i],
    )

    def weight_copy(g, shard, peer, slot):
        return pltpu.make_async_remote_copy(
            src_ref=parts[g](shard), dst_ref=parts[g](shard), send_sem=s.gather_send.at[3 * g + slot],
            recv_sem=s.gather_recv.at[3 * g + slot], device_id={"tensor": peer}, device_id_type=MESH,
        )

    def launch(g):
        weight_copy(g, t, far, 0).start()
        weight_copy(g, t, near, 1).start()

    def relay(g):
        weight_copy(g, t, far, 0).wait()
        weight_copy(g, far, near, 2).start()

    def near_here(g):
        weight_copy(g, t, near, 1).wait()

    def last_here(g):
        weight_copy(g, far, near, 2).wait()

    s.small_parts[t] = jnp.zeros((24, 128), F32)
    s.small_parts[t, 0:KS, 0:HEAD] = dk_ref[...]
    s.small_parts[t, 16:18, 0:HEAD] = bp_ref[...]
    s.ffn1[t, 0] = fi_ref[0].astype(BF16)
    s.ffn1[t, 1] = fo_ref[0].astype(BF16)
    greeted(counts)
    launch(1)
    blank = jnp.zeros((PADH - HEAD, D), F32)
    pieces = [ai_ref[m] for m in range(3)] + [ao_ref[...]] + [ci_ref[:, m, :] for m in range(2)] + [co_ref[...]]
    for i, piece in enumerate(pieces):
        s.mix[i, own, :] = jnp.concatenate([piece, blank], axis=0).astype(BF16)
    launch(2)
    launch(0)
    s.ffn2[t, 0] = fi_ref[1].astype(BF16)
    s.ffn2[t, 1] = fo_ref[1].astype(BF16)
    launch(3)
    for ref in (s.pad_f, s.pad_m, s.depth_grad, s.norm_grad, s.bn_grad):
        ref[...] = jnp.zeros_like(ref)

    def norm_one(u):
        rows = rows_of(u)
        x0 = x_ref[rows, :].astype(F32)
        s.x1[rows, :] = x0
        s.n1[rows, :] = (standardize(x0)[0] * np_ref[0, 0:1, :] + np_ref[0, 1:2, :]).astype(BF16)

    each(norm_one)

    def feed_forward(shard):
        def body(u):
            rows = rows_of(u, 2 * LEN)
            inner = nn(s.n1[rows, :], s.ffn1[shard, 0])
            s.inner1[shard, rows, :] = inner
            active = (inner * sigmoid(inner)).astype(BF16)
            s.act1[shard, rows, :] = active
            s.x1[rows, :] += 0.5 * nn(active, s.ffn1[shard, 1])

        each(body, 0, utts // 2)

    feed_forward(t)
    near_here(1)
    feed_forward(near)
    relay(1)
    feed_forward(far)
    last_here(1)
    feed_forward(last)
    relay(2)
    relay(0)
    near_here(2)
    near_here(0)
    last_here(2)
    last_here(0)
    for i in range(2):
        s.small[:, 128 * i : 128 * i + PADH] = s.small_parts[2 * i, :, 0:PADH]
        s.small[:, 128 * i + PADH : 128 * i + 128] = s.small_parts[2 * i + 1, :, 0:PADH]

    masks = lane_masks(BF16)

    def mix_forward(u):
        rows = rows_of(u)
        length = length_of(u)
        x1 = s.x1[rows, :]
        n2 = (standardize(x1)[0] * np_ref[1, 0:1, :] + np_ref[1, 1:2, :]).astype(BF16)
        s.n2[rows, :] = n2
        for i, ref in enumerate((s.q, s.k, s.v)):
            ref[rows, :] = nt(n2, s.mix[i]).astype(BF16)
        key_ok = lax.broadcasted_iota(jnp.int32, (1, LEN), 1) < length
        for half, lanes in enumerate(HALVES):
            q, k, v = s.q[rows, lanes], s.k[rows, lanes], s.v[rows, lanes]
            mixture = jnp.zeros((LEN, 128), F32)
            for side in range(2):
                scores = nt(q * masks[side], k) * HEAD ** (-0.5)
                scores = jnp.where(key_ok, scores, NEG_FILL)
                exps = jnp.exp(scores - jnp.max(scores, axis=-1, keepdims=True))
                probs = exps * (1.0 / jnp.sum(exps, axis=-1, keepdims=True))
                s.probs[u, 2 * half + side] = probs
                mixture = mixture + nn(probs.astype(BF16), v * masks[side])
            s.mixture[rows, lanes] = mixture.astype(BF16)
        x2 = x1 + nn(s.mixture[rows, :], s.mix[3])
        s.x2[rows, :] = x2
        n3 = (standardize(x2)[0] * np_ref[2, 0:1, :] + np_ref[2, 1:2, :]).astype(BF16)
        s.n3[rows, :] = n3
        value = nt(n3, s.mix[4])
        gate = nt(n3, s.mix[5])
        s.value[rows, :] = value
        s.gate[rows, :] = gate
        mask = row_mask(length)
        gated = value * sigmoid(gate) * mask
        count = length.astype(F32)
        for half, lanes in enumerate(HALVES):
            s.pad_f[half, 8 : 8 + LEN, :] = gated[:, lanes]
            running = jnp.zeros((LEN, 128), F32)
            for j in range(KS):
                running = running + s.pad_f[half, 1 + j : 1 + j + LEN, :] * s.small[j : j + 1, lanes]
            s.mid[rows, lanes] = running
            mean = jnp.sum(running * mask, axis=0, keepdims=True) / count
            centred = (running - mean) * mask
            s.stat[u, 0:1, lanes] = mean
            s.stat[u, 1:2, lanes] = jnp.sum(centred * centred, axis=0, keepdims=True)
            s.stat[u, 2:3, lanes] = jnp.full((1, 128), count, F32)

    each(mix_forward)

    held = pool(s.stat, utts)
    for axis, count in counts:
        slots = getattr(s, "moment_" + axis)
        sems = [getattr(s, "moment_" + axis + side) for side in ("_send", "_recv")]
        me = lax.axis_index(axis)
        slots[me] = jnp.concatenate([*held, jnp.zeros((5, wide), F32)], axis=0)
        share_start(axis, count, slots, sems)
        if axis == "dp":
            relay(3)
            near_here(3)
        share_finish(axis, count, slots, sems)
        held = pool(slots, count)
    last_here(3)
    mean, power, total = held
    inv_std = lax.rsqrt(power / total + 1e-05)
    inv_count = 1.0 / total
    s.bn[0:1, :] = mean
    s.bn[1:2, :] = inv_std
    s.bn[2:4, :] = s.small[16:18, :]
    s.bn[6:7, :] = inv_count

    def middle(u):
        rows = rows_of(u)
        mask = row_mask(length_of(u))
        mean, inv_std, gain, bias = [s.bn[i : i + 1, :] for i in range(4)]
        xhat = (s.mid[rows, :] - mean) * inv_std
        normal = xhat * gain + bias
        sigma = sigmoid(normal)
        act3 = (normal * sigma * mask).astype(BF16)
        s.act3[rows, :] = act3
        x3 = s.x2[rows, :] + nn(act3, s.mix[6])
        n4 = (standardize(x3)[0] * np_ref[3, 0:1, :] + np_ref[3, 1:2, :]).astype(BF16)
        s.n4[rows, :] = n4
        total = jnp.zeros((LEN, D), F32)
        for i in range(shards):
            inner = nn(n4, s.ffn2[i, 0])
            s.inner2[i] = inner
            active = (inner * sigmoid(inner)).astype(BF16)
            s.act2[i, rows, :] = active
            total = total + nn(active, s.ffn2[i, 1])
        x4 = x3 + 0.5 * total
        out_o[rows, :] = (standardize(x4)[0] * np_ref[4, 0:1, :] + np_ref[4, 1:2, :]).astype(BF16)
        d4, gain4, bias4 = norm_back(x4, np_ref[4, 0:1, :], cot_ref[rows, :].astype(F32))
        g2 = (0.5 * d4).astype(BF16)
        s.g2[rows, :] = g2
        d_n4 = jnp.zeros((LEN, D), F32)
        for i in range(shards):
            d_inner = (nt(g2, s.ffn2[i, 1]) * swish_slope(s.inner2[i])).astype(BF16)
            s.din[i, rows, :] = d_inner
            d_n4 = d_n4 + nt(d_inner, s.ffn2[i, 0])
        d3, gain3, bias3 = norm_back(x3, np_ref[3, 0:1, :], d_n4)
        d3 = d3 + d4
        s.d3[rows, :] = d3
        gc = d3.astype(BF16)
        s.gc[rows, :] = gc
        d_normal = nt(gc, s.mix[6]) * mask * (sigma * (1.0 + normal * (1.0 - sigma)))
        s.d_normal[rows, :] = d_normal
        for i, part in enumerate((gain3, bias3, gain4, bias4)):
            s.norm_grad[6 + i : 7 + i, :] += part
        s.bn_grad[0:1, :] += jnp.sum(d_normal * xhat, axis=0, keepdims=True)
        s.bn_grad[1:2, :] += jnp.sum(d_normal, axis=0, keepdims=True)

    each(middle)

    sem_ids = itertools.count()

    def move(src, dst, peer):
        i = next(sem_ids)
        return pltpu.make_async_remote_copy(
            src_ref=src, dst_ref=dst, send_sem=s.reduce_send.at[i], recv_sem=s.reduce_recv.at[i],
            device_id=peer, device_id_type=MESH,
        )

    def add(target, other):
        return (target.astype(F32) + other.astype(F32)).astype(BF16)

    landing = [0]

    def chain(c, first, length):
        window = pl.ds(first, length)
        flights = [
            move(s.chunk.at[c, last, window], s.near.at[c, 1, window], {"tensor": near}),
            move(s.chunk.at[c, near, window], s.near.at[c, 0, window], {"tensor": near}),
        ]
        for flight in flights:
            flight.start()
        yield
        flights[0].wait()
        s.acc[c, 1, window] = add(s.chunk[c, far, window], s.near[c, 1, window])
        flight = move(s.acc.at[c, 1, window], s.far.at[c, window], {"tensor": far})
        flight.start()
        flights[1].wait()
        s.acc[c, 0, window] = add(s.chunk[c, t, window], s.near[c, 0, window])
        yield
        flight.wait()
        s.acc[c, 0, window] = add(s.acc[c, 0, window], s.far[c, window])
        offset, size, trail = first, length, []
        for stride, radix, cut, piece in plan_of(dp_count, length):
            digit = (d // stride) % radix
            base = landing[0]
            landing[0] += radix * piece

            def slot(i):
                return pl.ds(pl.multiple_of(base + i * piece, 16), piece)

            def part(i):
                return pl.ds(pl.multiple_of(offset + i * piece if cut else offset, 16), piece)

            flights = []
            for k in range(1, radix):
                other = (digit + k) % radix
                peer = {"dp": d + (other - digit) * stride}
                flights.append(move(s.acc.at[c, 0, part(other)], s.land.at[slot(digit)], peer))
                flights[-1].start()
            s.land[slot(digit)] = s.acc[c, 0, part(digit)]
            yield
            for flight in flights:
                flight.wait()
            total = s.land[slot(0)].astype(F32)
            for i in range(1, radix):
                total = total + s.land[slot(i)].astype(F32)
            s.acc[c, 0, part(digit)] = total.astype(BF16)
            if cut:
                trail.append((stride, radix, offset))
                offset, size = offset + digit * piece, piece
        here = pl.ds(pl.multiple_of(offset, 16), size)
        red_o[c, here] = s.acc[c, 0, here]
        for stride, radix, before in trail[::-1]:
            digit = (d // stride) % radix
            here = pl.ds(pl.multiple_of(offset, 16), size)
            flights = []
            for k in range(1, radix):
                peer = {"dp": d + ((digit + k) % radix - digit) * stride}
                flights.append(move(red_o.at[c, here], red_o.at[c, here], peer))
                flights[-1].start()
            yield
            for flight in flights:
                flight.wait()
            offset, size = before, size * radix

    live = []

    def begin(i):
        live.append(chain(*CHAINS[i]))
        next(live[-1])

    def pump():
        for item in list(live):
            if next(item, item) is item:
                live.remove(item)

    def spread_rows(c, first, left, right):
        full = tn(left, right).astype(BF16)
        for i in range(shards):
            s.chunk[c, i, first : first + PADH, :] = full[PADH * i : PADH * (i + 1), :]

    totals = ("total_dp", "total_tensor")
    count_of = dict(counts)

    def sems_of(name):
        return [getattr(s, name + side) for side in ("_send", "_recv")]

    s.total_dp[d] = s.bn_grad[...]
    share_start("dp", dp_count, s.total_dp, sems_of("total_dp"))
    for i in range(shards):
        s.chunk[0, i, 0:D, :] = tn(s.n4[...], s.din[i]).astype(BF16)
        s.chunk[0, i, D : 2 * D, :] = tn(s.g2[...], s.act2[i]).astype(BF16)
        s.chunk[0, i, 2 * D :, :] = jnp.zeros((512 - 2 * D, D), BF16)
    begin(0)
    share_finish("dp", dp_count, s.total_dp, sems_of("total_dp"))
    s.total_tensor[t] = lax.fori_loop(1, dp_count, lambda i, a: a + s.total_dp[i], s.total_dp[0])
    share_start("tensor", shards, s.total_tensor, sems_of("total_tensor"))
    spread_rows(1, 3 * PADH, s.act3[...], s.gc[...])
    share_finish("tensor", shards, s.total_tensor, sems_of("total_tensor"))
    bn_sums = lax.fori_loop(1, shards, lambda i, a: a + s.total_tensor[i], s.total_tensor[0])
    s.bn[4:6, :] = bn_sums[0:2, :]

    def conv_back(u):
        rows = rows_of(u)
        mask = row_mask(length_of(u))
        mean, inv_std, gain, bias, sum_gain, sum_bias, inv_count = [s.bn[i : i + 1, :] for i in range(7)]
        xhat = (s.mid[rows, :] - mean) * inv_std
        d_mid = inv_std * gain * (s.d_normal[rows, :] - mask * ((sum_bias + xhat * sum_gain) * inv_count))
        value = s.value[rows, :]
        sigma = sigmoid(s.gate[rows, :])
        gated = value * sigma * mask
        for half, lanes in enumerate(HALVES):
            s.pad_f[half, 8 : 8 + LEN, :] = gated[:, lanes]
            s.pad_m[half, 8 : 8 + LEN, :] = d_mid[:, lanes]
            d_gated = jnp.zeros((LEN, 128), F32)
            mid_half = d_mid[:, lanes]
            for j in range(KS):
                d_gated = d_gated + s.pad_m[half, 15 - j : 15 - j + LEN, :] * s.small[j : j + 1, lanes]
                s.depth_grad[j : j + 1, lanes] += jnp.sum(
                    s.pad_f[half, 1 + j : 1 + j + LEN, :] * mid_half, axis=0, keepdims=True
                )
            d_gated = d_gated * mask
            sig = sigma[:, lanes]
            s.d_value[rows, lanes] = (d_gated * sig).astype(BF16)
            s.d_gate[rows, lanes] = (d_gated * value[:, lanes] * sig * (1.0 - sig)).astype(BF16)
        d_n3 = nn(s.d_value[rows, :], s.mix[4]) + nn(s.d_gate[rows, :], s.mix[5])
        d2, gain2, bias2 = norm_back(s.x2[rows, :], np_ref[2, 0:1, :], d_n3)
        d2 = d2 + s.d3[rows, :]
        s.d2[rows, :] = d2
        s.ga[rows, :] = d2.astype(BF16)
        for i, part in enumerate((gain2, bias2)):
            s.norm_grad[4 + i : 5 + i, :] += part

    each(conv_back, 0, utts // 2)
    pump()
    each(conv_back, utts // 2, utts)
    pump()
    eye = (
        lax.broadcasted_iota(jnp.int32, (16, D), 0) == lax.broadcasted_iota(jnp.int32, (16, D), 1)
    ).astype(BF16)
    spread_rows(1, 4 * PADH, s.d_value[...], s.n3[...])
    spread_rows(1, 5 * PADH, s.d_gate[...], s.n3[...])
    spread_rows(1, 6 * PADH, s.mixture[...], s.ga[...])
    spread_rows(1, 7 * PADH, s.depth_grad[...].astype(BF16), eye)
    begin(1)

    def attend_back(u):
        rows = rows_of(u)
        d_mix = nt(s.ga[rows, :], s.mix[3]).astype(BF16)
        for half, lanes in enumerate(HALVES):
            q, k, v, dm = s.q[rows, lanes], s.k[rows, lanes], s.v[rows, lanes], d_mix[:, lanes]
            dq = jnp.zeros((LEN, 128), F32)
            dk = jnp.zeros((LEN, 128), F32)
            dv = jnp.zeros((LEN, 128), F32)
            for side in range(2):
                probs = s.probs[u, 2 * half + side]
                dm_side = dm * masks[side]
                d_probs = nt(dm_side, v)
                dv = dv + tn(probs.astype(BF16), dm_side)
                row_sum = jnp.sum(probs * d_probs, axis=-1, keepdims=True)
                d_scores = (probs * (d_probs - row_sum)).astype(BF16)
                dq = dq + nn(d_scores, k * masks[side])
                dk = dk + tn(d_scores, q * masks[side])
            s.dq[rows, lanes] = (dq * HEAD ** (-0.5)).astype(BF16)
            s.dk[rows, lanes] = (dk * HEAD ** (-0.5)).astype(BF16)
            s.dv[rows, lanes] = dv.astype(BF16)
        d_n2 = nn(s.dq[rows, :], s.mix[0]) + nn(s.dk[rows, :], s.mix[1]) + nn(s.dv[rows, :], s.mix[2])
        d1, gain1, bias1 = norm_back(s.x1[rows, :], np_ref[1, 0:1, :], d_n2)
        d1 = d1 + s.d2[rows, :]
        s.d1[rows, :] = d1
        s.g1[rows, :] = (0.5 * d1).astype(BF16)
        s.d_n1[rows, :] = jnp.zeros((LEN, D), F32)
        for i, part in enumerate((gain1, bias1)):
            s.norm_grad[2 + i : 3 + i, :] += part

    each(attend_back, 0, utts // 2)
    pump()
    each(attend_back, utts // 2, utts)
    pump()
    spread_rows(1, 0, s.dq[...], s.n2[...])
    spread_rows(1, PADH, s.dk[...], s.n2[...])
    spread_rows(1, 2 * PADH, s.dv[...], s.n2[...])
    begin(2)
    for i in range(shards):
        s.chunk[2, i, 256 : 256 + D, :] = tn(s.g1[...], s.act1[i]).astype(BF16)
        s.chunk[2, i, 256 + D :, :] = jnp.zeros((256 - D, D), BF16)
        s.chunk[2, i, D:256, :] = jnp.zeros((256 - D, D), BF16)
    begin(3)

    for place, shard in enumerate((last, near, far, t)):
        def feed_back(u):
            rows = rows_of(u, 2 * LEN)
            d_inner = (nt(s.g1[rows, :], s.ffn1[shard, 1]) * swish_slope(s.inner1[shard, rows, :])).astype(BF16)
            s.din1[place, rows, :] = d_inner
            s.d_n1[rows, :] += nt(d_inner, s.ffn1[shard, 0])

        each(feed_back, 0, utts // 2)
        s.chunk[2, shard, 0:D, :] = tn(s.n1[...], s.din1[place]).astype(BF16)
        if place == 1:
            begin(4)
        elif place != 2:
            pump()

    def norm_zero(u):
        rows = rows_of(u)
        d0, gain0, bias0 = norm_back(x_ref[rows, :].astype(F32), np_ref[0, 0:1, :], s.d_n1[rows, :])
        ig_o[rows, :] = d0 + s.d1[rows, :]
        for i, part in enumerate((gain0, bias0)):
            s.norm_grad[i : i + 1, :] += part

    each(norm_zero)
    s.norm_dp[d] = s.norm_grad[...]
    share_start("dp", dp_count, s.norm_dp, sems_of("norm_dp"))
    pump()
    pump()
    share_finish("dp", dp_count, s.norm_dp, sems_of("norm_dp"))
    s.norm_tensor[t] = lax.fori_loop(1, dp_count, lambda i, a: a + s.norm_dp[i], s.norm_dp[0])
    share_start("tensor", shards, s.norm_tensor, sems_of("norm_tensor"))
    pump()
    share_finish("tensor", shards, s.norm_tensor, sems_of("norm_tensor"))
    norm_sums = lax.fori_loop(1, shards, lambda i, a: a + s.norm_tensor[i], s.norm_tensor[0])
    lng_o[...] = norm_sums
    while live:
        pump()

    def square_of(a):
        a = a.astype(F32)
        return total_of(a * a)

    own_block = lax.broadcasted_iota(jnp.int32, (1, wide), 1) // PADH == t
    gb = s.bn[4:6, :]
    gbn_o[...] = jnp.zeros_like(gbn_o)
    for i in range(4):
        @pl.when(t == i)
        def _():
            gbn_o[0:2, 0:PADH] = gb[:, i * PADH : (i + 1) * PADH]

    square = square_of(red_o[0]) + square_of(red_o[1]) + square_of(red_o[2])
    square = square + total_of(jnp.where(own_block, gb * gb, 0.0))
    s.square[t] = jnp.broadcast_to(square, (8, 128))
    share_start("tensor", shards, s.square, sems_of("square"))
    share_finish("tensor", shards, s.square, sems_of("square"))
    total = s.square[0] + s.square[1] + s.square[2] + s.square[3]
    tot_o[...] = total + jnp.broadcast_to(square_of(norm_sums), (8, 128))


def step_call(lengths, x, cot, norm_params, ffn_in, ffn_out, attn_in, attn_out, conv_in, conv_out, depth_kernel, bn_params):
    counts = tuple((axis, lax.axis_size(axis)) for axis in ("dp", "tensor"))
    dp_count, shards = counts[0][1], counts[1][1]
    frames = x.shape[0]
    utts = frames // LEN
    wide = 4 * PADH
    low = lambda *dims: pltpu.VMEM(dims, BF16)
    full = lambda *dims: pltpu.VMEM(dims, F32)
    copies = copy_count(dp_count)
    scratch = {
        "ffn1": low(shards, 2, D, D), "ffn2": low(shards, 2, D, D), "mix": low(7, wide, D),
        "small_parts": full(shards, 24, 128), "small": full(24, wide),
        "x1": full(frames, D), "x2": full(frames, D), "d1": full(frames, D), "d2": full(frames, D),
        "d3": full(frames, D), "d_n1": full(frames, D),
        "n1": low(frames, D), "n2": low(frames, D), "n3": low(frames, D), "n4": low(frames, D),
        "inner1": full(shards, frames, D), "act1": low(shards, frames, D), "din1": low(shards, frames, D),
        "inner2": full(shards, LEN, D), "act2": low(shards, frames, D), "din": low(shards, frames, D),
        "q": low(frames, wide), "k": low(frames, wide), "v": low(frames, wide), "mixture": low(frames, wide),
        "dq": low(frames, wide), "dk": low(frames, wide), "dv": low(frames, wide),
        "d_value": low(frames, wide), "d_gate": low(frames, wide), "act3": low(frames, wide),
        "probs": full(utts, 4, LEN, LEN), "value": full(frames, wide), "gate": full(frames, wide),
        "mid": full(frames, wide), "d_normal": full(frames, wide),
        "g1": low(frames, D), "g2": low(frames, D), "ga": low(frames, D), "gc": low(frames, D),
        "pad_f": full(2, LEN + 16, 128), "pad_m": full(2, LEN + 16, 128), "stat": full(utts, 8, wide),
        "bn": full(8, wide), "depth_grad": full(16, wide), "norm_grad": full(16, D), "bn_grad": full(8, wide),
        "chunk": low(3, shards, 512, D), "near": low(3, 2, 512, D), "acc": low(3, 2, 512, D), "far": low(3, 512, D),
        "land": low(landing_rows(dp_count), D),
        "square": full(shards, 8, 128),
        "gather_send": pltpu.SemaphoreType.DMA((12,)), "gather_recv": pltpu.SemaphoreType.DMA((12,)),
        "reduce_send": pltpu.SemaphoreType.DMA((copies,)), "reduce_recv": pltpu.SemaphoreType.DMA((copies,)),
    }
    for name, rows, width in (("moment", 8, wide), ("total", 8, wide), ("norm", 16, D)):
        for axis, count in counts:
            scratch[name + "_" + axis] = full(count, rows, width)
    for name, count in [(a + "_" + axis, count) for a in ("moment", "total", "norm") for axis, count in counts] + [
        ("square", shards)
    ]:
        for side in ("_send", "_recv"):
            scratch[name + side] = pltpu.SemaphoreType.DMA((count,))
    return pl.pallas_call(
        functools.partial(step_kernel, counts, tuple(scratch)),
        in_specs=[SMEM_SPEC] + [VMEM_SPEC] * 11,
        out_specs=[VMEM_SPEC] * 6,
        out_shape=[
            shape((frames, D), BF16), shape((frames, D)), shape((3, 512, D), BF16), shape((16, D)), shape((8, 128)),
            shape((8, 128)),
        ],
        scratch_shapes=list(scratch.values()),
        compiler_params=pltpu.CompilerParams(collective_id=0, has_side_effects=True, vmem_limit_bytes=VMEM_CAP),
        name="step_part",
    )(lengths, x, cot, norm_params, ffn_in, ffn_out, attn_in, attn_out, conv_in, conv_out, depth_kernel, bn_params)


def local(
    block_input, lengths, cotangent, norm_params, bn_params, ffn_in, ffn_out, attn_in, attn_out, conv_in,
    depth_kernel, conv_out, stat_wide, stat_head, stat_hidden, stat_kernel, norm_second, bn_second, step_count,
):
    attn_in, conv_in = attn_in.swapaxes(1, 2), conv_in.transpose(2, 0, 1)
    stat_head, stat_kernel = stat_head.swapaxes(1, 2), stat_kernel.swapaxes(0, 1)
    block_out, input_grad, reduced, lng, total_square, gbn = step_call(
        lengths, block_input, cotangent, norm_params, ffn_in, ffn_out, attn_in, attn_out, conv_in, conv_out,
        depth_kernel, bn_params,
    )
    weights = (ffn_in, ffn_out, attn_in, attn_out, conv_in, depth_kernel, conv_out)
    outs = list(
        update_call(
            step_count, total_square, reduced, lng, gbn, weights, (stat_wide, stat_head, stat_hidden, stat_kernel),
            norm_params, norm_second, bn_params, bn_second,
        )
    )
    for i in (5, 12):
        outs[i] = outs[i].swapaxes(1, 2)
    for i in (7, 14):
        outs[i] = outs[i].transpose(1, 2, 0)
    outs[22] = outs[22].swapaxes(1, 2)
    outs[24] = outs[24].swapaxes(0, 1)
    return (block_out, input_grad, outs[0][0, :1], *outs[1:])


def solution(mesh):
    weights_specs = (
        P(None, None, "tensor"), P(None, "tensor", None), P(None, None, "tensor"), P("tensor", None),
        P(None, None, "tensor"), P(None, "tensor"), P("tensor", None),
    )
    stat_specs = (
        P("tensor", None, None, None), P("tensor", None, None, None), P("tensor", None, None, None),
        P("tensor", None, None),
    )
    frames = P(("dp", "tensor"), None)
    channels = P(None, "tensor")
    return jax.shard_map(
        local,
        mesh=mesh,
        in_specs=(frames, P("dp"), frames, P(), channels, *weights_specs, *stat_specs, P(), channels, P()),
        out_specs=(
            frames, frames, P(), P(), channels, *weights_specs, *weights_specs, P(), channels, P(), channels,
            *stat_specs,
        ),
        check_vma=False,
    )
```

```python
import functools
import itertools
import math
import types

import jax
import jax.numpy as jnp
from jax import lax
from jax.experimental import pallas as pl
from jax.experimental.pallas import tpu as pltpu
from jax.sharding import PartitionSpec as P

D = 240
KS = 15
LEN = 192
HEAD = 60
PADH = 64
ROOT_ITERS = 8
NPARAM = 1331280
PEAK_RATE = 2.0
WARM_STEPS = 4.0
SMALL_RATE = 0.3
GRAFT_SCALE = 0.6
NEG_FILL = -1000000000.0
VMEM_CAP = 60 * 1024 * 1024

F32 = jnp.float32
BF16 = jnp.bfloat16


def nn(a, b):
    return lax.dot_general(a, b, (((1,), (0,)), ((), ())), preferred_element_type=F32)


def nt(a, b):
    return lax.dot_general(a, b, (((1,), (1,)), ((), ())), preferred_element_type=F32)


def tn(a, b):
    return lax.dot_general(a, b, (((0,), (0,)), ((), ())), preferred_element_type=F32)


def sigmoid(v):
    return 0.5 * jnp.tanh(0.5 * v) + 0.5


def standardize(h):
    centred = h - jnp.sum(h, axis=-1, keepdims=True) * (1.0 / D)
    spread = jnp.sum(centred * centred, axis=-1, keepdims=True) * (1.0 / D)
    inv = lax.rsqrt(spread + 1e-05)
    return centred * inv, inv


def norm_back(h, gain, dy):
    xhat, inv = standardize(h)
    scaled = dy * gain
    mean_a = jnp.sum(scaled, axis=-1, keepdims=True) * (1.0 / D)
    mean_b = jnp.sum(scaled * xhat, axis=-1, keepdims=True) * (1.0 / D)
    dh = inv * (scaled - mean_a - xhat * mean_b)
    return dh, jnp.sum(dy * xhat, axis=0, keepdims=True), jnp.sum(dy, axis=0, keepdims=True)


def row_mask(length):
    return (lax.broadcasted_iota(jnp.int32, (LEN, 1), 0) < length).astype(F32)


def lane_masks(dtype):
    lane = lax.broadcasted_iota(jnp.int32, (1, 128), 1)
    return ((lane < PADH).astype(dtype), (lane >= PADH).astype(dtype))


def split(a):
    high = a.astype(BF16)
    return high, (a - high.astype(F32)).astype(BF16)


def stacked(lefts, right):
    full = nn(jnp.concatenate(lefts, axis=0), right)
    places, at = [], 0
    for left in lefts:
        places.append(full[at : at + left.shape[0]])
        at += left.shape[0]
    return places


def mul_fine(a, b, rider=None):
    high, cross, *rest = stacked([*a] + ([] if rider is None else [rider]), b[0])
    return (high + (nn(a[0], b[1]) + cross), *rest)


def eye_of(n):
    return (lax.broadcasted_iota(jnp.int32, (n, n), 0) == lax.broadcasted_iota(jnp.int32, (n, n), 1)).astype(F32)


def next_power(own, direction, fine):
    rider = direction.astype(BF16)
    if fine:
        parts = split(own)
        square, moved = mul_fine(parts, parts, rider)
        step = 0.0625 * square - 0.625 * own
        halves = split(step)
        once = mul_fine(halves, parts)[0]
        twice = mul_fine(halves, split(once))[0]
    else:
        low = own.astype(BF16)
        square, moved = stacked([low, rider], low)
        step = (0.0625 * square - 0.625 * own).astype(BF16)
        once = nn(step, low)
        twice = nn(step, once.astype(BF16))
    return 2.44140625 * own + 3.125 * once + twice, 1.25 * direction - 0.25 * moved


def total_of(a):
    return jnp.sum(jnp.sum(a, axis=1, keepdims=True), axis=0, keepdims=True)


def update_kernel(
    step_ref, tot_ref, red_ref, lng_ref, gbn_ref, fi_ref, fo_ref, ai_ref, ao_ref, ci_ref, dk_ref, co_ref,
    sw_ref, sh_ref, sd_ref, sk_ref, np_ref, ns_ref, bp_ref, bs_ref,
    gn_o, cn_o, cb_o, cfi_o, cfo_o, cai_o, cao_o, cci_o, cdk_o, cco_o,
    nfi_o, nfo_o, nai_o, nao_o, nci_o, ndk_o, nco_o, nn_o, nb_o, nns_o, nbs_o,
    nsw_o, nsh_o, nsd_o, nsk_o,
    mat_f, mat_b, dir_f, dir_b,
):
    steps = jnp.full((1, 1), step_ref[0], jnp.int32).astype(F32)
    rate = PEAK_RATE * jnp.minimum(steps / WARM_STEPS, jnp.sqrt(WARM_STEPS / steps))
    grad_norm = jnp.sqrt(tot_ref[0:1, 0:1])
    threshold = math.sqrt(NPARAM)
    factor = threshold / jnp.maximum(grad_norm, threshold)
    square_factor = factor * factor
    gn_o[...] = jnp.broadcast_to(grad_norm, gn_o.shape)

    c_norm = lng_ref[...] * factor
    for i in range(5):
        clipped = c_norm[2 * i : 2 * i + 2, :]
        second = 0.5 * ns_ref[i] + 0.5 * clipped * clipped
        cn_o[i] = clipped
        nns_o[i] = second
        nn_o[i] = np_ref[i] - rate * SMALL_RATE * clipped * lax.rsqrt(second)
    c_bn = gbn_ref[0:2, 0:HEAD] * factor
    second = 0.5 * bs_ref[...] + 0.5 * c_bn * c_bn
    cb_o[...] = c_bn
    nbs_o[...] = second
    nb_o[...] = bp_ref[...] - rate * SMALL_RATE * c_bn * lax.rsqrt(second)

    eye_d = eye_of(D)
    scales_f = []
    for i in range(4):
        member, is_out = i // 2, i % 2
        chunk = (2, 0)[member]
        start = is_out * 256
        low = red_ref[chunk, start : start + D, :]
        wide_c = sw_ref[0, 2 * is_out + member, 0:1, 0:1]
        hidden_c = sd_ref[0, 2 * is_out + member, 0:1, 0:1]
        gram = tn(low, low) * square_factor
        wide = nt(low, low) * square_factor
        nsw_o[0, 2 * is_out + member] = 0.5 * wide_c * eye_d + 0.5 * wide
        nsd_o[0, 2 * is_out + member] = 0.5 * hidden_c * eye_d + 0.5 * gram
        clipped = low.astype(F32) * factor
        if is_out:
            cfo_o[member] = clipped.T
        else:
            cfi_o[member] = clipped
        dir_f[i] = clipped
        trace = total_of(clipped * clipped)
        power = total_of(gram * gram)
        scale = 1.0
        for k, c in enumerate((wide_c, hidden_c)):
            zoom = 2.5 * lax.rsqrt(0.25 * c * c * D + 0.5 * c * trace + 0.25 * power)
            mat_f[2 * i + k] = zoom * (0.5 * c * eye_d + 0.5 * gram)
            scale = scale * jnp.sqrt(jnp.sqrt(zoom))
        scales_f.append(scale)

    eye_b = eye_of(4 * PADH)
    row_block = lax.broadcasted_iota(jnp.int32, (4 * PADH, 1), 0) // PADH
    lane_block = lax.broadcasted_iota(jnp.int32, (1, 4 * PADH), 1) // PADH
    same_block = row_block == lane_block
    wide_of = (4, 5, 6, 10, 8, 9, 7, None)
    head_of = (0, 1, 2, 7, 4, 5, 3, 6)
    scales_b = []

    def spread(values):
        column = jnp.zeros((4 * PADH, 1), F32)
        for i, value in enumerate(values):
            column = jnp.where(row_block == i, value, column)
        return column

    for group in range(2):
        low = red_ref[1, group * 4 * PADH : (group + 1) * 4 * PADH, :]
        clipped = low.astype(F32) * factor
        dir_b[group] = clipped.T
        gram = jnp.where(same_block, nt(low, low), 0.0) * square_factor
        row_trace = jnp.sum(clipped * clipped, axis=1, keepdims=True)
        row_power = jnp.sum(gram * gram, axis=1, keepdims=True)
        wide_cs, head_cs, traces, powers, dims = [], [], [], [], []
        for i in range(4):
            index = group * 4 + i
            part = slice(i * PADH, (i + 1) * PADH)
            piece = low[part, :]
            head_c = sh_ref[0, 0, head_of[index] : head_of[index] + 1, 0:1]
            own_gram = nt(piece, piece)[:HEAD, :HEAD] * square_factor
            nsh_o[0, :, head_of[index], :] = 0.5 * head_c * eye_d[:HEAD, :HEAD] + 0.5 * own_gram
            wide = tn(piece, piece) * square_factor
            if wide_of[index] is None:
                wide_c = sk_ref[0, 0:1, 0:1]
                nsk_o[:, 0, :] = 0.5 * wide_c * eye_d[:KS, :KS] + 0.5 * wide[:KS, :KS]
                dims.append(KS)
            else:
                wide_c = sw_ref[0, wide_of[index], 0:1, 0:1]
                nsw_o[0, wide_of[index]] = 0.5 * wide_c * eye_d + 0.5 * wide
                dims.append(D)
            wide_cs.append(wide_c)
            head_cs.append(head_c)
            traces.append(jnp.sum(row_trace[part], axis=0, keepdims=True))
            powers.append(jnp.sum(row_power[part], axis=0, keepdims=True))
        scale = [1.0] * 4
        for k, (cs, sizes) in enumerate(((wide_cs, dims), (head_cs, [HEAD] * 4))):
            zooms = [
                2.5 * lax.rsqrt(0.25 * c * c * n + 0.5 * c * trace + 0.25 * power)
                for c, n, trace, power in zip(cs, sizes, traces, powers)
            ]
            mat_b[2 * group + k] = spread(zooms) * (0.5 * spread(cs) * eye_b + 0.5 * gram)
            scale = [s * jnp.sqrt(jnp.sqrt(zoom)) for s, zoom in zip(scale, zooms)]
        scales_b.append(scale)

    def advance(fine):
        for k in range(2):
            for mats, dirs, count in ((mat_f, dir_f, 4), (mat_b, dir_b, 2)):
                for i in range(count):
                    mats[2 * i + k], dirs[i] = next_power(mats[2 * i + k], dirs[i], fine)

    def coarse_step(i, carry):
        advance(False)
        return carry

    advance(True)
    lax.fori_loop(0, ROOT_ITERS - 2, coarse_step, 0)
    for k in range(2):
        for mats, dirs, count in ((mat_f, dir_f, 4), (mat_b, dir_b, 2)):
            for i in range(count):
                moved = nn(dirs[i].astype(BF16), mats[2 * i + k].astype(BF16))
                dirs[i] = 1.25 * dirs[i] - 0.25 * moved

    def graft(weight, direction):
        size = jnp.sqrt(total_of(weight * weight))
        return rate * GRAFT_SCALE * size / (jnp.sqrt(total_of(direction * direction)) + 1e-06)

    for i in range(4):
        member, is_out = i // 2, i % 2
        direction = dir_f[i] * scales_f[i]
        weight = (fi_ref, fo_ref)[is_out][member]
        if is_out:
            direction = direction.T
        (nfi_o, nfo_o)[is_out][member] = weight - graft(weight, direction) * direction
    turned_b = [dir_b[group].T for group in range(2)]
    for index in range(8):
        group, i = index // 4, index % 4
        part = slice(i * PADH, i * PADH + HEAD)
        direction = turned_b[group][part, :] * scales_b[group][i]
        clipped = red_ref[1, index * PADH : (index + 1) * PADH, :][:HEAD, :].astype(F32) * factor
        if index in (3, 6):
            weight_ref, clip_o, new_o = ((co_ref, cco_o, nco_o), None, None, (ao_ref, cao_o, nao_o))[index - 3]
            clip_o[...] = clipped
            new_o[...] = weight_ref[...] - graft(weight_ref[...], direction) * direction
        elif index == 7:
            turned = direction.T[:KS, :]
            cdk_o[...] = clipped.T[:KS, :]
            ndk_o[...] = dk_ref[...] - graft(dk_ref[...], turned) * turned
        else:
            weight_ref, clip_o, new_o = (ai_ref, cai_o, nai_o) if index < 3 else (ci_ref, cci_o, nci_o)
            at = (index,) if index < 3 else (slice(None), index - 4)
            weight = weight_ref[at]
            clip_o[at] = clipped
            new_o[at] = weight - graft(weight, direction) * direction


def shape(dims, dtype=F32):
    return jax.ShapeDtypeStruct(dims, dtype)


def whole(dims):
    zeros = (0,) * len(dims)
    return pl.BlockSpec(dims, lambda u: zeros)


SMEM_SPEC = pl.BlockSpec(memory_space=pltpu.SMEM)
VMEM_SPEC = pl.BlockSpec(memory_space=pltpu.VMEM)
PARAMS = pltpu.CompilerParams(vmem_limit_bytes=VMEM_CAP)


def update_call(step_count, total_square, reduced, lng, gbn, weights, stats, norm_params, norm_second, bn_params, bn_second):
    stat_wide, stat_head, stat_hidden, stat_kernel = stats
    corner = lambda a: pl.BlockSpec((1, a.shape[1], 8, 128), lambda i: (0, 0, 0, 0))
    one = lambda a: whole(a.shape)
    n_stat = lambda a: whole(a.shape)
    out_arrays = [
        shape((1, 128)), norm_params, bn_params, *weights, *weights, norm_params, bn_params, norm_params, bn_params,
        stat_wide, stat_head, stat_hidden, stat_kernel,
    ]
    in_arrays = [total_square, reduced, lng, gbn, *weights]
    wide = 4 * PADH
    return pl.pallas_call(
        update_kernel,
        grid=(1,),
        in_specs=[SMEM_SPEC] + [one(a) for a in in_arrays]
        + [corner(stat_wide), one(stat_head), corner(stat_hidden), one(stat_kernel)]
        + [one(a) for a in (norm_params, norm_second, bn_params, bn_second)],
        out_specs=[one(a) for a in out_arrays],
        out_shape=[shape(a.shape) for a in out_arrays],
        scratch_shapes=[
            pltpu.VMEM((8, D, D), F32), pltpu.VMEM((4, wide, wide), F32),
            pltpu.VMEM((4, D, D), F32), pltpu.VMEM((2, D, wide), F32),
        ],
        compiler_params=PARAMS,
        name="update_part",
    )(step_count, *in_arrays, *stats, norm_params, norm_second, bn_params, bn_second)


MESH = pl.DeviceIdType.MESH


def flip(index, bit):
    step = 2 ** bit
    return index + step - 2 * step * ((index // step) % 2)


def bits_of(count):
    bits = count.bit_length() - 1
    if 2 ** bits != count:
        raise ValueError("axis size")
    return bits


def greet_axes(counts):
    barrier = pltpu.get_barrier_semaphore()
    for axis, count in counts:
        me = lax.axis_index(axis)

        def signal(k, carry, axis=axis, count=count, me=me):
            pl.semaphore_signal(
                barrier, inc=1, device_id={axis: lax.rem(me + k, count)}, device_id_type=MESH
            )
            return carry

        lax.fori_loop(1, count, signal, 0)


def greeted(counts):
    pl.semaphore_wait(pltpu.get_barrier_semaphore(), sum(count - 1 for axis, count in counts))


def share_copy(axis, slots, sems, slot, peer, sent):
    return pltpu.make_async_remote_copy(
        src_ref=slots.at[slot], dst_ref=slots.at[slot], send_sem=sems[0].at[sent], recv_sem=sems[1].at[slot],
        device_id={axis: peer}, device_id_type=MESH,
    )


def share_start(axis, count, slots, sems):
    me = lax.axis_index(axis)

    def start(k, carry):
        peer = lax.rem(me + k, count)
        share_copy(axis, slots, sems, me, peer, peer).start()
        return carry

    lax.fori_loop(1, count, start, 0)


def share_finish(axis, count, slots, sems):
    me = lax.axis_index(axis)

    def finish(k, carry):
        peer = lax.rem(me + k, count)
        share_copy(axis, slots, sems, me, peer, peer).wait_send()
        share_copy(axis, slots, sems, peer, peer, peer).wait_recv()
        return carry

    lax.fori_loop(1, count, finish, 0)


def pool(slots, count):
    blank = jnp.zeros((1, 4 * PADH), F32)
    total = lax.fori_loop(0, count, lambda i, a: a + slots[i, 2:3, :], blank)
    mean = lax.fori_loop(0, count, lambda i, a: a + slots[i, 0:1, :] * slots[i, 2:3, :], blank) / total

    def power(i, a):
        off = slots[i, 0:1, :] - mean
        return a + slots[i, 1:2, :] + slots[i, 2:3, :] * off * off

    return mean, lax.fori_loop(0, count, power, blank), total


CHAINS = tuple((c, start, 256, 2) for c, start in ((0, 0), (0, 256), (1, 256), (1, 0), (2, 256), (2, 0)))
TAIL = (2, 5, 4, 0, 1, 5, 3, 0, 2, 1, 4, 5, 2, 3, 4, 5, 3, 4, 5)


def plan_of(dp_count, length, most):
    bits = bits_of(dp_count)
    radices = [2 ** (bits % most)] * (bits % most > 0) + [2**most] * (bits // most)
    plan, stride = [], 1
    for radix in radices:
        cut = length % (16 * radix) == 0
        length = length // radix if cut else length
        plan.append((stride, radix, cut, length))
        stride *= radix
    return plan


def landing_rows(dp_count):
    return sum(radix * piece for _, _, n, m in CHAINS for _, radix, _, piece in plan_of(dp_count, n, m))


def copy_count(dp_count):
    return sum(
        3 + sum((radix - 1) * (1 + cut) for _, radix, cut, _ in plan_of(dp_count, n, m)) for _, _, n, m in CHAINS
    )


def swish_slope(inner):
    sigma = sigmoid(inner)
    return sigma * (1.0 + inner * (1.0 - sigma))


HALVES = tuple(slice(i * 128, i * 128 + 128) for i in range(2))


def step_kernel(
    counts, names, lens_ref, x_ref, cot_ref, np_ref, fi_ref, fo_ref, ai_ref, ao_ref, ci_ref, co_ref, dk_ref, bp_ref,
    out_o, ig_o, red_o, lng_o, tot_o, gbn_o, *scratch,
):
    s = types.SimpleNamespace(**dict(zip(names, scratch)))
    dp_count = dict(counts)["dp"]
    shards = s.ffn1.shape[0]
    frames = x_ref.shape[1]
    utts = frames // LEN
    t, d = lax.axis_index("tensor"), lax.axis_index("dp")
    near, far = flip(t, 0), flip(t, 1)
    last = flip(near, 1)
    wide = 4 * PADH

    def rows_of(u, size=LEN):
        return pl.ds(pl.multiple_of(u * size, size), size)

    def length_of(u):
        return lens_ref[t * utts + u]

    def each(body, start=0, stop=utts):
        def turn(u, carry):
            body(u)
            return carry

        lax.fori_loop(start, stop, turn, 0)

    greet_axes(counts)

    own = pl.ds(pl.multiple_of(t * PADH, PADH), PADH)

    def mix_part(first, count):
        return lambda i: s.mix.at[pl.ds(first, count), pl.ds(pl.multiple_of(i * PADH, PADH), PADH), :]

    parts = (
        lambda i: s.small_parts.at[i],
        lambda i: s.ffn1.at[i],
        mix_part(0, 4),
        mix_part(4, 3),
        lambda i: s.ffn2.at[i],
    )

    def weight_copy(g, shard, peer, slot):
        return pltpu.make_async_remote_copy(
            src_ref=parts[g](shard), dst_ref=parts[g](shard), send_sem=s.gather_send.at[3 * g + slot],
            recv_sem=s.gather_recv.at[3 * g + slot], device_id={"tensor": peer}, device_id_type=MESH,
        )

    def launch(g):
        weight_copy(g, t, far, 0).start()
        weight_copy(g, t, near, 1).start()

    def relay(g):
        weight_copy(g, t, far, 0).wait()
        weight_copy(g, far, near, 2).start()

    def near_here(g):
        weight_copy(g, t, near, 1).wait()

    def last_here(g):
        weight_copy(g, far, near, 2).wait()

    def all_here(g):
        near_here(g)
        last_here(g)

    s.ffn1[t, 0] = fi_ref[0].astype(BF16)
    s.ffn1[t, 1] = fo_ref[0].astype(BF16)
    x0 = x_ref[...].astype(F32).T
    s.x1[...] = x0
    s.x0[...] = x0.astype(BF16)
    s.cot[...] = cot_ref[...].astype(F32).T.astype(BF16)
    blank = jnp.zeros((PADH - HEAD, D), F32)
    pieces = [ai_ref[m] for m in range(3)] + [ao_ref[...]] + [ci_ref[:, m, :] for m in range(2)] + [co_ref[...]]
    for i, piece in enumerate(pieces):
        s.mix[i, own, :] = jnp.concatenate([piece, blank], axis=0).astype(BF16)
    s.small_parts[t] = jnp.zeros((24, 128), F32)
    s.small_parts[t, 0:KS, 0:HEAD] = dk_ref[...]
    s.small_parts[t, 16:18, 0:HEAD] = bp_ref[...]
    greeted(counts)
    launch(1)
    launch(2)
    launch(0)
    launch(3)
    s.ffn2[t, 0] = fi_ref[1].astype(BF16)
    s.ffn2[t, 1] = fo_ref[1].astype(BF16)
    launch(4)
    for ref in (s.pad_f, s.pad_m, s.depth_grad, s.norm_grad, s.bn_grad):
        ref[...] = jnp.zeros_like(ref)

    def norm_one(u):
        rows = rows_of(u)
        x0 = s.x1[rows, :]
        s.n1[rows, :] = (standardize(x0)[0] * np_ref[0, 0:1, :] + np_ref[0, 1:2, :]).astype(BF16)

    each(norm_one)

    def feed_forward(shard):
        def body(u):
            rows = rows_of(u, 2 * LEN)
            inner = nn(s.n1[rows, :], s.ffn1[shard, 0])
            s.inner1[shard, rows, :] = inner
            active = (inner * sigmoid(inner)).astype(BF16)
            s.act1[shard, rows, :] = active
            s.x1[rows, :] += 0.5 * nn(active, s.ffn1[shard, 1])

        each(body, 0, utts // 2)

    feed_forward(t)
    near_here(1)
    feed_forward(near)
    relay(1)
    feed_forward(far)
    last_here(1)
    feed_forward(last)
    for g in (2, 0, 3):
        relay(g)
    for g in (2, 0, 3):
        all_here(g)
    for i in range(2):
        s.small[:, 128 * i : 128 * i + PADH] = s.small_parts[2 * i, :, 0:PADH]
        s.small[:, 128 * i + PADH : 128 * i + 128] = s.small_parts[2 * i + 1, :, 0:PADH]

    masks = lane_masks(BF16)

    def mix_forward(u):
        rows = rows_of(u)
        length = length_of(u)
        x1 = s.x1[rows, :]
        n2 = (standardize(x1)[0] * np_ref[1, 0:1, :] + np_ref[1, 1:2, :]).astype(BF16)
        s.n2[rows, :] = n2
        for i, ref in enumerate((s.q, s.k, s.v)):
            ref[rows, :] = nt(n2, s.mix[i]).astype(BF16)
        key_ok = lax.broadcasted_iota(jnp.int32, (1, LEN), 1) < length
        for half, lanes in enumerate(HALVES):
            q, k, v = s.q[rows, lanes], s.k[rows, lanes], s.v[rows, lanes]
            mixture = jnp.zeros((LEN, 128), F32)
            for side in range(2):
                scores = nt(q * masks[side], k) * HEAD ** (-0.5)
                scores = jnp.where(key_ok, scores, NEG_FILL)
                exps = jnp.exp(scores - jnp.max(scores, axis=-1, keepdims=True))
                probs = exps * (1.0 / jnp.sum(exps, axis=-1, keepdims=True))
                s.probs[u, 2 * half + side] = probs
                mixture = mixture + nn(probs.astype(BF16), v * masks[side])
            s.mixture[rows, lanes] = mixture.astype(BF16)
        x2 = x1 + nn(s.mixture[rows, :], s.mix[3])
        s.x2[rows, :] = x2
        n3 = (standardize(x2)[0] * np_ref[2, 0:1, :] + np_ref[2, 1:2, :]).astype(BF16)
        s.n3[rows, :] = n3
        value = nt(n3, s.mix[4])
        gate = nt(n3, s.mix[5])
        s.value[rows, :] = value
        s.gate[rows, :] = gate
        mask = row_mask(length)
        gated = value * sigmoid(gate) * mask
        count = length.astype(F32)
        for half, lanes in enumerate(HALVES):
            s.pad_f[half, 8 : 8 + LEN, :] = gated[:, lanes]
            running = jnp.zeros((LEN, 128), F32)
            for j in range(KS):
                running = running + s.pad_f[half, 1 + j : 1 + j + LEN, :] * s.small[j : j + 1, lanes]
            s.mid[rows, lanes] = running
            mean = jnp.sum(running * mask, axis=0, keepdims=True) / count
            centred = (running - mean) * mask
            s.stat[u, 0:1, lanes] = mean
            s.stat[u, 1:2, lanes] = jnp.sum(centred * centred, axis=0, keepdims=True)
            s.stat[u, 2:3, lanes] = jnp.full((1, 128), count, F32)

    each(mix_forward)

    held = pool(s.stat, utts)
    for axis, count in counts:
        slots = getattr(s, "moment_" + axis)
        sems = [getattr(s, "moment_" + axis + side) for side in ("_send", "_recv")]
        me = lax.axis_index(axis)
        slots[me] = jnp.concatenate([*held, jnp.zeros((5, wide), F32)], axis=0)
        share_start(axis, count, slots, sems)
        if axis == "dp":
            relay(4)
            near_here(4)
        share_finish(axis, count, slots, sems)
        held = pool(slots, count)
    last_here(4)
    mean, power, total = held
    inv_std = lax.rsqrt(power / total + 1e-05)
    inv_count = 1.0 / total
    s.bn[0:1, :] = mean
    s.bn[1:2, :] = inv_std
    s.bn[2:4, :] = s.small[16:18, :]
    s.bn[6:7, :] = inv_count

    def middle(u):
        rows = rows_of(u)
        mask = row_mask(length_of(u))
        mean, inv_std, gain, bias = [s.bn[i : i + 1, :] for i in range(4)]
        xhat = (s.mid[rows, :] - mean) * inv_std
        normal = xhat * gain + bias
        sigma = sigmoid(normal)
        act3 = (normal * sigma * mask).astype(BF16)
        s.act3[rows, :] = act3
        x3 = s.x2[rows, :] + nn(act3, s.mix[6])
        n4 = (standardize(x3)[0] * np_ref[3, 0:1, :] + np_ref[3, 1:2, :]).astype(BF16)
        s.n4[rows, :] = n4
        total = jnp.zeros((LEN, D), F32)
        for i in range(shards):
            inner = nn(n4, s.ffn2[i, 0])
            s.inner2[i] = inner
            active = (inner * sigmoid(inner)).astype(BF16)
            s.act2[i, rows, :] = active
            total = total + nn(active, s.ffn2[i, 1])
        x4 = x3 + 0.5 * total
        s.out[rows, :] = (standardize(x4)[0] * np_ref[4, 0:1, :] + np_ref[4, 1:2, :]).astype(BF16)
        d4, gain4, bias4 = norm_back(x4, np_ref[4, 0:1, :], s.cot[rows, :].astype(F32))
        g2 = (0.5 * d4).astype(BF16)
        s.g2[rows, :] = g2
        d_n4 = jnp.zeros((LEN, D), F32)
        for i in range(shards):
            d_inner = (nt(g2, s.ffn2[i, 1]) * swish_slope(s.inner2[i])).astype(BF16)
            s.din[i, rows, :] = d_inner
            d_n4 = d_n4 + nt(d_inner, s.ffn2[i, 0])
        d3, gain3, bias3 = norm_back(x3, np_ref[3, 0:1, :], d_n4)
        d3 = d3 + d4
        s.d3[rows, :] = d3
        gc = d3.astype(BF16)
        s.gc[rows, :] = gc
        d_normal = nt(gc, s.mix[6]) * mask * (sigma * (1.0 + normal * (1.0 - sigma)))
        s.d_normal[rows, :] = d_normal
        for i, part in enumerate((gain3, bias3, gain4, bias4)):
            s.norm_grad[6 + i : 7 + i, :] += part
        s.bn_grad[0:1, :] += jnp.sum(d_normal * xhat, axis=0, keepdims=True)
        s.bn_grad[1:2, :] += jnp.sum(d_normal, axis=0, keepdims=True)

    each(middle)

    sem_ids = itertools.count()

    def move(src, dst, peer):
        i = next(sem_ids)
        return pltpu.make_async_remote_copy(
            src_ref=src, dst_ref=dst, send_sem=s.reduce_send.at[i], recv_sem=s.reduce_recv.at[i],
            device_id=peer, device_id_type=MESH,
        )

    def add(target, other):
        return (target.astype(F32) + other.astype(F32)).astype(BF16)

    landing = [0]
    squares = []

    def square_of(a):
        a = a.astype(F32)
        return total_of(a * a)

    def chain(c, start, length, most):
        window = pl.ds(start, length)
        flights = [
            move(s.chunk.at[c, last, window], s.near.at[c, 1, window], {"tensor": near}),
            move(s.chunk.at[c, near, window], s.near.at[c, 0, window], {"tensor": near}),
        ]
        for flight in flights:
            flight.start()
        yield True
        flights[0].wait()
        s.acc[c, 1, window] = add(s.chunk[c, far, window], s.near[c, 1, window])
        flight = move(s.acc.at[c, 1, window], s.far.at[c, window], {"tensor": far})
        flight.start()
        flights[1].wait()
        yield True
        flight.wait()
        pair = s.chunk[c, t, window].astype(F32) + s.near[c, 0, window].astype(F32)
        s.acc[c, 0, window] = (pair + s.far[c, window].astype(F32)).astype(BF16)
        offset, size, trail, copies = start, length, [], 1
        for stride, radix, cut, piece in plan_of(dp_count, length, most):
            digit = (d // stride) % radix
            base = landing[0]
            landing[0] += radix * piece

            def slot(i):
                return pl.ds(pl.multiple_of(base + i * piece, 16), piece)

            def part(i):
                return pl.ds(pl.multiple_of(offset + i * piece if cut else offset, 16), piece)

            flights = []
            for k in range(1, radix):
                other = (digit + k) % radix
                peer = {"dp": d + (other - digit) * stride}
                flights.append(move(s.acc.at[c, 0, part(other)], s.land.at[slot(digit)], peer))
                flights[-1].start()
            s.land[slot(digit)] = s.acc[c, 0, part(digit)]
            yield True
            for flight in flights:
                flight.wait()
            total = s.land[slot(0)].astype(F32)
            for i in range(1, radix):
                total = total + s.land[slot(i)].astype(F32)
            s.acc[c, 0, part(digit)] = total.astype(BF16)
            if cut:
                trail.append((stride, radix, offset))
                offset, size = offset + digit * piece, piece
            else:
                copies *= radix
        here = pl.ds(pl.multiple_of(offset, 16), size)
        red_o[c, here] = s.acc[c, 0, here]
        squares.append(square_of(s.acc[c, 0, here]) * (1.0 / copies))
        for stride, radix, before in trail[::-1]:
            digit = (d // stride) % radix
            here = pl.ds(pl.multiple_of(offset, 16), size)
            flights = []
            for k in range(1, radix):
                peer = {"dp": d + ((digit + k) % radix - digit) * stride}
                flights.append(move(red_o.at[c, here], red_o.at[c, here], peer))
                flights[-1].start()
            yield True
            for flight in flights:
                flight.wait()
            offset, size = before, size * radix

    live = {}

    def begin(i):
        live[i] = chain(*CHAINS[i])
        next(live[i])

    def pump(*chosen):
        for i in chosen or tuple(live):
            if i in live and next(live[i], None) is None:
                del live[i]

    def spread_rows(c, first, left, right):
        full = tn(left, right).astype(BF16)
        for i in range(shards):
            s.chunk[c, i, first : first + PADH, :] = full[PADH * i : PADH * (i + 1), :]

    totals = ("total_dp", "total_tensor")
    count_of = dict(counts)

    def sems_of(name):
        return [getattr(s, name + side) for side in ("_send", "_recv")]

    s.total_dp[d] = s.bn_grad[...]
    share_start("dp", dp_count, s.total_dp, sems_of("total_dp"))
    for c in (0, 2):
        for i in range(shards):
            for first in (0, 256):
                s.chunk[c, i, first + D : first + 256, :] = jnp.zeros((256 - D, D), BF16)
    for i in range(shards):
        s.chunk[0, i, 0:D, :] = tn(s.n4[...], s.din[i]).astype(BF16)
    begin(0)
    share_finish("dp", dp_count, s.total_dp, sems_of("total_dp"))
    s.total_tensor[t] = lax.fori_loop(1, dp_count, lambda i, a: a + s.total_dp[i], s.total_dp[0])
    share_start("tensor", shards, s.total_tensor, sems_of("total_tensor"))
    for i in range(shards):
        s.chunk[0, i, 256 : 256 + D, :] = tn(s.g2[...], s.act2[i]).astype(BF16)
    begin(1)
    spread_rows(1, 3 * PADH, s.act3[...], s.gc[...])
    share_finish("tensor", shards, s.total_tensor, sems_of("total_tensor"))
    bn_sums = lax.fori_loop(1, shards, lambda i, a: a + s.total_tensor[i], s.total_tensor[0])
    s.bn[4:6, :] = bn_sums[0:2, :]

    def conv_back(u):
        rows = rows_of(u)
        mask = row_mask(length_of(u))
        mean, inv_std, gain, bias, sum_gain, sum_bias, inv_count = [s.bn[i : i + 1, :] for i in range(7)]
        xhat = (s.mid[rows, :] - mean) * inv_std
        d_mid = inv_std * gain * (s.d_normal[rows, :] - mask * ((sum_bias + xhat * sum_gain) * inv_count))
        value = s.value[rows, :]
        sigma = sigmoid(s.gate[rows, :])
        gated = value * sigma * mask
        for half, lanes in enumerate(HALVES):
            s.pad_f[half, 8 : 8 + LEN, :] = gated[:, lanes]
            s.pad_m[half, 8 : 8 + LEN, :] = d_mid[:, lanes]
            d_gated = jnp.zeros((LEN, 128), F32)
            mid_half = d_mid[:, lanes]
            for j in range(KS):
                d_gated = d_gated + s.pad_m[half, 15 - j : 15 - j + LEN, :] * s.small[j : j + 1, lanes]
                s.depth_grad[j : j + 1, lanes] += jnp.sum(
                    s.pad_f[half, 1 + j : 1 + j + LEN, :] * mid_half, axis=0, keepdims=True
                )
            d_gated = d_gated * mask
            sig = sigma[:, lanes]
            s.d_value[rows, lanes] = (d_gated * sig).astype(BF16)
            s.d_gate[rows, lanes] = (d_gated * value[:, lanes] * sig * (1.0 - sig)).astype(BF16)
        d_n3 = nn(s.d_value[rows, :], s.mix[4]) + nn(s.d_gate[rows, :], s.mix[5])
        d2, gain2, bias2 = norm_back(s.x2[rows, :], np_ref[2, 0:1, :], d_n3)
        d2 = d2 + s.d3[rows, :]
        s.d2[rows, :] = d2
        s.ga[rows, :] = d2.astype(BF16)
        for i, part in enumerate((gain2, bias2)):
            s.norm_grad[4 + i : 5 + i, :] += part

    each(conv_back)
    pump(0, 1)
    eye = (
        lax.broadcasted_iota(jnp.int32, (16, D), 0) == lax.broadcasted_iota(jnp.int32, (16, D), 1)
    ).astype(BF16)
    spread_rows(1, 4 * PADH, s.d_value[...], s.n3[...])
    spread_rows(1, 5 * PADH, s.d_gate[...], s.n3[...])
    spread_rows(1, 6 * PADH, s.mixture[...], s.ga[...])
    spread_rows(1, 7 * PADH, s.depth_grad[...].astype(BF16), eye)
    begin(2)

    def attend_back(u):
        rows = rows_of(u)
        d_mix = nt(s.ga[rows, :], s.mix[3]).astype(BF16)
        for half, lanes in enumerate(HALVES):
            q, k, v, dm = s.q[rows, lanes], s.k[rows, lanes], s.v[rows, lanes], d_mix[:, lanes]
            dq = jnp.zeros((LEN, 128), F32)
            dk = jnp.zeros((LEN, 128), F32)
            dv = jnp.zeros((LEN, 128), F32)
            for side in range(2):
                probs = s.probs[u, 2 * half + side]
                dm_side = dm * masks[side]
                d_probs = nt(dm_side, v)
                dv = dv + tn(probs.astype(BF16), dm_side)
                row_sum = jnp.sum(probs * d_probs, axis=-1, keepdims=True)
                d_scores = (probs * (d_probs - row_sum)).astype(BF16)
                dq = dq + nn(d_scores, k * masks[side])
                dk = dk + tn(d_scores, q * masks[side])
            s.dq[rows, lanes] = (dq * HEAD ** (-0.5)).astype(BF16)
            s.dk[rows, lanes] = (dk * HEAD ** (-0.5)).astype(BF16)
            s.dv[rows, lanes] = dv.astype(BF16)
        d_n2 = nn(s.dq[rows, :], s.mix[0]) + nn(s.dk[rows, :], s.mix[1]) + nn(s.dv[rows, :], s.mix[2])
        d1, gain1, bias1 = norm_back(s.x1[rows, :], np_ref[1, 0:1, :], d_n2)
        d1 = d1 + s.d2[rows, :]
        s.d1[rows, :] = d1
        s.g1[rows, :] = (0.5 * d1).astype(BF16)
        s.d_n1[rows, :] = jnp.zeros((LEN, D), F32)
        for i, part in enumerate((gain1, bias1)):
            s.norm_grad[2 + i : 3 + i, :] += part

    each(attend_back, 0, utts // 2)
    pump(2)
    each(attend_back, utts // 2, utts)
    pump(0)
    spread_rows(1, 0, s.dq[...], s.n2[...])
    spread_rows(1, PADH, s.dk[...], s.n2[...])
    spread_rows(1, 2 * PADH, s.dv[...], s.n2[...])
    begin(3)
    pump(1)
    for i in range(shards):
        s.chunk[2, i, 256 : 256 + D, :] = tn(s.g1[...], s.act1[i]).astype(BF16)
    begin(4)
    pump(3)

    for place, shard in enumerate((last, near, far, t)):
        def feed_back(u):
            rows = rows_of(u, 2 * LEN)
            d_inner = (nt(s.g1[rows, :], s.ffn1[shard, 1]) * swish_slope(s.inner1[shard, rows, :])).astype(BF16)
            s.din1[place, rows, :] = d_inner
            s.d_n1[rows, :] += nt(d_inner, s.ffn1[shard, 0])

        each(feed_back, 0, utts // 2)
        s.chunk[2, shard, 0:D, :] = tn(s.n1[...], s.din1[place]).astype(BF16)
        if place == 0:
            pump(0, 2, 4, 1)
        if place == 1:
            begin(5)
        if place == 2:
            pump(3, 2, 5, 0)
        if place == 3:
            pump(4, 1)

    def norm_zero(u):
        rows = rows_of(u)
        d0, gain0, bias0 = norm_back(s.x0[rows, :].astype(F32), np_ref[0, 0:1, :], s.d_n1[rows, :])
        s.d1[rows, :] += d0
        for i, part in enumerate((gain0, bias0)):
            s.norm_grad[i : i + 1, :] += part

    each(norm_zero)
    s.norm_dp[d] = s.norm_grad[...]
    share_start("dp", dp_count, s.norm_dp, sems_of("norm_dp"))
    pump(3)
    own_block = lax.broadcasted_iota(jnp.int32, (1, wide), 1) // PADH == t
    gb = s.bn[4:6, :]
    gbn_o[...] = jnp.zeros_like(gbn_o)
    for i in range(4):
        @pl.when(t == i)
        def _():
            gbn_o[0:2, 0:PADH] = gb[:, i * PADH : (i + 1) * PADH]

    out_o[...] = s.out[...].astype(F32).T.astype(BF16)
    for i in TAIL[:4]:
        pump(i)
    share_finish("dp", dp_count, s.norm_dp, sems_of("norm_dp"))
    s.norm_tensor[t] = lax.fori_loop(1, dp_count, lambda i, a: a + s.norm_dp[i], s.norm_dp[0])
    share_start("tensor", shards, s.norm_tensor, sems_of("norm_tensor"))
    ig_o[...] = s.d1[...].T
    for i in TAIL[4:8]:
        pump(i)
    share_finish("tensor", shards, s.norm_tensor, sems_of("norm_tensor"))
    norm_sums = lax.fori_loop(1, shards, lambda i, a: a + s.norm_tensor[i], s.norm_tensor[0])
    lng_o[...] = norm_sums
    rest = list(TAIL[8:])
    while len(squares) < len(CHAINS):
        pump(*([rest.pop(0)] if rest else []))
    square = functools.reduce(lambda a, b: a + b, squares)
    square = square + total_of(jnp.where(own_block, gb * gb, 0.0)) * (1.0 / dp_count)
    s.square_dp[d] = jnp.broadcast_to(square, (8, 128))
    share_start("dp", dp_count, s.square_dp, sems_of("square_dp"))
    for i in rest[:-1]:
        pump(i)
    share_finish("dp", dp_count, s.square_dp, sems_of("square_dp"))
    s.square_tensor[t] = lax.fori_loop(1, dp_count, lambda i, a: a + s.square_dp[i], s.square_dp[0])
    share_start("tensor", shards, s.square_tensor, sems_of("square_tensor"))
    while live:
        pump()
    share_finish("tensor", shards, s.square_tensor, sems_of("square_tensor"))
    square = lax.fori_loop(1, shards, lambda i, a: a + s.square_tensor[i], s.square_tensor[0])
    tot_o[...] = square + jnp.broadcast_to(square_of(norm_sums), (8, 128))


def step_call(lengths, x, cot, norm_params, ffn_in, ffn_out, attn_in, attn_out, conv_in, conv_out, depth_kernel, bn_params):
    counts = tuple((axis, lax.axis_size(axis)) for axis in ("dp", "tensor"))
    dp_count, shards = counts[0][1], counts[1][1]
    frames = x.shape[1]
    utts = frames // LEN
    wide = 4 * PADH
    low = lambda *dims: pltpu.VMEM(dims, BF16)
    full = lambda *dims: pltpu.VMEM(dims, F32)
    copies = copy_count(dp_count)
    scratch = {
        "ffn1": low(shards, 2, D, D), "ffn2": low(shards, 2, D, D), "mix": low(7, wide, D),
        "small_parts": full(shards, 24, 128), "small": full(24, wide),
        "x1": full(frames, D), "x2": full(frames, D), "d1": full(frames, D), "d2": full(frames, D),
        "d3": full(frames, D), "d_n1": full(frames, D),
        "x0": low(frames, D), "cot": low(frames, D), "out": low(frames, D),
        "n1": low(frames, D), "n2": low(frames, D), "n3": low(frames, D), "n4": low(frames, D),
        "inner1": full(shards, frames, D), "act1": low(shards, frames, D), "din1": low(shards, frames, D),
        "inner2": full(shards, LEN, D), "act2": low(shards, frames, D), "din": low(shards, frames, D),
        "q": low(frames, wide), "k": low(frames, wide), "v": low(frames, wide), "mixture": low(frames, wide),
        "dq": low(frames, wide), "dk": low(frames, wide), "dv": low(frames, wide),
        "d_value": low(frames, wide), "d_gate": low(frames, wide), "act3": low(frames, wide),
        "probs": full(utts, 4, LEN, LEN), "value": full(frames, wide), "gate": full(frames, wide),
        "mid": full(frames, wide), "d_normal": full(frames, wide),
        "g1": low(frames, D), "g2": low(frames, D), "ga": low(frames, D), "gc": low(frames, D),
        "pad_f": full(2, LEN + 16, 128), "pad_m": full(2, LEN + 16, 128), "stat": full(utts, 8, wide),
        "bn": full(8, wide), "depth_grad": full(16, wide), "norm_grad": full(16, D), "bn_grad": full(8, wide),
        "chunk": low(3, shards, 512, D), "near": low(3, 2, 512, D), "acc": low(3, 2, 512, D), "far": low(3, 512, D),
        "land": low(landing_rows(dp_count), D),
        "gather_send": pltpu.SemaphoreType.DMA((15,)), "gather_recv": pltpu.SemaphoreType.DMA((15,)),
        "reduce_send": pltpu.SemaphoreType.DMA((copies,)), "reduce_recv": pltpu.SemaphoreType.DMA((copies,)),
    }
    for name, rows, width in (("moment", 8, wide), ("total", 8, wide), ("norm", 16, D), ("square", 8, 128)):
        for axis, count in counts:
            scratch[name + "_" + axis] = full(count, rows, width)
            for side in ("_send", "_recv"):
                scratch[name + "_" + axis + side] = pltpu.SemaphoreType.DMA((count,))
    return pl.pallas_call(
        functools.partial(step_kernel, counts, tuple(scratch)),
        in_specs=[SMEM_SPEC] + [VMEM_SPEC] * 11,
        out_specs=[VMEM_SPEC] * 6,
        out_shape=[
            shape((D, frames), BF16), shape((D, frames)), shape((3, 512, D), BF16), shape((16, D)), shape((8, 128)),
            shape((8, 128)),
        ],
        scratch_shapes=list(scratch.values()),
        compiler_params=pltpu.CompilerParams(collective_id=0, has_side_effects=True, vmem_limit_bytes=VMEM_CAP),
        name="step_part",
    )(lengths, x, cot, norm_params, ffn_in, ffn_out, attn_in, attn_out, conv_in, conv_out, depth_kernel, bn_params)


def local(
    block_input, lengths, cotangent, norm_params, bn_params, ffn_in, ffn_out, attn_in, attn_out, conv_in,
    depth_kernel, conv_out, stat_wide, stat_head, stat_hidden, stat_kernel, norm_second, bn_second, step_count,
):
    attn_in, conv_in = attn_in.swapaxes(1, 2), conv_in.transpose(2, 0, 1)
    stat_head, stat_kernel = stat_head.swapaxes(1, 2), stat_kernel.swapaxes(0, 1)
    block_out, input_grad, reduced, lng, total_square, gbn = step_call(
        lengths, block_input.T, cotangent.T, norm_params, ffn_in, ffn_out, attn_in, attn_out, conv_in, conv_out,
        depth_kernel, bn_params,
    )
    weights = (ffn_in, ffn_out, attn_in, attn_out, conv_in, depth_kernel, conv_out)
    outs = list(
        update_call(
            step_count, total_square, reduced, lng, gbn, weights, (stat_wide, stat_head, stat_hidden, stat_kernel),
            norm_params, norm_second, bn_params, bn_second,
        )
    )
    for i in (5, 12):
        outs[i] = outs[i].swapaxes(1, 2)
    for i in (7, 14):
        outs[i] = outs[i].transpose(1, 2, 0)
    outs[22] = outs[22].swapaxes(1, 2)
    outs[24] = outs[24].swapaxes(0, 1)
    return (block_out.T, input_grad.T, outs[0][0, :1], *outs[1:])


def solution(mesh):
    weights_specs = (
        P(None, None, "tensor"), P(None, "tensor", None), P(None, None, "tensor"), P("tensor", None),
        P(None, None, "tensor"), P(None, "tensor"), P("tensor", None),
    )
    stat_specs = (
        P("tensor", None, None, None), P("tensor", None, None, None), P("tensor", None, None, None),
        P("tensor", None, None),
    )
    frames = P(("dp", "tensor"), None)
    channels = P(None, "tensor")
    return jax.shard_map(
        local,
        mesh=mesh,
        in_specs=(frames, P("dp"), frames, P(), channels, *weights_specs, *stat_specs, P(), channels, P()),
        out_specs=(
            frames, frames, P(), P(), channels, *weights_specs, *weights_specs, P(), channels, P(), channels,
            *stat_specs,
        ),
        check_vma=False,
    )
```

```python
import functools
import itertools
import math
import types

import jax
import jax.numpy as jnp
from jax import lax
from jax.experimental import pallas as pl
from jax.experimental.pallas import tpu as pltpu
from jax.sharding import PartitionSpec as P

D = 240
KS = 15
LEN = 192
HEAD = 60
PADH = 64
ROOT_ITERS = 8
NPARAM = 1331280
PEAK_RATE = 2.0
WARM_STEPS = 4.0
SMALL_RATE = 0.3
GRAFT_SCALE = 0.6
NEG_FILL = -1000000000.0
VMEM_CAP = 60 * 1024 * 1024

F32 = jnp.float32
BF16 = jnp.bfloat16


def nn(a, b):
    return lax.dot_general(a, b, (((1,), (0,)), ((), ())), preferred_element_type=F32)


def nt(a, b):
    return lax.dot_general(a, b, (((1,), (1,)), ((), ())), preferred_element_type=F32)


def tn(a, b):
    return lax.dot_general(a, b, (((0,), (0,)), ((), ())), preferred_element_type=F32)


def sigmoid(v):
    return 0.5 * jnp.tanh(0.5 * v) + 0.5


def standardize(h):
    centred = h - jnp.sum(h, axis=-1, keepdims=True) * (1.0 / D)
    spread = jnp.sum(centred * centred, axis=-1, keepdims=True) * (1.0 / D)
    inv = lax.rsqrt(spread + 1e-05)
    return centred * inv, inv


def norm_back(h, gain, dy):
    xhat, inv = standardize(h)
    scaled = dy * gain
    mean_a = jnp.sum(scaled, axis=-1, keepdims=True) * (1.0 / D)
    mean_b = jnp.sum(scaled * xhat, axis=-1, keepdims=True) * (1.0 / D)
    dh = inv * (scaled - mean_a - xhat * mean_b)
    return dh, jnp.sum(dy * xhat, axis=0, keepdims=True), jnp.sum(dy, axis=0, keepdims=True)


def row_mask(length):
    return (lax.broadcasted_iota(jnp.int32, (LEN, 1), 0) < length).astype(F32)


def lane_masks(dtype):
    lane = lax.broadcasted_iota(jnp.int32, (1, 128), 1)
    return ((lane < PADH).astype(dtype), (lane >= PADH).astype(dtype))


def split(a):
    high = a.astype(BF16)
    return high, (a - high.astype(F32)).astype(BF16)


def stacked(lefts, right):
    full = nn(jnp.concatenate(lefts, axis=0), right)
    places, at = [], 0
    for left in lefts:
        places.append(full[at : at + left.shape[0]])
        at += left.shape[0]
    return places


def mul_fine(a, b, rider=None):
    high, cross, *rest = stacked([*a] + ([] if rider is None else [rider]), b[0])
    return (high + (nn(a[0], b[1]) + cross), *rest)


def eye_of(n):
    return (lax.broadcasted_iota(jnp.int32, (n, n), 0) == lax.broadcasted_iota(jnp.int32, (n, n), 1)).astype(F32)


def next_power(own, direction, fine):
    rider = direction.astype(BF16)
    if fine:
        parts = split(own)
        square, moved = mul_fine(parts, parts, rider)
        step = 0.0625 * square - 0.625 * own
        halves = split(step)
        once = mul_fine(halves, parts)[0]
        twice = mul_fine(halves, split(once))[0]
    else:
        low = own.astype(BF16)
        square, moved = stacked([low, rider], low)
        step = (0.0625 * square - 0.625 * own).astype(BF16)
        once = nn(step, low)
        twice = nn(step, once.astype(BF16))
    return 2.44140625 * own + 3.125 * once + twice, 1.25 * direction - 0.25 * moved


def total_of(a):
    return jnp.sum(jnp.sum(a, axis=1, keepdims=True), axis=0, keepdims=True)


def update_kernel(
    step_ref, tot_ref, red_ref, lng_ref, gbn_ref, fi_far, fo_far, ai_ref, ao_ref, ci_ref, dk_ref, co_ref,
    sw_ref, sh_ref, sd_ref, sk_ref, np_ref, ns_ref, bp_ref, bs_ref, rows_far, back_far,
    gn_o, cn_o, cb_o, cfi_far, cfo_far, cai_o, cao_o, cci_o, cdk_o, cco_o,
    nfi_o, nfo_o, nai_o, nao_o, nci_o, ndk_o, nco_o, nn_o, nb_o, nns_o, nbs_o,
    nsw_far, nsh_o, nsd_far, nsk_o, turned_far, back_o,
    mat_f, mat_b, dir_f, dir_b, fi_ref, fo_ref, rows_sc, back_sc, cfi_o, cfo_o, nsw_o, nsd_o, turned_sc, turned_back,
    in_sem, out_sem,
):
    fetches = [
        pltpu.make_async_copy(src, dst, in_sem.at[i])
        for i, (src, dst) in enumerate(
            ((rows_far, rows_sc), (back_far, back_sc), (fi_far, fi_ref), (fo_far, fo_ref))
        )
    ]
    for fetch in fetches:
        fetch.start()
    stores = [
        pltpu.make_async_copy(src, dst, out_sem.at[i])
        for i, (src, dst) in enumerate(
            (
                (nsw_o, nsw_far), (nsd_o, nsd_far), (cfi_o, cfi_far), (cfo_o, cfo_far), (turned_sc, turned_far),
                (turned_back, back_o),
            )
        )
    ]
    steps = jnp.full((1, 1), step_ref[0], jnp.int32).astype(F32)
    rate = PEAK_RATE * jnp.minimum(steps / WARM_STEPS, jnp.sqrt(WARM_STEPS / steps))
    grad_norm = jnp.sqrt(tot_ref[0:1, 0:1])
    threshold = math.sqrt(NPARAM)
    factor = threshold / jnp.maximum(grad_norm, threshold)
    square_factor = factor * factor
    gn_o[...] = jnp.broadcast_to(grad_norm, gn_o.shape)

    c_norm = lng_ref[...] * factor
    for i in range(5):
        clipped = c_norm[2 * i : 2 * i + 2, :]
        second = 0.5 * ns_ref[i] + 0.5 * clipped * clipped
        cn_o[i] = clipped
        nns_o[i] = second
        nn_o[i] = np_ref[i] - rate * SMALL_RATE * clipped * lax.rsqrt(second)
    c_bn = gbn_ref[0:2, 0:HEAD] * factor
    second = 0.5 * bs_ref[...] + 0.5 * c_bn * c_bn
    cb_o[...] = c_bn
    nbs_o[...] = second
    nb_o[...] = bp_ref[...] - rate * SMALL_RATE * c_bn * lax.rsqrt(second)

    eye_d = eye_of(D)
    scales_f = []
    for i in range(4):
        member, is_out = i // 2, i % 2
        chunk = (2, 0)[member]
        start = is_out * 256
        low = red_ref[chunk, start : start + D, :]
        wide_c = sw_ref[0, 2 * is_out + member, 0:1, 0:1]
        hidden_c = sd_ref[0, 2 * is_out + member, 0:1, 0:1]
        gram = tn(low, low) * square_factor
        wide = nt(low, low) * square_factor
        nsw_o[0, 2 * is_out + member] = 0.5 * wide_c * eye_d + 0.5 * wide
        nsd_o[0, 2 * is_out + member] = 0.5 * hidden_c * eye_d + 0.5 * gram
        clipped = low.astype(F32) * factor
        if is_out:
            cfo_o[member] = clipped.T
        else:
            cfi_o[member] = clipped
        dir_f[i] = clipped
        trace = total_of(clipped * clipped)
        power = total_of(gram * gram)
        scale = 1.0
        for k, c in enumerate((wide_c, hidden_c)):
            zoom = 2.5 * lax.rsqrt(0.25 * c * c * D + 0.5 * c * trace + 0.25 * power)
            mat_f[2 * i + k] = zoom * (0.5 * c * eye_d + 0.5 * gram)
            scale = scale * jnp.sqrt(jnp.sqrt(zoom))
        scales_f.append(scale)

    eye_b = eye_of(4 * PADH)
    row_block = lax.broadcasted_iota(jnp.int32, (4 * PADH, 1), 0) // PADH
    lane_block = lax.broadcasted_iota(jnp.int32, (1, 4 * PADH), 1) // PADH
    same_block = row_block == lane_block
    wide_of = (4, 5, 6, 10, 8, 9, 7, None)
    head_of = (0, 1, 2, 7, 4, 5, 3, 6)
    scales_b = []

    def spread(values):
        column = jnp.zeros((4 * PADH, 1), F32)
        for i, value in enumerate(values):
            column = jnp.where(row_block == i, value, column)
        return column

    for group in range(2):
        low = red_ref[1, group * 4 * PADH : (group + 1) * 4 * PADH, :]
        clipped = low.astype(F32) * factor
        dir_b[group] = clipped.T
        gram = jnp.where(same_block, nt(low, low), 0.0) * square_factor
        row_trace = jnp.sum(clipped * clipped, axis=1, keepdims=True)
        row_power = jnp.sum(gram * gram, axis=1, keepdims=True)
        wide_cs, head_cs, traces, powers, dims = [], [], [], [], []
        for i in range(4):
            index = group * 4 + i
            part = slice(i * PADH, (i + 1) * PADH)
            piece = low[part, :]
            head_c = sh_ref[0, 0, head_of[index] : head_of[index] + 1, 0:1]
            own_gram = nt(piece, piece)[:HEAD, :HEAD] * square_factor
            nsh_o[0, :, head_of[index], :] = 0.5 * head_c * eye_d[:HEAD, :HEAD] + 0.5 * own_gram
            wide = tn(piece, piece) * square_factor
            if wide_of[index] is None:
                wide_c = sk_ref[0, 0:1, 0:1]
                nsk_o[:, 0, :] = 0.5 * wide_c * eye_d[:KS, :KS] + 0.5 * wide[:KS, :KS]
                dims.append(KS)
            else:
                wide_c = sw_ref[0, wide_of[index], 0:1, 0:1]
                nsw_o[0, wide_of[index]] = 0.5 * wide_c * eye_d + 0.5 * wide
                dims.append(D)
            wide_cs.append(wide_c)
            head_cs.append(head_c)
            traces.append(jnp.sum(row_trace[part], axis=0, keepdims=True))
            powers.append(jnp.sum(row_power[part], axis=0, keepdims=True))
        scale = [1.0] * 4
        for k, (cs, sizes) in enumerate(((wide_cs, dims), (head_cs, [HEAD] * 4))):
            zooms = [
                2.5 * lax.rsqrt(0.25 * c * c * n + 0.5 * c * trace + 0.25 * power)
                for c, n, trace, power in zip(cs, sizes, traces, powers)
            ]
            mat_b[2 * group + k] = spread(zooms) * (0.5 * spread(cs) * eye_b + 0.5 * gram)
            scale = [s * jnp.sqrt(jnp.sqrt(zoom)) for s, zoom in zip(scale, zooms)]
        scales_b.append(scale)

    def advance(fine):
        for k in range(2):
            for mats, dirs, count in ((mat_f, dir_f, 4), (mat_b, dir_b, 2)):
                for i in range(count):
                    mats[2 * i + k], dirs[i] = next_power(mats[2 * i + k], dirs[i], fine)

    def coarse_step(i, carry):
        advance(False)
        if width < frames:
            turn(i)
        return carry

    for store in stores[:4]:
        store.start()
    advance(True)
    for fetch in fetches:
        fetch.wait()
    frames = rows_sc.shape[0]
    steps = ROOT_ITERS - 2
    width = frames // steps if frames % (128 * steps) == 0 else frames

    def turn(i):
        here = pl.ds(pl.multiple_of(i * width, width), width)
        turned_sc[:, here] = rows_sc[here, :].astype(F32).T.astype(BF16)
        turned_back[:, here] = back_sc[here, :].T

    if width == frames:
        turn(0)
    lax.fori_loop(0, steps, coarse_step, 0)
    for store in stores[4:]:
        store.start()
    for k in range(2):
        for mats, dirs, count in ((mat_f, dir_f, 4), (mat_b, dir_b, 2)):
            for i in range(count):
                moved = nn(dirs[i].astype(BF16), mats[2 * i + k].astype(BF16))
                dirs[i] = 1.25 * dirs[i] - 0.25 * moved

    def graft(weight, direction):
        size = jnp.sqrt(total_of(weight * weight))
        return rate * GRAFT_SCALE * size / (jnp.sqrt(total_of(direction * direction)) + 1e-06)

    for i in range(4):
        member, is_out = i // 2, i % 2
        direction = dir_f[i] * scales_f[i]
        weight = (fi_ref, fo_ref)[is_out][member]
        if is_out:
            direction = direction.T
        (nfi_o, nfo_o)[is_out][member] = weight - graft(weight, direction) * direction
    turned_b = [dir_b[group].T for group in range(2)]
    for index in range(8):
        group, i = index // 4, index % 4
        part = slice(i * PADH, i * PADH + HEAD)
        direction = turned_b[group][part, :] * scales_b[group][i]
        clipped = red_ref[1, index * PADH : (index + 1) * PADH, :][:HEAD, :].astype(F32) * factor
        if index in (3, 6):
            weight_ref, clip_o, new_o = ((co_ref, cco_o, nco_o), None, None, (ao_ref, cao_o, nao_o))[index - 3]
            clip_o[...] = clipped
            new_o[...] = weight_ref[...] - graft(weight_ref[...], direction) * direction
        elif index == 7:
            turned = direction.T[:KS, :]
            cdk_o[...] = clipped.T[:KS, :]
            ndk_o[...] = dk_ref[...] - graft(dk_ref[...], turned) * turned
        else:
            weight_ref, clip_o, new_o = (ai_ref, cai_o, nai_o) if index < 3 else (ci_ref, cci_o, nci_o)
            at = (index,) if index < 3 else (slice(None), index - 4)
            weight = weight_ref[at]
            clip_o[at] = clipped
            new_o[at] = weight - graft(weight, direction) * direction
    for store in stores:
        store.wait()


def shape(dims, dtype=F32):
    return jax.ShapeDtypeStruct(dims, dtype)


def whole(dims):
    zeros = (0,) * len(dims)
    return pl.BlockSpec(dims, lambda u: zeros)


SMEM_SPEC = pl.BlockSpec(memory_space=pltpu.SMEM)
VMEM_SPEC = pl.BlockSpec(memory_space=pltpu.VMEM)
ANY_SPEC = pl.BlockSpec(memory_space=pl.ANY)
PARAMS = pltpu.CompilerParams(vmem_limit_bytes=VMEM_CAP)


def update_call(step_count, total_square, reduced, lng, gbn, weights, stats, norm_params, norm_second, bn_params, bn_second, rows, back):
    stat_wide, stat_head, stat_hidden, stat_kernel = stats
    corner = lambda a: pl.BlockSpec((1, a.shape[1], 8, 128), lambda i: (0, 0, 0, 0))
    one = lambda a: whole(a.shape)
    n_stat = lambda a: whole(a.shape)
    out_arrays = [
        shape((1, 128)), norm_params, bn_params, *weights, *weights, norm_params, bn_params, norm_params, bn_params,
        stat_wide, stat_head, stat_hidden, stat_kernel, shape((D, rows.shape[0]), BF16), shape((D, rows.shape[0])),
    ]
    far_out = (3, 4, 21, 23, 25, 26)
    in_arrays = [total_square, reduced, lng, gbn, *weights]
    wide = 4 * PADH
    return pl.pallas_call(
        update_kernel,
        grid=(1,),
        in_specs=[SMEM_SPEC] + [ANY_SPEC if i in (4, 5) else one(a) for i, a in enumerate(in_arrays)]
        + [corner(stat_wide), one(stat_head), corner(stat_hidden), one(stat_kernel)]
        + [one(a) for a in (norm_params, norm_second, bn_params, bn_second)] + [ANY_SPEC] * 2,
        out_specs=[ANY_SPEC if i in far_out else one(a) for i, a in enumerate(out_arrays)],
        out_shape=[shape(a.shape, a.dtype) for a in out_arrays],
        scratch_shapes=[
            pltpu.VMEM((8, D, D), F32), pltpu.VMEM((4, wide, wide), F32),
            pltpu.VMEM((4, D, D), F32), pltpu.VMEM((2, D, wide), F32),
            pltpu.VMEM(weights[0].shape, F32), pltpu.VMEM(weights[1].shape, F32),
            pltpu.VMEM(rows.shape, BF16), pltpu.VMEM(back.shape, F32),
        ] + [pltpu.VMEM(out_arrays[i].shape, out_arrays[i].dtype) for i in (3, 4, 21, 23, 25, 26)] + [
            pltpu.SemaphoreType.DMA((4,)), pltpu.SemaphoreType.DMA((6,)),
        ],
        compiler_params=PARAMS,
        name="update_part",
    )(step_count, *in_arrays, *stats, norm_params, norm_second, bn_params, bn_second, rows, back)


MESH = pl.DeviceIdType.MESH


def flip(index, bit):
    step = 2 ** bit
    return index + step - 2 * step * ((index // step) % 2)


def bits_of(count):
    bits = count.bit_length() - 1
    if 2 ** bits != count:
        raise ValueError("axis size")
    return bits


def greet_axes(counts):
    barrier = pltpu.get_barrier_semaphore()
    for axis, count in counts:
        me = lax.axis_index(axis)

        def signal(k, carry, axis=axis, count=count, me=me):
            pl.semaphore_signal(
                barrier, inc=1, device_id={axis: lax.rem(me + k, count)}, device_id_type=MESH
            )
            return carry

        lax.fori_loop(1, count, signal, 0)


def greeted(counts):
    pl.semaphore_wait(pltpu.get_barrier_semaphore(), sum(count - 1 for axis, count in counts))


def share_copy(axis, slots, sems, slot, peer, sent):
    return pltpu.make_async_remote_copy(
        src_ref=slots.at[slot], dst_ref=slots.at[slot], send_sem=sems[0].at[sent], recv_sem=sems[1].at[slot],
        device_id={axis: peer}, device_id_type=MESH,
    )


def share_start(axis, count, slots, sems):
    me = lax.axis_index(axis)

    def start(k, carry):
        peer = lax.rem(me + k, count)
        share_copy(axis, slots, sems, me, peer, peer).start()
        return carry

    lax.fori_loop(1, count, start, 0)


def share_finish(axis, count, slots, sems):
    me = lax.axis_index(axis)

    def finish(k, carry):
        peer = lax.rem(me + k, count)
        share_copy(axis, slots, sems, me, peer, peer).wait_send()
        share_copy(axis, slots, sems, peer, peer, peer).wait_recv()
        return carry

    lax.fori_loop(1, count, finish, 0)


def pool(slots, count):
    blank = jnp.zeros((1, 4 * PADH), F32)
    total = lax.fori_loop(0, count, lambda i, a: a + slots[i, 2:3, :], blank)
    mean = lax.fori_loop(0, count, lambda i, a: a + slots[i, 0:1, :] * slots[i, 2:3, :], blank) / total

    def power(i, a):
        off = slots[i, 0:1, :] - mean
        return a + slots[i, 1:2, :] + slots[i, 2:3, :] * off * off

    return mean, lax.fori_loop(0, count, power, blank), total


CHAINS = tuple((c, start, 256, 2) for c, start in ((0, 0), (0, 256), (1, 256), (1, 0), (2, 256), (2, 0)))
TAIL = (2, 5, 4, 0, 1, 5, 3, 0, 2, 1, 4, 5, 2, 3, 4, 5, 3, 4, 5)


def plan_of(dp_count, length, most):
    bits = bits_of(dp_count)
    radices = [2 ** (bits % most)] * (bits % most > 0) + [2**most] * (bits // most)
    plan, stride = [], 1
    for radix in radices:
        cut = length % (16 * radix) == 0
        length = length // radix if cut else length
        plan.append((stride, radix, cut, length))
        stride *= radix
    return plan


def landing_rows(dp_count):
    return sum(radix * piece for _, _, n, m in CHAINS for _, radix, _, piece in plan_of(dp_count, n, m))


def copy_count(dp_count):
    return sum(
        3 + sum((radix - 1) * (1 + cut) for _, radix, cut, _ in plan_of(dp_count, n, m)) for _, _, n, m in CHAINS
    )


def swish_slope(inner):
    sigma = sigmoid(inner)
    return sigma * (1.0 + inner * (1.0 - sigma))


HALVES = tuple(slice(i * 128, i * 128 + 128) for i in range(2))


def step_kernel(
    counts, names, lens_ref, np_ref, ai_ref, ao_ref, ci_ref, co_ref, dk_ref, bp_ref, fi_far, x_far, fo_far, cot_far,
    out_o, ig_o, red_o, lng_o, tot_o, gbn_o, *scratch,
):
    s = types.SimpleNamespace(**dict(zip(names, scratch)))
    dp_count = dict(counts)["dp"]
    shards = s.ffn1.shape[0]
    frames = x_far.shape[1]
    utts = frames // LEN
    t, d = lax.axis_index("tensor"), lax.axis_index("dp")
    near, far = flip(t, 0), flip(t, 1)
    last = flip(near, 1)
    wide = 4 * PADH

    def rows_of(u, size=LEN):
        return pl.ds(pl.multiple_of(u * size, size), size)

    def length_of(u):
        return lens_ref[t * utts + u]

    def each(body, start=0, stop=utts):
        def turn(u, carry):
            body(u)
            return carry

        lax.fori_loop(start, stop, turn, 0)

    greet_axes(counts)
    fi_ref, x_ref, fo_ref, cot_ref = held_in = (s.fi, s.x, s.fo, s.cot_in)
    fetches = [
        pltpu.make_async_copy(src, dst, s.fetch.at[i])
        for i, (src, dst) in enumerate(zip((fi_far, x_far, fo_far, cot_far), held_in))
    ]
    for fetch in fetches:
        fetch.start()

    own = pl.ds(pl.multiple_of(t * PADH, PADH), PADH)

    def mix_part(first, count):
        return lambda i: s.mix.at[pl.ds(first, count), pl.ds(pl.multiple_of(i * PADH, PADH), PADH), :]

    parts = (
        lambda i: s.small_parts.at[i],
        lambda i: s.ffn1.at[i],
        mix_part(0, 4),
        mix_part(4, 3),
        lambda i: s.ffn2.at[i],
    )

    def weight_copy(g, shard, peer, slot):
        return pltpu.make_async_remote_copy(
            src_ref=parts[g](shard), dst_ref=parts[g](shard), send_sem=s.gather_send.at[3 * g + slot],
            recv_sem=s.gather_recv.at[3 * g + slot], device_id={"tensor": peer}, device_id_type=MESH,
        )

    def launch(g):
        weight_copy(g, t, far, 0).start()
        weight_copy(g, t, near, 1).start()

    def relay(g):
        weight_copy(g, t, far, 0).wait()
        weight_copy(g, far, near, 2).start()

    def near_here(g):
        weight_copy(g, t, near, 1).wait()

    def last_here(g):
        weight_copy(g, far, near, 2).wait()

    def all_here(g):
        near_here(g)
        last_here(g)

    blank = jnp.zeros((PADH - HEAD, D), F32)
    pieces = [ai_ref[m] for m in range(3)] + [ao_ref[...]] + [ci_ref[:, m, :] for m in range(2)] + [co_ref[...]]
    for i, piece in enumerate(pieces):
        s.mix[i, own, :] = jnp.concatenate([piece, blank], axis=0).astype(BF16)
    s.small_parts[t] = jnp.zeros((24, 128), F32)
    s.small_parts[t, 0:KS, 0:HEAD] = dk_ref[...]
    s.small_parts[t, 16:18, 0:HEAD] = bp_ref[...]
    for fetch in fetches:
        fetch.wait()
    s.ffn1[t, 0] = fi_ref[0].astype(BF16)
    s.ffn1[t, 1] = fo_ref[0].astype(BF16)
    x0 = x_ref[...].astype(F32).T
    s.x1[...] = x0
    s.x0[...] = x0.astype(BF16)
    s.cot[...] = cot_ref[...].astype(F32).T.astype(BF16)
    greeted(counts)
    launch(1)
    launch(2)
    launch(0)
    launch(3)
    s.ffn2[t, 0] = fi_ref[1].astype(BF16)
    s.ffn2[t, 1] = fo_ref[1].astype(BF16)
    launch(4)
    for ref in (s.pad_f, s.pad_m, s.depth_grad, s.norm_grad, s.bn_grad):
        ref[...] = jnp.zeros_like(ref)

    def norm_one(u):
        rows = rows_of(u)
        x0 = s.x1[rows, :]
        s.n1[rows, :] = (standardize(x0)[0] * np_ref[0, 0:1, :] + np_ref[0, 1:2, :]).astype(BF16)

    each(norm_one)

    def feed_forward(shard):
        def body(u):
            rows = rows_of(u, 2 * LEN)
            inner = nn(s.n1[rows, :], s.ffn1[shard, 0])
            s.inner1[shard, rows, :] = inner
            active = (inner * sigmoid(inner)).astype(BF16)
            s.act1[shard, rows, :] = active
            s.x1[rows, :] += 0.5 * nn(active, s.ffn1[shard, 1])

        each(body, 0, utts // 2)

    feed_forward(t)
    near_here(1)
    feed_forward(near)
    relay(1)
    feed_forward(far)
    last_here(1)
    feed_forward(last)
    for g in (2, 0, 3):
        relay(g)
    for g in (2, 0, 3):
        all_here(g)
    for i in range(2):
        s.small[:, 128 * i : 128 * i + PADH] = s.small_parts[2 * i, :, 0:PADH]
        s.small[:, 128 * i + PADH : 128 * i + 128] = s.small_parts[2 * i + 1, :, 0:PADH]

    masks = lane_masks(BF16)

    def mix_forward(u):
        rows = rows_of(u)
        length = length_of(u)
        x1 = s.x1[rows, :]
        n2 = (standardize(x1)[0] * np_ref[1, 0:1, :] + np_ref[1, 1:2, :]).astype(BF16)
        s.n2[rows, :] = n2
        for i, ref in enumerate((s.q, s.k, s.v)):
            ref[rows, :] = nt(n2, s.mix[i]).astype(BF16)
        key_ok = lax.broadcasted_iota(jnp.int32, (1, LEN), 1) < length
        for half, lanes in enumerate(HALVES):
            q, k, v = s.q[rows, lanes], s.k[rows, lanes], s.v[rows, lanes]
            mixture = jnp.zeros((LEN, 128), F32)
            for side in range(2):
                scores = nt(q * masks[side], k) * HEAD ** (-0.5)
                scores = jnp.where(key_ok, scores, NEG_FILL)
                exps = jnp.exp(scores - jnp.max(scores, axis=-1, keepdims=True))
                probs = exps * (1.0 / jnp.sum(exps, axis=-1, keepdims=True))
                s.probs[u, 2 * half + side] = probs
                mixture = mixture + nn(probs.astype(BF16), v * masks[side])
            s.mixture[rows, lanes] = mixture.astype(BF16)
        x2 = x1 + nn(s.mixture[rows, :], s.mix[3])
        s.x2[rows, :] = x2
        n3 = (standardize(x2)[0] * np_ref[2, 0:1, :] + np_ref[2, 1:2, :]).astype(BF16)
        s.n3[rows, :] = n3
        value = nt(n3, s.mix[4])
        gate = nt(n3, s.mix[5])
        s.value[rows, :] = value
        s.gate[rows, :] = gate
        mask = row_mask(length)
        gated = value * sigmoid(gate) * mask
        count = length.astype(F32)
        for half, lanes in enumerate(HALVES):
            s.pad_f[half, 8 : 8 + LEN, :] = gated[:, lanes]
            running = jnp.zeros((LEN, 128), F32)
            for j in range(KS):
                running = running + s.pad_f[half, 1 + j : 1 + j + LEN, :] * s.small[j : j + 1, lanes]
            s.mid[rows, lanes] = running
            mean = jnp.sum(running * mask, axis=0, keepdims=True) / count
            centred = (running - mean) * mask
            s.stat[u, 0:1, lanes] = mean
            s.stat[u, 1:2, lanes] = jnp.sum(centred * centred, axis=0, keepdims=True)
            s.stat[u, 2:3, lanes] = jnp.full((1, 128), count, F32)

    each(mix_forward)

    held = pool(s.stat, utts)
    for axis, count in counts:
        slots = getattr(s, "moment_" + axis)
        sems = [getattr(s, "moment_" + axis + side) for side in ("_send", "_recv")]
        me = lax.axis_index(axis)
        slots[me] = jnp.concatenate([*held, jnp.zeros((5, wide), F32)], axis=0)
        share_start(axis, count, slots, sems)
        if axis == "dp":
            relay(4)
            near_here(4)
        share_finish(axis, count, slots, sems)
        held = pool(slots, count)
    last_here(4)
    mean, power, total = held
    inv_std = lax.rsqrt(power / total + 1e-05)
    inv_count = 1.0 / total
    s.bn[0:1, :] = mean
    s.bn[1:2, :] = inv_std
    s.bn[2:4, :] = s.small[16:18, :]
    s.bn[6:7, :] = inv_count

    def middle(u):
        rows = rows_of(u)
        mask = row_mask(length_of(u))
        mean, inv_std, gain, bias = [s.bn[i : i + 1, :] for i in range(4)]
        xhat = (s.mid[rows, :] - mean) * inv_std
        normal = xhat * gain + bias
        sigma = sigmoid(normal)
        act3 = (normal * sigma * mask).astype(BF16)
        s.act3[rows, :] = act3
        x3 = s.x2[rows, :] + nn(act3, s.mix[6])
        n4 = (standardize(x3)[0] * np_ref[3, 0:1, :] + np_ref[3, 1:2, :]).astype(BF16)
        s.n4[rows, :] = n4
        total = jnp.zeros((LEN, D), F32)
        for i in range(shards):
            inner = nn(n4, s.ffn2[i, 0])
            s.inner2[i] = inner
            active = (inner * sigmoid(inner)).astype(BF16)
            s.act2[i, rows, :] = active
            total = total + nn(active, s.ffn2[i, 1])
        x4 = x3 + 0.5 * total
        out_o[rows, :] = (standardize(x4)[0] * np_ref[4, 0:1, :] + np_ref[4, 1:2, :]).astype(BF16)
        d4, gain4, bias4 = norm_back(x4, np_ref[4, 0:1, :], s.cot[rows, :].astype(F32))
        g2 = (0.5 * d4).astype(BF16)
        s.g2[rows, :] = g2
        d_n4 = jnp.zeros((LEN, D), F32)
        for i in range(shards):
            d_inner = (nt(g2, s.ffn2[i, 1]) * swish_slope(s.inner2[i])).astype(BF16)
            s.din[i, rows, :] = d_inner
            d_n4 = d_n4 + nt(d_inner, s.ffn2[i, 0])
        d3, gain3, bias3 = norm_back(x3, np_ref[3, 0:1, :], d_n4)
        d3 = d3 + d4
        s.d3[rows, :] = d3
        gc = d3.astype(BF16)
        s.gc[rows, :] = gc
        d_normal = nt(gc, s.mix[6]) * mask * (sigma * (1.0 + normal * (1.0 - sigma)))
        s.d_normal[rows, :] = d_normal
        for i, part in enumerate((gain3, bias3, gain4, bias4)):
            s.norm_grad[6 + i : 7 + i, :] += part
        s.bn_grad[0:1, :] += jnp.sum(d_normal * xhat, axis=0, keepdims=True)
        s.bn_grad[1:2, :] += jnp.sum(d_normal, axis=0, keepdims=True)

    each(middle)

    sem_ids = itertools.count()

    def move(src, dst, peer):
        i = next(sem_ids)
        return pltpu.make_async_remote_copy(
            src_ref=src, dst_ref=dst, send_sem=s.reduce_send.at[i], recv_sem=s.reduce_recv.at[i],
            device_id=peer, device_id_type=MESH,
        )

    def add(target, other):
        return (target.astype(F32) + other.astype(F32)).astype(BF16)

    landing = [0]
    squares = []

    def square_of(a):
        a = a.astype(F32)
        return total_of(a * a)

    def chain(c, start, length, most):
        window = pl.ds(start, length)
        flights = [
            move(s.chunk.at[c, last, window], s.near.at[c, 1, window], {"tensor": near}),
            move(s.chunk.at[c, near, window], s.near.at[c, 0, window], {"tensor": near}),
        ]
        for flight in flights:
            flight.start()
        yield True
        flights[0].wait()
        s.acc[c, 1, window] = add(s.chunk[c, far, window], s.near[c, 1, window])
        flight = move(s.acc.at[c, 1, window], s.far.at[c, window], {"tensor": far})
        flight.start()
        flights[1].wait()
        yield True
        flight.wait()
        pair = s.chunk[c, t, window].astype(F32) + s.near[c, 0, window].astype(F32)
        s.acc[c, 0, window] = (pair + s.far[c, window].astype(F32)).astype(BF16)
        offset, size, trail, copies = start, length, [], 1
        for stride, radix, cut, piece in plan_of(dp_count, length, most):
            digit = (d // stride) % radix
            base = landing[0]
            landing[0] += radix * piece

            def slot(i):
                return pl.ds(pl.multiple_of(base + i * piece, 16), piece)

            def part(i):
                return pl.ds(pl.multiple_of(offset + i * piece if cut else offset, 16), piece)

            flights = []
            for k in range(1, radix):
                other = (digit + k) % radix
                peer = {"dp": d + (other - digit) * stride}
                flights.append(move(s.acc.at[c, 0, part(other)], s.land.at[slot(digit)], peer))
                flights[-1].start()
            s.land[slot(digit)] = s.acc[c, 0, part(digit)]
            yield True
            for flight in flights:
                flight.wait()
            total = s.land[slot(0)].astype(F32)
            for i in range(1, radix):
                total = total + s.land[slot(i)].astype(F32)
            s.acc[c, 0, part(digit)] = total.astype(BF16)
            if cut:
                trail.append((stride, radix, offset))
                offset, size = offset + digit * piece, piece
            else:
                copies *= radix
        here = pl.ds(pl.multiple_of(offset, 16), size)
        red_o[c, here] = s.acc[c, 0, here]
        squares.append(square_of(s.acc[c, 0, here]) * (1.0 / copies))
        for stride, radix, before in trail[::-1]:
            digit = (d // stride) % radix
            here = pl.ds(pl.multiple_of(offset, 16), size)
            flights = []
            for k in range(1, radix):
                peer = {"dp": d + ((digit + k) % radix - digit) * stride}
                flights.append(move(red_o.at[c, here], red_o.at[c, here], peer))
                flights[-1].start()
            yield True
            for flight in flights:
                flight.wait()
            offset, size = before, size * radix

    live = {}

    def begin(i):
        live[i] = chain(*CHAINS[i])
        next(live[i])

    def pump(*chosen):
        for i in chosen or tuple(live):
            if i in live and next(live[i], None) is None:
                del live[i]

    def spread_rows(c, first, left, right):
        full = tn(left, right).astype(BF16)
        for i in range(shards):
            s.chunk[c, i, first : first + PADH, :] = full[PADH * i : PADH * (i + 1), :]

    totals = ("total_dp", "total_tensor")
    count_of = dict(counts)

    def sems_of(name):
        return [getattr(s, name + side) for side in ("_send", "_recv")]

    s.total_dp[d] = s.bn_grad[...]
    share_start("dp", dp_count, s.total_dp, sems_of("total_dp"))
    for c in (0, 2):
        for i in range(shards):
            for first in (0, 256):
                s.chunk[c, i, first + D : first + 256, :] = jnp.zeros((256 - D, D), BF16)
    for i in range(shards):
        s.chunk[0, i, 0:D, :] = tn(s.n4[...], s.din[i]).astype(BF16)
    begin(0)
    share_finish("dp", dp_count, s.total_dp, sems_of("total_dp"))
    s.total_tensor[t] = lax.fori_loop(1, dp_count, lambda i, a: a + s.total_dp[i], s.total_dp[0])
    share_start("tensor", shards, s.total_tensor, sems_of("total_tensor"))
    for i in range(shards):
        s.chunk[0, i, 256 : 256 + D, :] = tn(s.g2[...], s.act2[i]).astype(BF16)
    begin(1)
    spread_rows(1, 3 * PADH, s.act3[...], s.gc[...])
    share_finish("tensor", shards, s.total_tensor, sems_of("total_tensor"))
    bn_sums = lax.fori_loop(1, shards, lambda i, a: a + s.total_tensor[i], s.total_tensor[0])
    s.bn[4:6, :] = bn_sums[0:2, :]

    def conv_back(u):
        rows = rows_of(u)
        mask = row_mask(length_of(u))
        mean, inv_std, gain, bias, sum_gain, sum_bias, inv_count = [s.bn[i : i + 1, :] for i in range(7)]
        xhat = (s.mid[rows, :] - mean) * inv_std
        d_mid = inv_std * gain * (s.d_normal[rows, :] - mask * ((sum_bias + xhat * sum_gain) * inv_count))
        value = s.value[rows, :]
        sigma = sigmoid(s.gate[rows, :])
        gated = value * sigma * mask
        for half, lanes in enumerate(HALVES):
            s.pad_f[half, 8 : 8 + LEN, :] = gated[:, lanes]
            s.pad_m[half, 8 : 8 + LEN, :] = d_mid[:, lanes]
            d_gated = jnp.zeros((LEN, 128), F32)
            mid_half = d_mid[:, lanes]
            for j in range(KS):
                d_gated = d_gated + s.pad_m[half, 15 - j : 15 - j + LEN, :] * s.small[j : j + 1, lanes]
                s.depth_grad[j : j + 1, lanes] += jnp.sum(
                    s.pad_f[half, 1 + j : 1 + j + LEN, :] * mid_half, axis=0, keepdims=True
                )
            d_gated = d_gated * mask
            sig = sigma[:, lanes]
            s.d_value[rows, lanes] = (d_gated * sig).astype(BF16)
            s.d_gate[rows, lanes] = (d_gated * value[:, lanes] * sig * (1.0 - sig)).astype(BF16)
        d_n3 = nn(s.d_value[rows, :], s.mix[4]) + nn(s.d_gate[rows, :], s.mix[5])
        d2, gain2, bias2 = norm_back(s.x2[rows, :], np_ref[2, 0:1, :], d_n3)
        d2 = d2 + s.d3[rows, :]
        s.d2[rows, :] = d2
        s.ga[rows, :] = d2.astype(BF16)
        for i, part in enumerate((gain2, bias2)):
            s.norm_grad[4 + i : 5 + i, :] += part

    each(conv_back)
    pump(0, 1)
    eye = (
        lax.broadcasted_iota(jnp.int32, (16, D), 0) == lax.broadcasted_iota(jnp.int32, (16, D), 1)
    ).astype(BF16)
    spread_rows(1, 4 * PADH, s.d_value[...], s.n3[...])
    spread_rows(1, 5 * PADH, s.d_gate[...], s.n3[...])
    spread_rows(1, 6 * PADH, s.mixture[...], s.ga[...])
    spread_rows(1, 7 * PADH, s.depth_grad[...].astype(BF16), eye)
    begin(2)

    def attend_back(u):
        rows = rows_of(u)
        d_mix = nt(s.ga[rows, :], s.mix[3]).astype(BF16)
        for half, lanes in enumerate(HALVES):
            q, k, v, dm = s.q[rows, lanes], s.k[rows, lanes], s.v[rows, lanes], d_mix[:, lanes]
            dq = jnp.zeros((LEN, 128), F32)
            dk = jnp.zeros((LEN, 128), F32)
            dv = jnp.zeros((LEN, 128), F32)
            for side in range(2):
                probs = s.probs[u, 2 * half + side]
                dm_side = dm * masks[side]
                d_probs = nt(dm_side, v)
                dv = dv + tn(probs.astype(BF16), dm_side)
                row_sum = jnp.sum(probs * d_probs, axis=-1, keepdims=True)
                d_scores = (probs * (d_probs - row_sum)).astype(BF16)
                dq = dq + nn(d_scores, k * masks[side])
                dk = dk + tn(d_scores, q * masks[side])
            s.dq[rows, lanes] = (dq * HEAD ** (-0.5)).astype(BF16)
            s.dk[rows, lanes] = (dk * HEAD ** (-0.5)).astype(BF16)
            s.dv[rows, lanes] = dv.astype(BF16)
        d_n2 = nn(s.dq[rows, :], s.mix[0]) + nn(s.dk[rows, :], s.mix[1]) + nn(s.dv[rows, :], s.mix[2])
        d1, gain1, bias1 = norm_back(s.x1[rows, :], np_ref[1, 0:1, :], d_n2)
        d1 = d1 + s.d2[rows, :]
        s.d1[rows, :] = d1
        s.g1[rows, :] = (0.5 * d1).astype(BF16)
        s.d_n1[rows, :] = jnp.zeros((LEN, D), F32)
        for i, part in enumerate((gain1, bias1)):
            s.norm_grad[2 + i : 3 + i, :] += part

    each(attend_back, 0, utts // 2)
    pump(2)
    each(attend_back, utts // 2, utts)
    pump(0)
    spread_rows(1, 0, s.dq[...], s.n2[...])
    spread_rows(1, PADH, s.dk[...], s.n2[...])
    spread_rows(1, 2 * PADH, s.dv[...], s.n2[...])
    begin(3)
    pump(1)
    for i in range(shards):
        s.chunk[2, i, 256 : 256 + D, :] = tn(s.g1[...], s.act1[i]).astype(BF16)
    begin(4)
    pump(3)

    for place, shard in enumerate((last, near, far, t)):
        def feed_back(u):
            rows = rows_of(u, 2 * LEN)
            d_inner = (nt(s.g1[rows, :], s.ffn1[shard, 1]) * swish_slope(s.inner1[shard, rows, :])).astype(BF16)
            s.din1[place, rows, :] = d_inner
            s.d_n1[rows, :] += nt(d_inner, s.ffn1[shard, 0])

        each(feed_back, 0, utts // 2)
        s.chunk[2, shard, 0:D, :] = tn(s.n1[...], s.din1[place]).astype(BF16)
        if place == 0:
            pump(0, 2, 4, 1)
        if place == 1:
            begin(5)
        if place == 2:
            pump(3, 2, 5, 0)
        if place == 3:
            pump(4, 1)

    def norm_zero(u):
        rows = rows_of(u)
        d0, gain0, bias0 = norm_back(s.x0[rows, :].astype(F32), np_ref[0, 0:1, :], s.d_n1[rows, :])
        ig_o[rows, :] = s.d1[rows, :] + d0
        for i, part in enumerate((gain0, bias0)):
            s.norm_grad[i : i + 1, :] += part

    each(norm_zero)
    s.norm_dp[d] = s.norm_grad[...]
    share_start("dp", dp_count, s.norm_dp, sems_of("norm_dp"))
    pump(3)
    own_block = lax.broadcasted_iota(jnp.int32, (1, wide), 1) // PADH == t
    gb = s.bn[4:6, :]
    gbn_o[...] = jnp.zeros_like(gbn_o)
    for i in range(4):
        @pl.when(t == i)
        def _():
            gbn_o[0:2, 0:PADH] = gb[:, i * PADH : (i + 1) * PADH]

    for i in TAIL[:4]:
        pump(i)
    share_finish("dp", dp_count, s.norm_dp, sems_of("norm_dp"))
    s.norm_tensor[t] = lax.fori_loop(1, dp_count, lambda i, a: a + s.norm_dp[i], s.norm_dp[0])
    share_start("tensor", shards, s.norm_tensor, sems_of("norm_tensor"))
    for i in TAIL[4:8]:
        pump(i)
    share_finish("tensor", shards, s.norm_tensor, sems_of("norm_tensor"))
    norm_sums = lax.fori_loop(1, shards, lambda i, a: a + s.norm_tensor[i], s.norm_tensor[0])
    lng_o[...] = norm_sums
    rest = list(TAIL[8:])
    while len(squares) < len(CHAINS):
        pump(*([rest.pop(0)] if rest else []))
    square = functools.reduce(lambda a, b: a + b, squares)
    square = square + total_of(jnp.where(own_block, gb * gb, 0.0)) * (1.0 / dp_count)
    s.square_dp[d] = jnp.broadcast_to(square, (8, 128))
    share_start("dp", dp_count, s.square_dp, sems_of("square_dp"))
    for i in rest[:-1]:
        pump(i)
    share_finish("dp", dp_count, s.square_dp, sems_of("square_dp"))
    s.square_tensor[t] = lax.fori_loop(1, dp_count, lambda i, a: a + s.square_dp[i], s.square_dp[0])
    share_start("tensor", shards, s.square_tensor, sems_of("square_tensor"))
    while live:
        pump()
    share_finish("tensor", shards, s.square_tensor, sems_of("square_tensor"))
    square = lax.fori_loop(1, shards, lambda i, a: a + s.square_tensor[i], s.square_tensor[0])
    tot_o[...] = square + jnp.broadcast_to(square_of(norm_sums), (8, 128))


def step_call(lengths, x, cot, norm_params, ffn_in, ffn_out, attn_in, attn_out, conv_in, conv_out, depth_kernel, bn_params):
    counts = tuple((axis, lax.axis_size(axis)) for axis in ("dp", "tensor"))
    dp_count, shards = counts[0][1], counts[1][1]
    frames = x.shape[1]
    utts = frames // LEN
    wide = 4 * PADH
    low = lambda *dims: pltpu.VMEM(dims, BF16)
    full = lambda *dims: pltpu.VMEM(dims, F32)
    copies = copy_count(dp_count)
    scratch = {
        "ffn1": low(shards, 2, D, D), "ffn2": low(shards, 2, D, D), "mix": low(7, wide, D),
        "small_parts": full(shards, 24, 128), "small": full(24, wide),
        "x1": full(frames, D), "x2": full(frames, D), "d1": full(frames, D), "d2": full(frames, D),
        "d3": full(frames, D), "d_n1": full(frames, D),
        "fi": full(*ffn_in.shape), "fo": full(*ffn_out.shape), "x": low(D, frames), "cot_in": low(D, frames),
        "fetch": pltpu.SemaphoreType.DMA((4,)),
        "x0": low(frames, D), "cot": low(frames, D),
        "n1": low(frames, D), "n2": low(frames, D), "n3": low(frames, D), "n4": low(frames, D),
        "inner1": full(shards, frames, D), "act1": low(shards, frames, D), "din1": low(shards, frames, D),
        "inner2": full(shards, LEN, D), "act2": low(shards, frames, D), "din": low(shards, frames, D),
        "q": low(frames, wide), "k": low(frames, wide), "v": low(frames, wide), "mixture": low(frames, wide),
        "dq": low(frames, wide), "dk": low(frames, wide), "dv": low(frames, wide),
        "d_value": low(frames, wide), "d_gate": low(frames, wide), "act3": low(frames, wide),
        "probs": full(utts, 4, LEN, LEN), "value": full(frames, wide), "gate": full(frames, wide),
        "mid": full(frames, wide), "d_normal": full(frames, wide),
        "g1": low(frames, D), "g2": low(frames, D), "ga": low(frames, D), "gc": low(frames, D),
        "pad_f": full(2, LEN + 16, 128), "pad_m": full(2, LEN + 16, 128), "stat": full(utts, 8, wide),
        "bn": full(8, wide), "depth_grad": full(16, wide), "norm_grad": full(16, D), "bn_grad": full(8, wide),
        "chunk": low(3, shards, 512, D), "near": low(3, 2, 512, D), "acc": low(3, 2, 512, D), "far": low(3, 512, D),
        "land": low(landing_rows(dp_count), D),
        "gather_send": pltpu.SemaphoreType.DMA((15,)), "gather_recv": pltpu.SemaphoreType.DMA((15,)),
        "reduce_send": pltpu.SemaphoreType.DMA((copies,)), "reduce_recv": pltpu.SemaphoreType.DMA((copies,)),
    }
    for name, rows, width in (("moment", 8, wide), ("total", 8, wide), ("norm", 16, D), ("square", 8, 128)):
        for axis, count in counts:
            scratch[name + "_" + axis] = full(count, rows, width)
            for side in ("_send", "_recv"):
                scratch[name + "_" + axis + side] = pltpu.SemaphoreType.DMA((count,))
    return pl.pallas_call(
        functools.partial(step_kernel, counts, tuple(scratch)),
        in_specs=[SMEM_SPEC] + [VMEM_SPEC] * 7 + [ANY_SPEC] * 4,
        out_specs=[VMEM_SPEC] * 6,
        out_shape=[
            shape((frames, D), BF16), shape((frames, D)), shape((3, 512, D), BF16), shape((16, D)), shape((8, 128)),
            shape((8, 128)),
        ],
        scratch_shapes=list(scratch.values()),
        compiler_params=pltpu.CompilerParams(collective_id=0, has_side_effects=True, vmem_limit_bytes=VMEM_CAP),
        name="step_part",
    )(lengths, norm_params, attn_in, attn_out, conv_in, conv_out, depth_kernel, bn_params, ffn_in, x, ffn_out, cot)


def local(
    block_input, lengths, cotangent, norm_params, bn_params, ffn_in, ffn_out, attn_in, attn_out, conv_in,
    depth_kernel, conv_out, stat_wide, stat_head, stat_hidden, stat_kernel, norm_second, bn_second, step_count,
):
    attn_in, conv_in = attn_in.swapaxes(1, 2), conv_in.transpose(2, 0, 1)
    stat_head, stat_kernel = stat_head.swapaxes(1, 2), stat_kernel.swapaxes(0, 1)
    block_out, input_grad, reduced, lng, total_square, gbn = step_call(
        lengths, block_input.T, cotangent.T, norm_params, ffn_in, ffn_out, attn_in, attn_out, conv_in, conv_out,
        depth_kernel, bn_params,
    )
    weights = (ffn_in, ffn_out, attn_in, attn_out, conv_in, depth_kernel, conv_out)
    outs = list(
        update_call(
            step_count, total_square, reduced, lng, gbn, weights, (stat_wide, stat_head, stat_hidden, stat_kernel),
            norm_params, norm_second, bn_params, bn_second, block_out, input_grad,
        )
    )
    for i in (5, 12):
        outs[i] = outs[i].swapaxes(1, 2)
    for i in (7, 14):
        outs[i] = outs[i].transpose(1, 2, 0)
    outs[22] = outs[22].swapaxes(1, 2)
    outs[24] = outs[24].swapaxes(0, 1)
    return (outs[25].T, outs[26].T, outs[0][0, :1], *outs[1:25])


def solution(mesh):
    weights_specs = (
        P(None, None, "tensor"), P(None, "tensor", None), P(None, None, "tensor"), P("tensor", None),
        P(None, None, "tensor"), P(None, "tensor"), P("tensor", None),
    )
    stat_specs = (
        P("tensor", None, None, None), P("tensor", None, None, None), P("tensor", None, None, None),
        P("tensor", None, None),
    )
    frames = P(("dp", "tensor"), None)
    channels = P(None, "tensor")
    return jax.shard_map(
        local,
        mesh=mesh,
        in_specs=(frames, P("dp"), frames, P(), channels, *weights_specs, *stat_specs, P(), channels, P()),
        out_specs=(
            frames, frames, P(), P(), channels, *weights_specs, *weights_specs, P(), channels, P(), channels,
            *stat_specs,
        ),
        check_vma=False,
    )
```

```python
import functools
import itertools
import math
import types

import jax
import jax.numpy as jnp
from jax import lax
from jax.experimental import pallas as pl
from jax.experimental.pallas import tpu as pltpu
from jax.sharding import PartitionSpec as P

D = 240
KS = 15
LEN = 192
HEAD = 60
PADH = 64
ROOT_ITERS = 8
NPARAM = 1331280
PEAK_RATE = 2.0
WARM_STEPS = 4.0
SMALL_RATE = 0.3
GRAFT_SCALE = 0.6
NEG_FILL = -1000000000.0
VMEM_CAP = 60 * 1024 * 1024

F32 = jnp.float32
BF16 = jnp.bfloat16


def nn(a, b):
    return lax.dot_general(a, b, (((1,), (0,)), ((), ())), preferred_element_type=F32)


def nt(a, b):
    return lax.dot_general(a, b, (((1,), (1,)), ((), ())), preferred_element_type=F32)


def tn(a, b):
    return lax.dot_general(a, b, (((0,), (0,)), ((), ())), preferred_element_type=F32)


def sigmoid(v):
    return 0.5 * jnp.tanh(0.5 * v) + 0.5


def standardize(h):
    centred = h - jnp.sum(h, axis=-1, keepdims=True) * (1.0 / D)
    spread = jnp.sum(centred * centred, axis=-1, keepdims=True) * (1.0 / D)
    inv = lax.rsqrt(spread + 1e-05)
    return centred * inv, inv


def norm_back(h, gain, dy):
    xhat, inv = standardize(h)
    scaled = dy * gain
    mean_a = jnp.sum(scaled, axis=-1, keepdims=True) * (1.0 / D)
    mean_b = jnp.sum(scaled * xhat, axis=-1, keepdims=True) * (1.0 / D)
    dh = inv * (scaled - mean_a - xhat * mean_b)
    return dh, jnp.sum(dy * xhat, axis=0, keepdims=True), jnp.sum(dy, axis=0, keepdims=True)


def row_mask(length):
    return (lax.broadcasted_iota(jnp.int32, (LEN, 1), 0) < length).astype(F32)


def lane_masks(dtype):
    lane = lax.broadcasted_iota(jnp.int32, (1, 128), 1)
    return ((lane < PADH).astype(dtype), (lane >= PADH).astype(dtype))


def split(a):
    high = a.astype(BF16)
    return high, (a - high.astype(F32)).astype(BF16)


def stacked(lefts, right):
    full = nn(jnp.concatenate(lefts, axis=0), right)
    places, at = [], 0
    for left in lefts:
        places.append(full[at : at + left.shape[0]])
        at += left.shape[0]
    return places


def mul_fine(a, b, rider=None):
    high, cross, *rest = stacked([*a] + ([] if rider is None else [rider]), b[0])
    return (high + (nn(a[0], b[1]) + cross), *rest)


def eye_of(n):
    return (lax.broadcasted_iota(jnp.int32, (n, n), 0) == lax.broadcasted_iota(jnp.int32, (n, n), 1)).astype(F32)


def next_power(own, direction, fine):
    rider = direction.astype(BF16)
    if fine:
        parts = split(own)
        square, moved = mul_fine(parts, parts, rider)
        step = 0.0625 * square - 0.625 * own
        halves = split(step)
        once = mul_fine(halves, parts)[0]
        twice = nn(halves[0], once.astype(BF16))
    else:
        low = own.astype(BF16)
        square, moved = stacked([low, rider], low)
        step = (0.0625 * square - 0.625 * own).astype(BF16)
        once = nn(step, low)
        twice = nn(step, once.astype(BF16))
    return 2.44140625 * own + 3.125 * once + twice, 1.25 * direction - 0.25 * moved


def total_of(a):
    return jnp.sum(jnp.sum(a, axis=1, keepdims=True), axis=0, keepdims=True)


def update_kernel(
    step_ref, tot_ref, red_ref, lng_ref, gbn_ref, fi_far, fo_far, ai_ref, ao_ref, ci_ref, dk_ref, co_ref,
    sw_ref, sh_ref, sd_ref, sk_ref, np_ref, ns_ref, bp_ref, bs_ref, rows_far, back_far,
    gn_o, cn_o, cb_o, cfi_far, cfo_far, cai_o, cao_o, cci_o, cdk_o, cco_o,
    nfi_o, nfo_o, nai_o, nao_o, nci_o, ndk_o, nco_o, nn_o, nb_o, nns_o, nbs_o,
    nsw_far, nsh_o, nsd_far, nsk_o, turned_far, back_o,
    mat_f, mat_b, dir_f, dir_b, fi_ref, fo_ref, rows_sc, back_sc, cfi_o, cfo_o, nsw_o, nsd_o, turned_sc, turned_back,
    in_sem, out_sem,
):
    fetches = [
        pltpu.make_async_copy(src, dst, in_sem.at[i])
        for i, (src, dst) in enumerate(
            ((rows_far, rows_sc), (back_far, back_sc), (fi_far, fi_ref), (fo_far, fo_ref))
        )
    ]
    for fetch in fetches:
        fetch.start()
    stores = [
        pltpu.make_async_copy(src, dst, out_sem.at[i])
        for i, (src, dst) in enumerate(
            (
                (nsw_o, nsw_far), (nsd_o, nsd_far), (cfi_o, cfi_far), (cfo_o, cfo_far), (turned_sc, turned_far),
                (turned_back, back_o),
            )
        )
    ]
    steps = jnp.full((1, 1), step_ref[0], jnp.int32).astype(F32)
    rate = PEAK_RATE * jnp.minimum(steps / WARM_STEPS, jnp.sqrt(WARM_STEPS / steps))
    grad_norm = jnp.sqrt(tot_ref[0:1, 0:1])
    threshold = math.sqrt(NPARAM)
    factor = threshold / jnp.maximum(grad_norm, threshold)
    square_factor = factor * factor
    gn_o[...] = jnp.broadcast_to(grad_norm, gn_o.shape)

    c_norm = lng_ref[...] * factor
    for i in range(5):
        clipped = c_norm[2 * i : 2 * i + 2, :]
        second = 0.5 * ns_ref[i] + 0.5 * clipped * clipped
        cn_o[i] = clipped
        nns_o[i] = second
        nn_o[i] = np_ref[i] - rate * SMALL_RATE * clipped * lax.rsqrt(second)
    c_bn = gbn_ref[0:2, 0:HEAD] * factor
    second = 0.5 * bs_ref[...] + 0.5 * c_bn * c_bn
    cb_o[...] = c_bn
    nbs_o[...] = second
    nb_o[...] = bp_ref[...] - rate * SMALL_RATE * c_bn * lax.rsqrt(second)

    eye_d = eye_of(D)
    scales_f = []
    for i in range(4):
        member, is_out = i // 2, i % 2
        chunk = (2, 0)[member]
        start = is_out * 256
        low = red_ref[chunk, start : start + D, :]
        wide_c = sw_ref[0, 2 * is_out + member, 0:1, 0:1]
        hidden_c = sd_ref[0, 2 * is_out + member, 0:1, 0:1]
        gram = tn(low, low) * square_factor
        wide = nt(low, low) * square_factor
        nsw_o[0, 2 * is_out + member] = 0.5 * wide_c * eye_d + 0.5 * wide
        nsd_o[0, 2 * is_out + member] = 0.5 * hidden_c * eye_d + 0.5 * gram
        clipped = low.astype(F32) * factor
        if is_out:
            cfo_o[member] = clipped.T
        else:
            cfi_o[member] = clipped
        dir_f[i] = clipped
        trace = total_of(clipped * clipped)
        power = total_of(gram * gram)
        scale = 1.0
        for k, c in enumerate((wide_c, hidden_c)):
            zoom = 2.5 * lax.rsqrt(0.25 * c * c * D + 0.5 * c * trace + 0.25 * power)
            mat_f[2 * i + k] = zoom * (0.5 * c * eye_d + 0.5 * gram)
            scale = scale * jnp.sqrt(jnp.sqrt(zoom))
        scales_f.append(scale)

    eye_b = eye_of(4 * PADH)
    row_block = lax.broadcasted_iota(jnp.int32, (4 * PADH, 1), 0) // PADH
    lane_block = lax.broadcasted_iota(jnp.int32, (1, 4 * PADH), 1) // PADH
    same_block = row_block == lane_block
    wide_of = (4, 5, 6, 10, 8, 9, 7, None)
    head_of = (0, 1, 2, 7, 4, 5, 3, 6)
    scales_b = []

    def spread(values):
        column = jnp.zeros((4 * PADH, 1), F32)
        for i, value in enumerate(values):
            column = jnp.where(row_block == i, value, column)
        return column

    for group in range(2):
        low = red_ref[1, group * 4 * PADH : (group + 1) * 4 * PADH, :]
        clipped = low.astype(F32) * factor
        dir_b[group] = clipped.T
        gram = jnp.where(same_block, nt(low, low), 0.0) * square_factor
        row_trace = jnp.sum(clipped * clipped, axis=1, keepdims=True)
        row_power = jnp.sum(gram * gram, axis=1, keepdims=True)
        wide_cs, head_cs, traces, powers, dims = [], [], [], [], []
        for i in range(4):
            index = group * 4 + i
            part = slice(i * PADH, (i + 1) * PADH)
            piece = low[part, :]
            head_c = sh_ref[0, 0, head_of[index] : head_of[index] + 1, 0:1]
            own_gram = nt(piece, piece)[:HEAD, :HEAD] * square_factor
            nsh_o[0, :, head_of[index], :] = 0.5 * head_c * eye_d[:HEAD, :HEAD] + 0.5 * own_gram
            wide = tn(piece, piece) * square_factor
            if wide_of[index] is None:
                wide_c = sk_ref[0, 0:1, 0:1]
                nsk_o[:, 0, :] = 0.5 * wide_c * eye_d[:KS, :KS] + 0.5 * wide[:KS, :KS]
                dims.append(KS)
            else:
                wide_c = sw_ref[0, wide_of[index], 0:1, 0:1]
                nsw_o[0, wide_of[index]] = 0.5 * wide_c * eye_d + 0.5 * wide
                dims.append(D)
            wide_cs.append(wide_c)
            head_cs.append(head_c)
            traces.append(jnp.sum(row_trace[part], axis=0, keepdims=True))
            powers.append(jnp.sum(row_power[part], axis=0, keepdims=True))
        scale = [1.0] * 4
        for k, (cs, sizes) in enumerate(((wide_cs, dims), (head_cs, [HEAD] * 4))):
            zooms = [
                2.5 * lax.rsqrt(0.25 * c * c * n + 0.5 * c * trace + 0.25 * power)
                for c, n, trace, power in zip(cs, sizes, traces, powers)
            ]
            mat_b[2 * group + k] = spread(zooms) * (0.5 * spread(cs) * eye_b + 0.5 * gram)
            scale = [s * jnp.sqrt(jnp.sqrt(zoom)) for s, zoom in zip(scale, zooms)]
        scales_b.append(scale)

    def advance(fine):
        for k in range(2):
            for mats, dirs, count in ((mat_f, dir_f, 4), (mat_b, dir_b, 2)):
                for i in range(count):
                    mats[2 * i + k], dirs[i] = next_power(mats[2 * i + k], dirs[i], fine)

    def coarse_step(i, carry):
        advance(False)
        if width < frames:
            turn(i)
        return carry

    for store in stores[:4]:
        store.start()
    advance(True)
    for fetch in fetches:
        fetch.wait()
    frames = rows_sc.shape[0]
    steps = ROOT_ITERS - 2
    width = frames // steps if frames % (128 * steps) == 0 else frames

    def turn(i):
        here = pl.ds(pl.multiple_of(i * width, width), width)
        turned_sc[:, here] = rows_sc[here, :].astype(F32).T.astype(BF16)
        turned_back[:, here] = back_sc[here, :].T

    if width == frames:
        turn(0)
    lax.fori_loop(0, steps, coarse_step, 0)
    for store in stores[4:]:
        store.start()
    for k in range(2):
        for mats, dirs, count in ((mat_f, dir_f, 4), (mat_b, dir_b, 2)):
            for i in range(count):
                moved = nn(dirs[i].astype(BF16), mats[2 * i + k].astype(BF16))
                dirs[i] = 1.25 * dirs[i] - 0.25 * moved

    def graft(weight, direction):
        size = jnp.sqrt(total_of(weight * weight))
        return rate * GRAFT_SCALE * size / (jnp.sqrt(total_of(direction * direction)) + 1e-06)

    for i in range(4):
        member, is_out = i // 2, i % 2
        direction = dir_f[i] * scales_f[i]
        weight = (fi_ref, fo_ref)[is_out][member]
        if is_out:
            direction = direction.T
        (nfi_o, nfo_o)[is_out][member] = weight - graft(weight, direction) * direction
    turned_b = [dir_b[group].T for group in range(2)]
    for index in range(8):
        group, i = index // 4, index % 4
        part = slice(i * PADH, i * PADH + HEAD)
        direction = turned_b[group][part, :] * scales_b[group][i]
        clipped = red_ref[1, index * PADH : (index + 1) * PADH, :][:HEAD, :].astype(F32) * factor
        if index in (3, 6):
            weight_ref, clip_o, new_o = ((co_ref, cco_o, nco_o), None, None, (ao_ref, cao_o, nao_o))[index - 3]
            clip_o[...] = clipped
            new_o[...] = weight_ref[...] - graft(weight_ref[...], direction) * direction
        elif index == 7:
            turned = direction.T[:KS, :]
            cdk_o[...] = clipped.T[:KS, :]
            ndk_o[...] = dk_ref[...] - graft(dk_ref[...], turned) * turned
        else:
            weight_ref, clip_o, new_o = (ai_ref, cai_o, nai_o) if index < 3 else (ci_ref, cci_o, nci_o)
            at = (index,) if index < 3 else (slice(None), index - 4)
            weight = weight_ref[at]
            clip_o[at] = clipped
            new_o[at] = weight - graft(weight, direction) * direction
    for store in stores:
        store.wait()


def shape(dims, dtype=F32):
    return jax.ShapeDtypeStruct(dims, dtype)


def whole(dims):
    zeros = (0,) * len(dims)
    return pl.BlockSpec(dims, lambda u: zeros)


SMEM_SPEC = pl.BlockSpec(memory_space=pltpu.SMEM)
VMEM_SPEC = pl.BlockSpec(memory_space=pltpu.VMEM)
ANY_SPEC = pl.BlockSpec(memory_space=pl.ANY)
PARAMS = pltpu.CompilerParams(vmem_limit_bytes=VMEM_CAP)


def update_call(step_count, total_square, reduced, lng, gbn, weights, stats, norm_params, norm_second, bn_params, bn_second, rows, back):
    stat_wide, stat_head, stat_hidden, stat_kernel = stats
    corner = lambda a: pl.BlockSpec((1, a.shape[1], 8, 128), lambda i: (0, 0, 0, 0))
    one = lambda a: whole(a.shape)
    n_stat = lambda a: whole(a.shape)
    out_arrays = [
        shape((1, 128)), norm_params, bn_params, *weights, *weights, norm_params, bn_params, norm_params, bn_params,
        stat_wide, stat_head, stat_hidden, stat_kernel, shape((D, rows.shape[0]), BF16), shape((D, rows.shape[0])),
    ]
    far_out = (3, 4, 21, 23, 25, 26)
    in_arrays = [total_square, reduced, lng, gbn, *weights]
    wide = 4 * PADH
    return pl.pallas_call(
        update_kernel,
        grid=(1,),
        in_specs=[SMEM_SPEC] + [ANY_SPEC if i in (4, 5) else one(a) for i, a in enumerate(in_arrays)]
        + [corner(stat_wide), one(stat_head), corner(stat_hidden), one(stat_kernel)]
        + [one(a) for a in (norm_params, norm_second, bn_params, bn_second)] + [ANY_SPEC] * 2,
        out_specs=[ANY_SPEC if i in far_out else one(a) for i, a in enumerate(out_arrays)],
        out_shape=[shape(a.shape, a.dtype) for a in out_arrays],
        scratch_shapes=[
            pltpu.VMEM((8, D, D), F32), pltpu.VMEM((4, wide, wide), F32),
            pltpu.VMEM((4, D, D), F32), pltpu.VMEM((2, D, wide), F32),
            pltpu.VMEM(weights[0].shape, F32), pltpu.VMEM(weights[1].shape, F32),
            pltpu.VMEM(rows.shape, BF16), pltpu.VMEM(back.shape, F32),
        ] + [pltpu.VMEM(out_arrays[i].shape, out_arrays[i].dtype) for i in (3, 4, 21, 23, 25, 26)] + [
            pltpu.SemaphoreType.DMA((4,)), pltpu.SemaphoreType.DMA((6,)),
        ],
        compiler_params=PARAMS,
        name="update_part",
    )(step_count, *in_arrays, *stats, norm_params, norm_second, bn_params, bn_second, rows, back)


MESH = pl.DeviceIdType.MESH


def flip(index, bit):
    step = 2 ** bit
    return index + step - 2 * step * ((index // step) % 2)


def bits_of(count):
    bits = count.bit_length() - 1
    if 2 ** bits != count:
        raise ValueError("axis size")
    return bits


def greet_axes(counts):
    barrier = pltpu.get_barrier_semaphore()
    for axis, count in counts:
        me = lax.axis_index(axis)

        def signal(k, carry, axis=axis, count=count, me=me):
            pl.semaphore_signal(
                barrier, inc=1, device_id={axis: lax.rem(me + k, count)}, device_id_type=MESH
            )
            return carry

        lax.fori_loop(1, count, signal, 0)


def greeted(counts):
    pl.semaphore_wait(pltpu.get_barrier_semaphore(), sum(count - 1 for axis, count in counts))


def share_copy(axis, slots, sems, slot, peer, sent):
    return pltpu.make_async_remote_copy(
        src_ref=slots.at[slot], dst_ref=slots.at[slot], send_sem=sems[0].at[sent], recv_sem=sems[1].at[slot],
        device_id={axis: peer}, device_id_type=MESH,
    )


def share_start(axis, count, slots, sems):
    me = lax.axis_index(axis)

    def start(k, carry):
        peer = lax.rem(me + k, count)
        share_copy(axis, slots, sems, me, peer, peer).start()
        return carry

    lax.fori_loop(1, count, start, 0)


def share_finish(axis, count, slots, sems):
    me = lax.axis_index(axis)

    def finish(k, carry):
        peer = lax.rem(me + k, count)
        share_copy(axis, slots, sems, me, peer, peer).wait_send()
        share_copy(axis, slots, sems, peer, peer, peer).wait_recv()
        return carry

    lax.fori_loop(1, count, finish, 0)


def pool(slots, count):
    blank = jnp.zeros((1, 4 * PADH), F32)
    total = lax.fori_loop(0, count, lambda i, a: a + slots[i, 2:3, :], blank)
    mean = lax.fori_loop(0, count, lambda i, a: a + slots[i, 0:1, :] * slots[i, 2:3, :], blank) / total

    def power(i, a):
        off = slots[i, 0:1, :] - mean
        return a + slots[i, 1:2, :] + slots[i, 2:3, :] * off * off

    return mean, lax.fori_loop(0, count, power, blank), total


CHAINS = tuple((c, start, 256, 2) for c, start in ((0, 0), (0, 256), (1, 256), (1, 0), (2, 256), (2, 0)))
TAIL = (2, 5, 4, 0, 1, 5, 3, 0, 2, 1, 4, 5, 2, 3, 4, 5, 3, 4, 5)


def plan_of(dp_count, length, most):
    bits = bits_of(dp_count)
    radices = [2 ** (bits % most)] * (bits % most > 0) + [2**most] * (bits // most)
    plan, stride = [], 1
    for radix in radices:
        cut = length % (16 * radix) == 0
        length = length // radix if cut else length
        plan.append((stride, radix, cut, length))
        stride *= radix
    return plan


def landing_rows(dp_count):
    return sum(radix * piece for _, _, n, m in CHAINS for _, radix, _, piece in plan_of(dp_count, n, m))


def copy_count(dp_count):
    return sum(
        3 + sum((radix - 1) * (1 + cut) for _, radix, cut, _ in plan_of(dp_count, n, m)) for _, _, n, m in CHAINS
    )


def turn(a):
    return a.astype(F32).T.astype(BF16)


def swish_slope(inner):
    sigma = sigmoid(inner)
    return sigma * (1.0 + inner * (1.0 - sigma))


HALVES = tuple(slice(i * 128, i * 128 + 128) for i in range(2))


def step_kernel(
    counts, names, lens_ref, np_ref, ai_ref, ao_ref, ci_ref, co_ref, dk_ref, bp_ref, fi_far, x_far, fo_far, cot_far,
    out_o, ig_o, red_o, lng_o, tot_o, gbn_o, *scratch,
):
    s = types.SimpleNamespace(**dict(zip(names, scratch)))
    dp_count = dict(counts)["dp"]
    shards = s.ffn1.shape[0]
    frames = x_far.shape[1]
    utts = frames // LEN
    t, d = lax.axis_index("tensor"), lax.axis_index("dp")
    near, far = flip(t, 0), flip(t, 1)
    last = flip(near, 1)
    wide = 4 * PADH

    def rows_of(u, size=LEN):
        return pl.ds(pl.multiple_of(u * size, size), size)

    def length_of(u):
        return lens_ref[t * utts + u]

    def each(body, start=0, stop=utts):
        def turn(u, carry):
            body(u)
            return carry

        lax.fori_loop(start, stop, turn, 0)

    greet_axes(counts)
    fi_ref, x_ref, fo_ref, cot_ref = held_in = (s.fi, s.x, s.fo, s.cot_in)
    fetches = [
        pltpu.make_async_copy(src, dst, s.fetch.at[i])
        for i, (src, dst) in enumerate(zip((fi_far, x_far, fo_far, cot_far), held_in))
    ]
    for fetch in fetches:
        fetch.start()

    own = pl.ds(pl.multiple_of(t * PADH, PADH), PADH)

    def mix_part(first, count):
        return lambda i: s.mix.at[pl.ds(first, count), pl.ds(pl.multiple_of(i * PADH, PADH), PADH), :]

    parts = (
        lambda i: s.small_parts.at[i],
        lambda i: s.ffn1.at[i],
        mix_part(0, 4),
        mix_part(4, 3),
        lambda i: s.ffn2.at[i],
    )

    def weight_copy(g, shard, peer, slot):
        return pltpu.make_async_remote_copy(
            src_ref=parts[g](shard), dst_ref=parts[g](shard), send_sem=s.gather_send.at[3 * g + slot],
            recv_sem=s.gather_recv.at[3 * g + slot], device_id={"tensor": peer}, device_id_type=MESH,
        )

    def launch(g):
        weight_copy(g, t, far, 0).start()
        weight_copy(g, t, near, 1).start()

    def relay(g):
        weight_copy(g, t, far, 0).wait()
        weight_copy(g, far, near, 2).start()

    def near_here(g):
        weight_copy(g, t, near, 1).wait()

    def last_here(g):
        weight_copy(g, far, near, 2).wait()

    def all_here(g):
        near_here(g)
        last_here(g)

    blank = jnp.zeros((PADH - HEAD, D), F32)
    pieces = [ai_ref[m] for m in range(3)] + [ao_ref[...]] + [ci_ref[:, m, :] for m in range(2)] + [co_ref[...]]
    for i, piece in enumerate(pieces):
        s.mix[i, own, :] = jnp.concatenate([piece, blank], axis=0).astype(BF16)
    s.small_parts[t] = jnp.zeros((24, 128), F32)
    s.small_parts[t, 0:KS, 0:HEAD] = dk_ref[...]
    s.small_parts[t, 16:18, 0:HEAD] = bp_ref[...]
    for fetch in fetches:
        fetch.wait()
    s.ffn1[t, 0] = fi_ref[0].astype(BF16)
    s.ffn1[t, 1] = fo_ref[0].astype(BF16)
    x0 = x_ref[...].astype(F32).T
    s.x1[...] = x0
    s.x0[...] = x0.astype(BF16)
    s.cot[...] = cot_ref[...].astype(F32).T.astype(BF16)
    greeted(counts)
    launch(1)
    launch(2)
    launch(0)
    launch(3)
    s.ffn2[t, 0] = fi_ref[1].astype(BF16)
    s.ffn2[t, 1] = fo_ref[1].astype(BF16)
    launch(4)
    for ref in (s.pad_f, s.pad_m, s.depth_grad, s.norm_grad, s.bn_grad):
        ref[...] = jnp.zeros_like(ref)

    def norm_one(u):
        rows = rows_of(u)
        x0 = s.x1[rows, :]
        s.n1[rows, :] = (standardize(x0)[0] * np_ref[0, 0:1, :] + np_ref[0, 1:2, :]).astype(BF16)

    each(norm_one)
    s.n1_turned[...] = turn(s.n1[...])

    def feed_forward(shard):
        def body(u):
            rows = rows_of(u, 2 * LEN)
            inner = nn(s.n1[rows, :], s.ffn1[shard, 0])
            s.inner1[shard, rows, :] = inner
            active = (inner * sigmoid(inner)).astype(BF16)
            s.act1[shard, rows, :] = active
            s.x1[rows, :] += 0.5 * nn(active, s.ffn1[shard, 1])

        each(body, 0, utts // 2)

    feed_forward(t)
    near_here(1)
    feed_forward(near)
    relay(1)
    feed_forward(far)
    last_here(1)
    feed_forward(last)
    for g in (2, 0, 3):
        relay(g)
    for g in (2, 0, 3):
        all_here(g)
    for i in range(2):
        s.small[:, 128 * i : 128 * i + PADH] = s.small_parts[2 * i, :, 0:PADH]
        s.small[:, 128 * i + PADH : 128 * i + 128] = s.small_parts[2 * i + 1, :, 0:PADH]

    masks = lane_masks(BF16)

    def mix_forward(u):
        rows = rows_of(u)
        length = length_of(u)
        x1 = s.x1[rows, :]
        n2 = (standardize(x1)[0] * np_ref[1, 0:1, :] + np_ref[1, 1:2, :]).astype(BF16)
        s.n2[rows, :] = n2
        for i, ref in enumerate((s.q, s.k, s.v)):
            ref[rows, :] = nt(n2, s.mix[i]).astype(BF16)
        key_ok = lax.broadcasted_iota(jnp.int32, (1, LEN), 1) < length
        for half, lanes in enumerate(HALVES):
            q, k, v = s.q[rows, lanes], s.k[rows, lanes], s.v[rows, lanes]
            mixture = jnp.zeros((LEN, 128), F32)
            for side in range(2):
                scores = nt(q * masks[side], k) * HEAD ** (-0.5)
                scores = jnp.where(key_ok, scores, NEG_FILL)
                exps = jnp.exp(scores - jnp.max(scores, axis=-1, keepdims=True))
                probs = exps * (1.0 / jnp.sum(exps, axis=-1, keepdims=True))
                s.probs[u, 2 * half + side] = probs
                mixture = mixture + nn(probs.astype(BF16), v * masks[side])
            s.mixture[rows, lanes] = mixture.astype(BF16)
        x2 = x1 + nn(s.mixture[rows, :], s.mix[3])
        s.x2[rows, :] = x2
        n3 = (standardize(x2)[0] * np_ref[2, 0:1, :] + np_ref[2, 1:2, :]).astype(BF16)
        s.n3[rows, :] = n3
        value = nt(n3, s.mix[4])
        gate = nt(n3, s.mix[5])
        s.value[rows, :] = value
        s.gate[rows, :] = gate
        mask = row_mask(length)
        gated = value * sigmoid(gate) * mask
        count = length.astype(F32)
        for half, lanes in enumerate(HALVES):
            s.pad_f[half, 8 : 8 + LEN, :] = gated[:, lanes]
            running = jnp.zeros((LEN, 128), F32)
            for j in range(KS):
                running = running + s.pad_f[half, 1 + j : 1 + j + LEN, :] * s.small[j : j + 1, lanes]
            s.mid[rows, lanes] = running
            mean = jnp.sum(running * mask, axis=0, keepdims=True) / count
            centred = (running - mean) * mask
            s.stat[u, 0:1, lanes] = mean
            s.stat[u, 1:2, lanes] = jnp.sum(centred * centred, axis=0, keepdims=True)
            s.stat[u, 2:3, lanes] = jnp.full((1, 128), count, F32)

    each(mix_forward)

    held = pool(s.stat, utts)
    for axis, count in counts:
        slots = getattr(s, "moment_" + axis)
        sems = [getattr(s, "moment_" + axis + side) for side in ("_send", "_recv")]
        me = lax.axis_index(axis)
        slots[me] = jnp.concatenate([*held, jnp.zeros((5, wide), F32)], axis=0)
        share_start(axis, count, slots, sems)
        if axis == "dp":
            relay(4)
            near_here(4)
        share_finish(axis, count, slots, sems)
        held = pool(slots, count)
    last_here(4)
    mean, power, total = held
    inv_std = lax.rsqrt(power / total + 1e-05)
    inv_count = 1.0 / total
    s.bn[0:1, :] = mean
    s.bn[1:2, :] = inv_std
    s.bn[2:4, :] = s.small[16:18, :]
    s.bn[6:7, :] = inv_count

    def middle(u):
        rows = rows_of(u)
        mask = row_mask(length_of(u))
        mean, inv_std, gain, bias = [s.bn[i : i + 1, :] for i in range(4)]
        xhat = (s.mid[rows, :] - mean) * inv_std
        normal = xhat * gain + bias
        sigma = sigmoid(normal)
        act3 = (normal * sigma * mask).astype(BF16)
        s.act3[rows, :] = act3
        x3 = s.x2[rows, :] + nn(act3, s.mix[6])
        n4 = (standardize(x3)[0] * np_ref[3, 0:1, :] + np_ref[3, 1:2, :]).astype(BF16)
        s.n4[rows, :] = n4
        total = jnp.zeros((LEN, D), F32)
        for i in range(shards):
            inner = nn(n4, s.ffn2[i, 0])
            s.inner2[i] = inner
            active = (inner * sigmoid(inner)).astype(BF16)
            s.act2[i, rows, :] = active
            total = total + nn(active, s.ffn2[i, 1])
        x4 = x3 + 0.5 * total
        out_o[rows, :] = (standardize(x4)[0] * np_ref[4, 0:1, :] + np_ref[4, 1:2, :]).astype(BF16)
        d4, gain4, bias4 = norm_back(x4, np_ref[4, 0:1, :], s.cot[rows, :].astype(F32))
        g2 = (0.5 * d4).astype(BF16)
        s.g2[rows, :] = g2
        d_n4 = jnp.zeros((LEN, D), F32)
        for i in range(shards):
            d_inner = (nt(g2, s.ffn2[i, 1]) * swish_slope(s.inner2[i])).astype(BF16)
            s.din[i, rows, :] = d_inner
            d_n4 = d_n4 + nt(d_inner, s.ffn2[i, 0])
        d3, gain3, bias3 = norm_back(x3, np_ref[3, 0:1, :], d_n4)
        d3 = d3 + d4
        s.d3[rows, :] = d3
        gc = d3.astype(BF16)
        s.gc[rows, :] = gc
        d_normal = nt(gc, s.mix[6]) * mask * (sigma * (1.0 + normal * (1.0 - sigma)))
        s.d_normal[rows, :] = d_normal
        for i, part in enumerate((gain3, bias3, gain4, bias4)):
            s.norm_grad[6 + i : 7 + i, :] += part
        s.bn_grad[0:1, :] += jnp.sum(d_normal * xhat, axis=0, keepdims=True)
        s.bn_grad[1:2, :] += jnp.sum(d_normal, axis=0, keepdims=True)

    each(middle)

    sem_ids = itertools.count()

    def move(src, dst, peer):
        i = next(sem_ids)
        return pltpu.make_async_remote_copy(
            src_ref=src, dst_ref=dst, send_sem=s.reduce_send.at[i], recv_sem=s.reduce_recv.at[i],
            device_id=peer, device_id_type=MESH,
        )

    def add(target, other):
        return (target.astype(F32) + other.astype(F32)).astype(BF16)

    landing = [0]
    squares = []

    def square_of(a):
        a = a.astype(F32)
        return total_of(a * a)

    def chain(c, start, length, most):
        window = pl.ds(start, length)
        flights = [
            move(s.chunk.at[c, last, window], s.near.at[c, 1, window], {"tensor": near}),
            move(s.chunk.at[c, near, window], s.near.at[c, 0, window], {"tensor": near}),
        ]
        for flight in flights:
            flight.start()
        yield True
        flights[0].wait()
        s.acc[c, 1, window] = add(s.chunk[c, far, window], s.near[c, 1, window])
        flight = move(s.acc.at[c, 1, window], s.far.at[c, window], {"tensor": far})
        flight.start()
        flights[1].wait()
        yield True
        flight.wait()
        pair = s.chunk[c, t, window].astype(F32) + s.near[c, 0, window].astype(F32)
        s.acc[c, 0, window] = (pair + s.far[c, window].astype(F32)).astype(BF16)
        offset, size, trail, copies = start, length, [], 1
        for stride, radix, cut, piece in plan_of(dp_count, length, most):
            digit = (d // stride) % radix
            base = landing[0]
            landing[0] += radix * piece

            def slot(i):
                return pl.ds(pl.multiple_of(base + i * piece, 16), piece)

            def part(i):
                return pl.ds(pl.multiple_of(offset + i * piece if cut else offset, 16), piece)

            flights = []
            for k in range(1, radix):
                other = (digit + k) % radix
                peer = {"dp": d + (other - digit) * stride}
                flights.append(move(s.acc.at[c, 0, part(other)], s.land.at[slot(digit)], peer))
                flights[-1].start()
            s.land[slot(digit)] = s.acc[c, 0, part(digit)]
            yield True
            for flight in flights:
                flight.wait()
            total = s.land[slot(0)].astype(F32)
            for i in range(1, radix):
                total = total + s.land[slot(i)].astype(F32)
            s.acc[c, 0, part(digit)] = total.astype(BF16)
            if cut:
                trail.append((stride, radix, offset))
                offset, size = offset + digit * piece, piece
            else:
                copies *= radix
        here = pl.ds(pl.multiple_of(offset, 16), size)
        red_o[c, here] = s.acc[c, 0, here]
        squares.append(square_of(s.acc[c, 0, here]) * (1.0 / copies))
        for stride, radix, before in trail[::-1]:
            digit = (d // stride) % radix
            here = pl.ds(pl.multiple_of(offset, 16), size)
            flights = []
            for k in range(1, radix):
                peer = {"dp": d + ((digit + k) % radix - digit) * stride}
                flights.append(move(red_o.at[c, here], red_o.at[c, here], peer))
                flights[-1].start()
            yield True
            for flight in flights:
                flight.wait()
            offset, size = before, size * radix

    live = {}

    def begin(i):
        live[i] = chain(*CHAINS[i])
        next(live[i])

    def pump(*chosen):
        for i in chosen or tuple(live):
            if i in live and next(live[i], None) is None:
                del live[i]

    def spread_rows(c, first, left, right):
        full = tn(left, right).astype(BF16)
        for i in range(shards):
            s.chunk[c, i, first : first + PADH, :] = full[PADH * i : PADH * (i + 1), :]

    totals = ("total_dp", "total_tensor")
    count_of = dict(counts)

    def sems_of(name):
        return [getattr(s, name + side) for side in ("_send", "_recv")]

    s.total_dp[d] = s.bn_grad[...]
    share_start("dp", dp_count, s.total_dp, sems_of("total_dp"))
    for c in (0, 2):
        for i in range(shards):
            for first in (0, 256):
                s.chunk[c, i, first + D : first + 256, :] = jnp.zeros((256 - D, D), BF16)
    turned = turn(s.n4[...])
    for i in range(shards):
        s.chunk[0, i, 0:D, :] = nn(turned, s.din[i]).astype(BF16)
    begin(0)
    share_finish("dp", dp_count, s.total_dp, sems_of("total_dp"))
    s.total_tensor[t] = lax.fori_loop(1, dp_count, lambda i, a: a + s.total_dp[i], s.total_dp[0])
    share_start("tensor", shards, s.total_tensor, sems_of("total_tensor"))
    turned = turn(s.g2[...])
    for i in range(shards):
        s.chunk[0, i, 256 : 256 + D, :] = nn(turned, s.act2[i]).astype(BF16)
    begin(1)
    spread_rows(1, 3 * PADH, s.act3[...], s.gc[...])
    share_finish("tensor", shards, s.total_tensor, sems_of("total_tensor"))
    bn_sums = lax.fori_loop(1, shards, lambda i, a: a + s.total_tensor[i], s.total_tensor[0])
    s.bn[4:6, :] = bn_sums[0:2, :]

    def conv_back(u):
        rows = rows_of(u)
        mask = row_mask(length_of(u))
        mean, inv_std, gain, bias, sum_gain, sum_bias, inv_count = [s.bn[i : i + 1, :] for i in range(7)]
        xhat = (s.mid[rows, :] - mean) * inv_std
        d_mid = inv_std * gain * (s.d_normal[rows, :] - mask * ((sum_bias + xhat * sum_gain) * inv_count))
        value = s.value[rows, :]
        sigma = sigmoid(s.gate[rows, :])
        gated = value * sigma * mask
        for half, lanes in enumerate(HALVES):
            s.pad_f[half, 8 : 8 + LEN, :] = gated[:, lanes]
            s.pad_m[half, 8 : 8 + LEN, :] = d_mid[:, lanes]
            d_gated = jnp.zeros((LEN, 128), F32)
            mid_half = d_mid[:, lanes]
            for j in range(KS):
                d_gated = d_gated + s.pad_m[half, 15 - j : 15 - j + LEN, :] * s.small[j : j + 1, lanes]
                s.depth_grad[j : j + 1, lanes] += jnp.sum(
                    s.pad_f[half, 1 + j : 1 + j + LEN, :] * mid_half, axis=0, keepdims=True
                )
            d_gated = d_gated * mask
            sig = sigma[:, lanes]
            s.d_value[rows, lanes] = (d_gated * sig).astype(BF16)
            s.d_gate[rows, lanes] = (d_gated * value[:, lanes] * sig * (1.0 - sig)).astype(BF16)
        d_n3 = nn(s.d_value[rows, :], s.mix[4]) + nn(s.d_gate[rows, :], s.mix[5])
        d2, gain2, bias2 = norm_back(s.x2[rows, :], np_ref[2, 0:1, :], d_n3)
        d2 = d2 + s.d3[rows, :]
        s.d2[rows, :] = d2
        s.ga[rows, :] = d2.astype(BF16)
        for i, part in enumerate((gain2, bias2)):
            s.norm_grad[4 + i : 5 + i, :] += part

    each(conv_back)
    pump(0, 1)
    eye = (
        lax.broadcasted_iota(jnp.int32, (16, D), 0) == lax.broadcasted_iota(jnp.int32, (16, D), 1)
    ).astype(BF16)
    spread_rows(1, 4 * PADH, s.d_value[...], s.n3[...])
    spread_rows(1, 5 * PADH, s.d_gate[...], s.n3[...])
    spread_rows(1, 6 * PADH, s.mixture[...], s.ga[...])
    spread_rows(1, 7 * PADH, s.depth_grad[...].astype(BF16), eye)
    begin(2)

    def attend_back(u):
        rows = rows_of(u)
        d_mix = nt(s.ga[rows, :], s.mix[3]).astype(BF16)
        for half, lanes in enumerate(HALVES):
            q, k, v, dm = s.q[rows, lanes], s.k[rows, lanes], s.v[rows, lanes], d_mix[:, lanes]
            dq = jnp.zeros((LEN, 128), F32)
            dk = jnp.zeros((LEN, 128), F32)
            dv = jnp.zeros((LEN, 128), F32)
            for side in range(2):
                probs = s.probs[u, 2 * half + side]
                dm_side = dm * masks[side]
                d_probs = nt(dm_side, v)
                dv = dv + tn(probs.astype(BF16), dm_side)
                row_sum = jnp.sum(probs * d_probs, axis=-1, keepdims=True)
                d_scores = (probs * (d_probs - row_sum)).astype(BF16)
                dq = dq + nn(d_scores, k * masks[side])
                dk = dk + tn(d_scores, q * masks[side])
            s.dq[rows, lanes] = (dq * HEAD ** (-0.5)).astype(BF16)
            s.dk[rows, lanes] = (dk * HEAD ** (-0.5)).astype(BF16)
            s.dv[rows, lanes] = dv.astype(BF16)
        d_n2 = nn(s.dq[rows, :], s.mix[0]) + nn(s.dk[rows, :], s.mix[1]) + nn(s.dv[rows, :], s.mix[2])
        d1, gain1, bias1 = norm_back(s.x1[rows, :], np_ref[1, 0:1, :], d_n2)
        d1 = d1 + s.d2[rows, :]
        s.d1[rows, :] = d1
        s.g1[rows, :] = (0.5 * d1).astype(BF16)
        s.d_n1[rows, :] = jnp.zeros((LEN, D), F32)
        for i, part in enumerate((gain1, bias1)):
            s.norm_grad[2 + i : 3 + i, :] += part

    each(attend_back, 0, utts // 2)
    pump(2)
    each(attend_back, utts // 2, utts)
    pump(0)
    spread_rows(1, 0, s.dq[...], s.n2[...])
    spread_rows(1, PADH, s.dk[...], s.n2[...])
    spread_rows(1, 2 * PADH, s.dv[...], s.n2[...])
    begin(3)
    pump(1)
    turned = turn(s.g1[...])
    for i in range(shards):
        s.chunk[2, i, 256 : 256 + D, :] = nn(turned, s.act1[i]).astype(BF16)
    begin(4)
    pump(3)

    for place, shard in enumerate((last, near, far, t)):
        def feed_back(u):
            rows = rows_of(u, 2 * LEN)
            d_inner = (nt(s.g1[rows, :], s.ffn1[shard, 1]) * swish_slope(s.inner1[shard, rows, :])).astype(BF16)
            s.din1[place, rows, :] = d_inner
            s.d_n1[rows, :] += nt(d_inner, s.ffn1[shard, 0])

        each(feed_back, 0, utts // 2)
        s.chunk[2, shard, 0:D, :] = nn(s.n1_turned[...], s.din1[place]).astype(BF16)
        if place == 0:
            pump(0, 2, 4, 1)
        if place == 1:
            begin(5)
        if place == 2:
            pump(3, 2, 5, 0)
        if place == 3:
            pump(4, 1)

    def norm_zero(u):
        rows = rows_of(u)
        d0, gain0, bias0 = norm_back(s.x0[rows, :].astype(F32), np_ref[0, 0:1, :], s.d_n1[rows, :])
        ig_o[rows, :] = s.d1[rows, :] + d0
        for i, part in enumerate((gain0, bias0)):
            s.norm_grad[i : i + 1, :] += part

    each(norm_zero)
    s.norm_dp[d] = s.norm_grad[...]
    share_start("dp", dp_count, s.norm_dp, sems_of("norm_dp"))
    pump(3)
    own_block = lax.broadcasted_iota(jnp.int32, (1, wide), 1) // PADH == t
    gb = s.bn[4:6, :]
    gbn_o[...] = jnp.zeros_like(gbn_o)
    for i in range(4):
        @pl.when(t == i)
        def _():
            gbn_o[0:2, 0:PADH] = gb[:, i * PADH : (i + 1) * PADH]

    for i in TAIL[:4]:
        pump(i)
    share_finish("dp", dp_count, s.norm_dp, sems_of("norm_dp"))
    s.norm_tensor[t] = lax.fori_loop(1, dp_count, lambda i, a: a + s.norm_dp[i], s.norm_dp[0])
    share_start("tensor", shards, s.norm_tensor, sems_of("norm_tensor"))
    for i in TAIL[4:8]:
        pump(i)
    share_finish("tensor", shards, s.norm_tensor, sems_of("norm_tensor"))
    norm_sums = lax.fori_loop(1, shards, lambda i, a: a + s.norm_tensor[i], s.norm_tensor[0])
    lng_o[...] = norm_sums
    rest = list(TAIL[8:])
    while len(squares) < len(CHAINS):
        pump(*([rest.pop(0)] if rest else []))
    square = functools.reduce(lambda a, b: a + b, squares)
    square = square + total_of(jnp.where(own_block, gb * gb, 0.0)) * (1.0 / dp_count)
    s.square_dp[d] = jnp.broadcast_to(square, (8, 128))
    share_start("dp", dp_count, s.square_dp, sems_of("square_dp"))
    for i in rest[:-1]:
        pump(i)
    share_finish("dp", dp_count, s.square_dp, sems_of("square_dp"))
    s.square_tensor[t] = lax.fori_loop(1, dp_count, lambda i, a: a + s.square_dp[i], s.square_dp[0])
    share_start("tensor", shards, s.square_tensor, sems_of("square_tensor"))
    while live:
        pump()
    share_finish("tensor", shards, s.square_tensor, sems_of("square_tensor"))
    square = lax.fori_loop(1, shards, lambda i, a: a + s.square_tensor[i], s.square_tensor[0])
    tot_o[...] = square + jnp.broadcast_to(square_of(norm_sums), (8, 128))


def step_call(lengths, x, cot, norm_params, ffn_in, ffn_out, attn_in, attn_out, conv_in, conv_out, depth_kernel, bn_params):
    counts = tuple((axis, lax.axis_size(axis)) for axis in ("dp", "tensor"))
    dp_count, shards = counts[0][1], counts[1][1]
    frames = x.shape[1]
    utts = frames // LEN
    wide = 4 * PADH
    low = lambda *dims: pltpu.VMEM(dims, BF16)
    full = lambda *dims: pltpu.VMEM(dims, F32)
    copies = copy_count(dp_count)
    scratch = {
        "ffn1": low(shards, 2, D, D), "ffn2": low(shards, 2, D, D), "mix": low(7, wide, D),
        "small_parts": full(shards, 24, 128), "small": full(24, wide),
        "x1": full(frames, D), "x2": full(frames, D), "d1": full(frames, D), "d2": full(frames, D),
        "d3": full(frames, D), "d_n1": full(frames, D),
        "fi": full(*ffn_in.shape), "fo": full(*ffn_out.shape), "x": low(D, frames), "cot_in": low(D, frames),
        "fetch": pltpu.SemaphoreType.DMA((4,)),
        "n1_turned": low(D, frames), "x0": low(frames, D), "cot": low(frames, D),
        "n1": low(frames, D), "n2": low(frames, D), "n3": low(frames, D), "n4": low(frames, D),
        "inner1": full(shards, frames, D), "act1": low(shards, frames, D), "din1": low(shards, frames, D),
        "inner2": full(shards, LEN, D), "act2": low(shards, frames, D), "din": low(shards, frames, D),
        "q": low(frames, wide), "k": low(frames, wide), "v": low(frames, wide), "mixture": low(frames, wide),
        "dq": low(frames, wide), "dk": low(frames, wide), "dv": low(frames, wide),
        "d_value": low(frames, wide), "d_gate": low(frames, wide), "act3": low(frames, wide),
        "probs": full(utts, 4, LEN, LEN), "value": full(frames, wide), "gate": full(frames, wide),
        "mid": full(frames, wide), "d_normal": full(frames, wide),
        "g1": low(frames, D), "g2": low(frames, D), "ga": low(frames, D), "gc": low(frames, D),
        "pad_f": full(2, LEN + 16, 128), "pad_m": full(2, LEN + 16, 128), "stat": full(utts, 8, wide),
        "bn": full(8, wide), "depth_grad": full(16, wide), "norm_grad": full(16, D), "bn_grad": full(8, wide),
        "chunk": low(3, shards, 512, D), "near": low(3, 2, 512, D), "acc": low(3, 2, 512, D), "far": low(3, 512, D),
        "land": low(landing_rows(dp_count), D),
        "gather_send": pltpu.SemaphoreType.DMA((15,)), "gather_recv": pltpu.SemaphoreType.DMA((15,)),
        "reduce_send": pltpu.SemaphoreType.DMA((copies,)), "reduce_recv": pltpu.SemaphoreType.DMA((copies,)),
    }
    for name, rows, width in (("moment", 8, wide), ("total", 8, wide), ("norm", 16, D), ("square", 8, 128)):
        for axis, count in counts:
            scratch[name + "_" + axis] = full(count, rows, width)
            for side in ("_send", "_recv"):
                scratch[name + "_" + axis + side] = pltpu.SemaphoreType.DMA((count,))
    return pl.pallas_call(
        functools.partial(step_kernel, counts, tuple(scratch)),
        in_specs=[SMEM_SPEC] + [VMEM_SPEC] * 7 + [ANY_SPEC] * 4,
        out_specs=[VMEM_SPEC] * 6,
        out_shape=[
            shape((frames, D), BF16), shape((frames, D)), shape((3, 512, D), BF16), shape((16, D)), shape((8, 128)),
            shape((8, 128)),
        ],
        scratch_shapes=list(scratch.values()),
        compiler_params=pltpu.CompilerParams(collective_id=0, has_side_effects=True, vmem_limit_bytes=VMEM_CAP),
        name="step_part",
    )(lengths, norm_params, attn_in, attn_out, conv_in, conv_out, depth_kernel, bn_params, ffn_in, x, ffn_out, cot)


def local(
    block_input, lengths, cotangent, norm_params, bn_params, ffn_in, ffn_out, attn_in, attn_out, conv_in,
    depth_kernel, conv_out, stat_wide, stat_head, stat_hidden, stat_kernel, norm_second, bn_second, step_count,
):
    attn_in, conv_in = attn_in.swapaxes(1, 2), conv_in.transpose(2, 0, 1)
    stat_head, stat_kernel = stat_head.swapaxes(1, 2), stat_kernel.swapaxes(0, 1)
    block_out, input_grad, reduced, lng, total_square, gbn = step_call(
        lengths, block_input.T, cotangent.T, norm_params, ffn_in, ffn_out, attn_in, attn_out, conv_in, conv_out,
        depth_kernel, bn_params,
    )
    weights = (ffn_in, ffn_out, attn_in, attn_out, conv_in, depth_kernel, conv_out)
    outs = list(
        update_call(
            step_count, total_square, reduced, lng, gbn, weights, (stat_wide, stat_head, stat_hidden, stat_kernel),
            norm_params, norm_second, bn_params, bn_second, block_out, input_grad,
        )
    )
    for i in (5, 12):
        outs[i] = outs[i].swapaxes(1, 2)
    for i in (7, 14):
        outs[i] = outs[i].transpose(1, 2, 0)
    outs[22] = outs[22].swapaxes(1, 2)
    outs[24] = outs[24].swapaxes(0, 1)
    return (outs[25].T, outs[26].T, outs[0][0, :1], *outs[1:25])


def solution(mesh):
    weights_specs = (
        P(None, None, "tensor"), P(None, "tensor", None), P(None, None, "tensor"), P("tensor", None),
        P(None, None, "tensor"), P(None, "tensor"), P("tensor", None),
    )
    stat_specs = (
        P("tensor", None, None, None), P("tensor", None, None, None), P("tensor", None, None, None),
        P("tensor", None, None),
    )
    frames = P(("dp", "tensor"), None)
    channels = P(None, "tensor")
    return jax.shard_map(
        local,
        mesh=mesh,
        in_specs=(frames, P("dp"), frames, P(), channels, *weights_specs, *stat_specs, P(), channels, P()),
        out_specs=(
            frames, frames, P(), P(), channels, *weights_specs, *weights_specs, P(), channels, P(), channels,
            *stat_specs,
        ),
        check_vma=False,
    )
```
